32 devices in a mesh: dp: 8 (over z, x), tensor: 4 (over y, core).
Axes of the slice: x: 2, y: 2, z: 4, core: 2. Of those that a mesh axis runs over, the one named last changes fastest.
Arguments:
- tokens: bfloat16 [32768, 768], P(('dp', 'tensor')), may hold values from -6 to 6
- segment_ids: int32 [8, 4096], P('dp'), may hold values from 0 to 15, never falling along the last dimension, each value on 1 to 2048 neighbouring positions
- valid_mask: int32 [32768], P(('dp', 'tensor')), may hold values from 0 to 1, as said below
- teacher: bfloat16 [32768, 768], P(('dp', 'tensor')), may hold values from -6 to 6
- ask_query_weight: bfloat16 [768, 768], P('dp', 'tensor'), may hold values from -0.21875 to 0.21875
- ask_key_weight: bfloat16 [768, 768], P('dp', 'tensor'), may hold values from -0.21875 to 0.21875
- ask_value_weight: bfloat16 [768, 768], P('dp', 'tensor'), may hold values from -0.21875 to 0.21875
- ask_query_bias: float32 [768], P('tensor'), may hold values from -3 to 3
- ask_value_bias: float32 [768], P('tensor'), may hold values from -1 to 1
- ask_out_weight: bfloat16 [768, 768], P('tensor', 'dp'), may hold values from -0.875 to 0.875
- ask_out_bias: float32 [768], replicated, may hold values from -3 to 3
- ask_attn_gain: float32 [768], replicated, may hold values from 0.25 to 1.75
- ask_attn_shift: float32 [768], replicated, may hold values from -1.8 to 1.8
- ask_up_weight: bfloat16 [768, 3072], P('dp', 'tensor'), may hold values from -0.21875 to 0.21875
- ask_up_bias: float32 [3072], P('tensor'), may hold values from -3 to 3
- ask_down_weight: bfloat16 [3072, 768], P('tensor', 'dp'), may hold values from -0.109375 to 0.109375
- ask_down_bias: float32 [768], replicated, may hold values from -1.8 to 1.8
- ask_ffn_gain: float32 [768], replicated, may hold values from 0.25 to 1.75
- ask_ffn_shift: float32 [768], replicated, may hold values from -1.8 to 1.8
- doc_query_weight: bfloat16 [768, 768], P('dp', 'tensor'), may hold values from -0.21875 to 0.21875
- doc_key_weight: bfloat16 [768, 768], P('dp', 'tensor'), may hold values from -0.21875 to 0.21875
- doc_value_weight: bfloat16 [768, 768], P('dp', 'tensor'), may hold values from -0.21875 to 0.21875
- doc_query_bias: float32 [768], P('tensor'), may hold values from -3 to 3
- doc_value_bias: float32 [768], P('tensor'), may hold values from -1 to 1
- doc_out_weight: bfloat16 [768, 768], P('tensor', 'dp'), may hold values from -0.875 to 0.875
- doc_out_bias: float32 [768], replicated, may hold values from -3 to 3
- doc_attn_gain: float32 [768], replicated, may hold values from 0.25 to 1.75
- doc_attn_shift: float32 [768], replicated, may hold values from -1.8 to 1.8
- doc_up_weight: bfloat16 [768, 3072], P('dp', 'tensor'), may hold values from -0.21875 to 0.21875
- doc_up_bias: float32 [3072], P('tensor'), may hold values from -3 to 3
- doc_down_weight: bfloat16 [3072, 768], P('tensor', 'dp'), may hold values from -0.109375 to 0.109375
- doc_down_bias: float32 [768], replicated, may hold values from -1.8 to 1.8
- doc_ffn_gain: float32 [768], replicated, may hold values from 0.25 to 1.75
- doc_ffn_shift: float32 [768], replicated, may hold values from -1.8 to 1.8
Outputs:
- output: bfloat16 [32768, 768], P(('dp', 'tensor'))
- input_grad: float32 [32768, 768], P(('dp', 'tensor'))
- grad_ask_query_weight: float32 [768, 768], P('dp', 'tensor')
- grad_ask_key_weight: float32 [768, 768], P('dp', 'tensor')
- grad_ask_value_weight: float32 [768, 768], P('dp', 'tensor')
- grad_ask_query_bias: float32 [768], P('tensor')
- grad_ask_value_bias: float32 [768], P('tensor')
- grad_ask_out_weight: float32 [768, 768], P('tensor', 'dp')
- grad_ask_out_bias: float32 [768], replicated
- grad_ask_attn_gain: float32 [768], replicated
- grad_ask_attn_shift: float32 [768], replicated
- grad_ask_up_weight: float32 [768, 3072], P('dp', 'tensor')
- grad_ask_up_bias: float32 [3072], P('tensor')
- grad_ask_down_weight: float32 [3072, 768], P('tensor', 'dp')
- grad_ask_down_bias: float32 [768], replicated
- grad_ask_ffn_gain: float32 [768], replicated
- grad_ask_ffn_shift: float32 [768], replicated
- grad_doc_query_weight: float32 [768, 768], P('dp', 'tensor')
- grad_doc_key_weight: float32 [768, 768], P('dp', 'tensor')
- grad_doc_value_weight: float32 [768, 768], P('dp', 'tensor')
- grad_doc_query_bias: float32 [768], P('tensor')
- grad_doc_value_bias: float32 [768], P('tensor')
- grad_doc_out_weight: float32 [768, 768], P('tensor', 'dp')
- grad_doc_out_bias: float32 [768], replicated
- grad_doc_attn_gain: float32 [768], replicated
- grad_doc_attn_shift: float32 [768], replicated
- grad_doc_up_weight: float32 [768, 3072], P('dp', 'tensor')
- grad_doc_up_bias: float32 [3072], P('tensor')
- grad_doc_down_weight: float32 [3072, 768], P('tensor', 'dp')
- grad_doc_down_bias: float32 [768], replicated
- grad_doc_ffn_gain: float32 [768], replicated
- grad_doc_ffn_shift: float32 [768], replicated
The draws below stay inside these ranges and needn't reach their ends.
Inputs may be any that keep to these rules, and one draw needn't show every extreme that they name: `segment_ids`: segment numbers never fall along a sequence; a document has 1 to 2048 tokens, and some document has exactly 2048. `valid_mask`: the first token is always valid.
All inputs are finite; a program needn't handle non-finite values.
Results may differ from the reference program's by a relative error of at most 0.025.
Values may be sent and summed in bfloat16 or wider, within the bound.
No kernel may reach another device: no remote copies, remote signals or barrier semaphores. Data moves between devices by JAX's collectives and lax.ppermute only.
A program may use at most 320 MiB of HBM per device.

```python
import math
import jax
import jax.numpy as jnp
import numpy as np
from jax import lax

D = 768
HEADS = 12
HEAD_DIM = 64
FF = 3072
SEQ = 4096
NSEQ = 8
TOKENS = 32768


def draw_valid_mask(key, part):
    positions = jnp.arange(TOKENS, dtype=jnp.int32)
    threshold = 300 + 600 * positions // TOKENS
    random_picks = jax.random.randint(key, (TOKENS,), 0, 1000, dtype=jnp.int32)
    chosen = (random_picks < threshold) | (positions == 0)
    return jnp.where(chosen, 1, 0).astype(jnp.int32)


def raised(result, own_key, source, target, shards_of, factor):
    owner, partner = [(jnp.arange(result.shape[dim]) // (result.shape[dim] // shards_of)).reshape([-1 if axis == dim else 1 for axis in range(result.ndim)]) for dim in (source, target)]
    chosen = jax.random.permutation(own_key, shards_of)[partner]
    strong = (owner == chosen) | (owner == (partner + shards_of // 2) % shards_of)
    return jnp.where(strong, factor * result, result)


def block_levels(rng, extent, shards, low, high):
    def one(dim, shards_of):
        heights = jax.random.uniform(jax.random.fold_in(jax.random.fold_in(rng, 6), dim), (shards_of,), jnp.float32, low / len(shards), high / len(shards))
        return jnp.repeat(jnp.exp(heights), extent[dim] // shards_of).reshape((-1,) + (1,) * (len(extent) - dim - 1))

    factor_of = one(*shards[0])
    for cut in shards[1:]:
        factor_of = factor_of * one(*cut)
    return factor_of


def length_profile(amount, total, reach, slope):
    loads = [(1 << 20) // math.isqrt(standing ** slope) + 1 for standing in range(2, amount + 1)]
    surplus, holding = total - reach - (amount - 1), [1] * (amount - 1)
    while surplus > 0:
        movable = [i for i in range(amount - 1) if holding[i] < reach]
        whole, budget = sum([loads[i] for i in movable]), surplus
        for i in movable:
            more = min(reach - holding[i], max(1, budget * loads[i] // whole), surplus)
            holding[i] = holding[i] + more
            surplus = surplus - more
    return np.array([reach] + holding)


def ragged(rng, amount, total, reach, lean):
    if amount == 2:
        one = jax.random.randint(rng, (), max(1, total - reach), min(reach, total - 1) + 1)
        return jnp.stack([one, total - one])
    lengths = jnp.asarray(length_profile(amount, total, reach, lean), jnp.int32)
    pairs = (amount - 1) // 2
    giver, sink = lengths[1:1 + 2 * pairs:2], lengths[2:2 + 2 * pairs:2]
    slack = jnp.minimum(giver - 1, reach - sink)
    shifted = jax.random.randint(jax.random.fold_in(rng, 1), (pairs,), 0, 1 << 20) % (slack + 1)
    lengths = lengths.at[1:1 + 2 * pairs:2].set(giver - shifted).at[2:2 + 2 * pairs:2].set(sink + shifted)
    return lengths[jax.random.permutation(jax.random.fold_in(rng, 2), amount)]


def normal_values(rng, extent, deviation, most, cuts=(), kind=jnp.bfloat16):
    gain = block_levels(rng, extent, cuts, -0.22, 0.18) if cuts else 1.0
    entries = jax.random.normal(rng, extent, jnp.float32) * deviation * gain
    return jnp.minimum(jnp.maximum(entries, -most), most).astype(kind)


def gaussian_with(stream_key, dims, deviation, bound, split, heavy, kind=jnp.bfloat16):
    entries = deviation * jax.random.normal(stream_key, dims, jnp.float32)
    if split:
        entries = entries * block_levels(stream_key, dims, split, -0.22, 0.18)
    return jnp.clip(raised(entries, jax.random.fold_in(stream_key, 3), *heavy), -bound, bound).astype(kind)


def setup_inputs(seed: int = 0) -> dict:
    splits = jax.random.split(jax.random.key(seed), 35)
    tokens = gaussian_with(splits[0], (TOKENS, D), 1.0, 6.0, ((0, 32),), (0, 1, 32, 2.75))
    segment_ids = jax.vmap(lambda own: jnp.searchsorted(jnp.cumsum(ragged(own, 16, SEQ, SEQ // 2, 2)), jnp.arange(SEQ), side="right"))(jax.random.split(splits[1], NSEQ)).reshape((NSEQ, SEQ)).astype(jnp.int32)
    valid_mask = draw_valid_mask(jax.random.fold_in(splits[34], 71), 0)
    teacher = gaussian_with(splits[3], (TOKENS, D), 1.0, 6.0, ((0, 32),), (0, 1, 32, 2.75))
    ask_query_weight = normal_values(splits[4], (D, D), D ** -0.5, 0.21875, ((0, 8), (1, 4)))
    ask_key_weight = normal_values(splits[5], (D, D), D ** -0.5, 0.21875, ((0, 8), (1, 4)))
    ask_value_weight = normal_values(splits[6], (D, D), D ** -0.5, 0.21875, ((0, 8), (1, 4)))
    ask_query_bias = normal_values(splits[7], (D,), 0.5, 3.0, ((0, 4),), jnp.float32)
    ask_value_bias = normal_values(splits[8], (D,), 0.2, 1.0, ((0, 4),), jnp.float32)
    ask_out_weight = normal_values(splits[9], (D, D), (D // 16) ** -0.5, 0.875, ((0, 4), (1, 8)))
    ask_out_bias = normal_values(splits[10], (D,), 0.5, 3.0, (), jnp.float32)
    ask_attn_gain = jnp.clip(1.0 + 0.15 * jax.random.normal(splits[11], (D,), jnp.float32), 0.25, 1.75)
    ask_attn_shift = normal_values(splits[12], (D,), 0.3, 1.8, (), jnp.float32)
    ask_up_weight = normal_values(splits[13], (D, FF), D ** -0.5, 0.21875, ((0, 8), (1, 4)))
    ask_up_bias = normal_values(splits[14], (FF,), 0.5, 3.0, ((0, 4),), jnp.float32)
    ask_down_weight = normal_values(splits[15], (FF, D), FF ** -0.5, 0.109375, ((0, 4), (1, 8)))
    ask_down_bias = normal_values(splits[16], (D,), 0.3, 1.8, (), jnp.float32)
    ask_ffn_gain = jnp.clip(1.0 + 0.15 * jax.random.normal(splits[17], (D,), jnp.float32), 0.25, 1.75)
    ask_ffn_shift = normal_values(splits[18], (D,), 0.3, 1.8, (), jnp.float32)
    doc_query_weight = normal_values(splits[19], (D, D), D ** -0.5, 0.21875, ((0, 8), (1, 4)))
    doc_key_weight = normal_values(splits[20], (D, D), D ** -0.5, 0.21875, ((0, 8), (1, 4)))
    doc_value_weight = normal_values(splits[21], (D, D), D ** -0.5, 0.21875, ((0, 8), (1, 4)))
    doc_query_bias = normal_values(splits[22], (D,), 0.5, 3.0, ((0, 4),), jnp.float32)
    doc_value_bias = normal_values(splits[23], (D,), 0.2, 1.0, ((0, 4),), jnp.float32)
    doc_out_weight = normal_values(splits[24], (D, D), (D // 16) ** -0.5, 0.875, ((0, 4), (1, 8)))
    doc_out_bias = normal_values(splits[25], (D,), 0.5, 3.0, (), jnp.float32)
    doc_attn_gain = jnp.clip(1.0 + 0.15 * jax.random.normal(splits[26], (D,), jnp.float32), 0.25, 1.75)
    doc_attn_shift = normal_values(splits[27], (D,), 0.3, 1.8, (), jnp.float32)
    doc_up_weight = normal_values(splits[28], (D, FF), D ** -0.5, 0.21875, ((0, 8), (1, 4)))
    doc_up_bias = normal_values(splits[29], (FF,), 0.5, 3.0, ((0, 4),), jnp.float32)
    doc_down_weight = normal_values(splits[30], (FF, D), FF ** -0.5, 0.109375, ((0, 4), (1, 8)))
    doc_down_bias = normal_values(splits[31], (D,), 0.3, 1.8, (), jnp.float32)
    doc_ffn_gain = jnp.clip(1.0 + 0.15 * jax.random.normal(splits[32], (D,), jnp.float32), 0.25, 1.75)
    doc_ffn_shift = normal_values(splits[33], (D,), 0.3, 1.8, (), jnp.float32)
    return dict(tokens=tokens, segment_ids=segment_ids, valid_mask=valid_mask, teacher=teacher, ask_query_weight=ask_query_weight, ask_key_weight=ask_key_weight, ask_value_weight=ask_value_weight, ask_query_bias=ask_query_bias, ask_value_bias=ask_value_bias, ask_out_weight=ask_out_weight, ask_out_bias=ask_out_bias, ask_attn_gain=ask_attn_gain, ask_attn_shift=ask_attn_shift, ask_up_weight=ask_up_weight, ask_up_bias=ask_up_bias, ask_down_weight=ask_down_weight, ask_down_bias=ask_down_bias, ask_ffn_gain=ask_ffn_gain, ask_ffn_shift=ask_ffn_shift, doc_query_weight=doc_query_weight, doc_key_weight=doc_key_weight, doc_value_weight=doc_value_weight, doc_query_bias=doc_query_bias, doc_value_bias=doc_value_bias, doc_out_weight=doc_out_weight, doc_out_bias=doc_out_bias, doc_attn_gain=doc_attn_gain, doc_attn_shift=doc_attn_shift, doc_up_weight=doc_up_weight, doc_up_bias=doc_up_bias, doc_down_weight=doc_down_weight, doc_down_bias=doc_down_bias, doc_ffn_gain=doc_ffn_gain, doc_ffn_shift=doc_ffn_shift)


@jax.custom_vjp
def low(v):
    return lax.optimization_barrier(v.astype(jnp.bfloat16)).astype(jnp.float32)

@jax.custom_vjp
def low_back(v):
    return v

def low_keep(v):
    return (low(v), None)

def low_pass(kept, grad):
    return (grad,)

def back_keep(v):
    return (v, None)

def back_low(kept, grad):
    return (low(grad),)
low.defvjp(low_keep, low_pass)
low_back.defvjp(back_keep, back_low)
highest = lax.Precision.HIGHEST
eps_norm = 1e-12

def matmul(first_mat, second_mat):
    return jnp.dot(first_mat, second_mat, precision=highest, preferred_element_type=jnp.float32)

def layer_norm(values, scale_vec, shift_vec):
    centered = values - lax.optimization_barrier(jnp.mean(values, axis=-1, keepdims=True))
    variance = lax.optimization_barrier(jnp.mean(centered * centered, axis=-1, keepdims=True))
    return centered * lax.rsqrt(variance + eps_norm) * scale_vec + shift_vec

def attend_sequence(query_seq, key_seq, value_seq, segment_row):
    block_rows = min(512, SEQ)
    score_scale = HEAD_DIM ** (-0.5)

    def one_block(block_index):
        query_part = lax.dynamic_slice_in_dim(query_seq, block_index * block_rows, block_rows, 0)
        row_segments = lax.dynamic_slice_in_dim(segment_row, block_index * block_rows, block_rows, 0)
        raw_scores = jnp.einsum('qhd,khd->hqk', query_part, key_seq, precision=highest)
        same_doc = row_segments[:, None] == segment_row[None, :]
        scores = jnp.where(same_doc[None], low_back(raw_scores) * score_scale, -1000000000.0)
        attn_probs = jax.nn.softmax(scores, axis=-1)
        return jnp.einsum('hqk,khd->qhd', low(attn_probs), value_seq, precision=highest)
    blocks = jnp.arange(SEQ // block_rows, dtype=jnp.int32)
    contexts = lax.map(jax.checkpoint(one_block), blocks)
    return contexts.reshape(SEQ, HEADS, HEAD_DIM)

def layer(hidden_in, segment_ids, params):
    query_mat, key_mat, value_mat, query_bias, value_bias, out_mat, out_bias, attn_gain, attn_shift, up_mat, up_bias, down_mat, down_bias, ffn_gain, ffn_shift = params
    sent = low(hidden_in)
    queries = low(low_back(matmul(sent, query_mat) + query_bias))
    key_rows = low(low_back(matmul(sent, key_mat)))
    value_rows = low(low_back(matmul(sent, value_mat) + value_bias))
    shaped = (queries.reshape(NSEQ, SEQ, HEADS, HEAD_DIM), key_rows.reshape(NSEQ, SEQ, HEADS, HEAD_DIM), value_rows.reshape(NSEQ, SEQ, HEADS, HEAD_DIM), segment_ids)
    context = lax.map(lambda items: attend_sequence(items[0], items[1], items[2], items[3]), shaped)
    context = low(low_back(context.reshape(TOKENS, D)))
    attn_branch = low_back(matmul(context, out_mat))
    first_sum = hidden_in + attn_branch + out_bias
    normed = layer_norm(first_sum, attn_gain, attn_shift)
    inner = low_back(matmul(low(normed), up_mat) + up_bias)
    activated = low(jax.nn.gelu(inner, approximate=False))
    ffn_branch = low_back(matmul(activated, down_mat))
    second_sum = normed + ffn_branch + down_bias
    return layer_norm(second_sum, ffn_gain, ffn_shift)

def reference(tokens, segment_ids, valid_mask, teacher, ask_query_weight, ask_key_weight, ask_value_weight, ask_query_bias, ask_value_bias, ask_out_weight, ask_out_bias, ask_attn_gain, ask_attn_shift, ask_up_weight, ask_up_bias, ask_down_weight, ask_down_bias, ask_ffn_gain, ask_ffn_shift, doc_query_weight, doc_key_weight, doc_value_weight, doc_query_bias, doc_value_bias, doc_out_weight, doc_out_bias, doc_attn_gain, doc_attn_shift, doc_up_weight, doc_up_bias, doc_down_weight, doc_down_bias, doc_ffn_gain, doc_ffn_shift):
    ask_params = tuple((item.astype(jnp.float32) for item in (ask_query_weight, ask_key_weight, ask_value_weight, ask_query_bias, ask_value_bias, ask_out_weight, ask_out_bias, ask_attn_gain, ask_attn_shift, ask_up_weight, ask_up_bias, ask_down_weight, ask_down_bias, ask_ffn_gain, ask_ffn_shift)))
    doc_params = tuple((item.astype(jnp.float32) for item in (doc_query_weight, doc_key_weight, doc_value_weight, doc_query_bias, doc_value_bias, doc_out_weight, doc_out_bias, doc_attn_gain, doc_attn_shift, doc_up_weight, doc_up_bias, doc_down_weight, doc_down_bias, doc_ffn_gain, doc_ffn_shift)))
    mask_rows = valid_mask.astype(jnp.float32)
    valid_total = jnp.sum(mask_rows)
    target = teacher.astype(jnp.float32)
    hidden_in = tokens.astype(jnp.float32)

    def forward(inputs, first_params, second_params):
        middle = layer(inputs, segment_ids, first_params)
        final = layer(middle, segment_ids, second_params)
        offset = final - target
        loss = 0.5 * (TOKENS / valid_total) * jnp.sum(mask_rows[:, None] * offset * offset)
        return (loss, final)
    loss, vjp_back, final = jax.vjp(forward, hidden_in, ask_params, doc_params, has_aux=True)
    grad_in, grad_ask, grad_doc = vjp_back(jnp.ones((), jnp.float32))
    return (final.astype(jnp.bfloat16), grad_in, grad_ask[0], grad_ask[1], grad_ask[2], grad_ask[3], grad_ask[4], grad_ask[5], grad_ask[6], grad_ask[7], grad_ask[8], grad_ask[9], grad_ask[10], grad_ask[11], grad_ask[12], grad_ask[13], grad_ask[14], grad_doc[0], grad_doc[1], grad_doc[2], grad_doc[3], grad_doc[4], grad_doc[5], grad_doc[6], grad_doc[7], grad_doc[8], grad_doc[9], grad_doc[10], grad_doc[11], grad_doc[12], grad_doc[13], grad_doc[14])
```

```python
import jax
import jax.numpy as jnp
from jax import lax
from jax.experimental import pallas as pl
from jax.experimental.pallas import tpu as pltpu
from jax.sharding import PartitionSpec as P

HEAD_DIM = 64
LANES = 128
TILE = 256
BLOCKED = 1e9
SEGMENTS = 16
eps_norm = 1e-12

bf16 = jnp.bfloat16
f32 = jnp.float32
NT = (((1,), (1,)), ((), ()))
TN = (((0,), (0,)), ((), ()))
WHOLE = pl.BlockSpec(memory_space=pltpu.VMEM)


def dot_nn(first_mat, second_mat):
    return jnp.dot(first_mat, second_mat, preferred_element_type=f32)


def dot_nt(first_mat, second_mat):
    return lax.dot_general(first_mat, second_mat, NT, preferred_element_type=f32)


def dot_tn(first_mat, second_mat):
    return lax.dot_general(first_mat, second_mat, TN, preferred_element_type=f32)


def kernel_params():
    return pltpu.CompilerParams(vmem_limit_bytes=60 * 1024 * 1024)


def flip(values, bit):
    size = lax.axis_size("tensor")
    return lax.ppermute(values, "tensor", [(i, i ^ bit) for i in range(size)])


def gather_chunks(own):
    half = own.shape[0] // 2
    near = flip(own, 1)
    far = [flip(own[:half], 2), flip(own[half:], 2)]
    last = [flip(part, 1) for part in far]
    return own, near, jnp.concatenate(far, axis=0), jnp.concatenate(last, axis=0)


def exchange_pieces(pieces):
    return [pieces[0]] + [flip(pieces[r], r) for r in range(1, 4)]


def scatter_chunks(chunks):
    crossing = chunks[2].astype(f32) + flip(chunks[3], 1).astype(f32)
    near = flip(chunks[1], 1).astype(f32)
    far = flip(crossing.astype(bf16), 2).astype(f32)
    return chunks[0].astype(f32) + near + far


def butterfly(values, axes):
    for axis in axes:
        size = lax.axis_size(axis)
        step = 1
        while step < size:
            other = lax.ppermute(values, axis, [(i, i ^ step) for i in range(size)])
            values = values + other
            step *= 2
    return values


def project(pieces, matrix, query_bias, value_bias, query_marks, key_marks):
    rows, width = pieces[0].shape
    heads = matrix.shape[1] // 3 // HEAD_DIM
    group = heads * HEAD_DIM
    wide = heads * LANES
    sub = rows // 2

    def body(p0, p1, p2, p3, mat, bias_q, bias_v, mark_q, mark_k, out_q, out_k, out_v):
        chunk = pl.program_id(0)
        lane = lax.broadcasted_iota(jnp.int32, (sub, HEAD_DIM), 1)
        ones = jnp.where(lane < 2, 1.0, 0.0).astype(bf16)

        def run(piece):
            for part in range(2):
                at = slice(part * sub, (part + 1) * sub)
                full = dot_nn(piece[at, :], mat[...])
                for h in range(heads):
                    lo = h * HEAD_DIM
                    to = slice(h * LANES, (h + 1) * LANES)
                    q = full[:, lo : lo + HEAD_DIM] + bias_q[:, lo : lo + HEAD_DIM]
                    q = (q.astype(bf16).astype(f32) * HEAD_DIM ** (-0.5)).astype(bf16)
                    k = full[:, group + lo : group + lo + HEAD_DIM].astype(bf16)
                    v = full[:, 2 * group + lo : 2 * group + lo + HEAD_DIM]
                    v = (v + bias_v[:, lo : lo + HEAD_DIM]).astype(bf16)
                    out_q[at, to] = jnp.concatenate([q, mark_q[at, :]], axis=1)
                    out_k[at, to] = jnp.concatenate([k, mark_k[at, :]], axis=1)
                    out_v[at, to] = jnp.concatenate([v, ones], axis=1)

        for r, piece in enumerate((p0, p1, p2, p3)):

            @pl.when(chunk == r)
            def _(piece=piece):
                run(piece)

    out = jax.ShapeDtypeStruct((4 * rows, wide), bf16)
    spec = pl.BlockSpec((rows, wide), lambda i: (i, 0))
    mark_spec = pl.BlockSpec((rows, HEAD_DIM), lambda i: (i, 0))
    return pl.pallas_call(
        body,
        grid=(4,),
        in_specs=[WHOLE] * 7 + [mark_spec] * 2,
        out_specs=[spec] * 3,
        out_shape=[out] * 3,
        compiler_params=kernel_params(),
        name="project",
    )(*pieces, matrix, query_bias[None], value_bias[None], query_marks, key_marks)


def attention_forward(low, high, place, queries, keys, values):
    rows, wide = queries.shape
    heads = wide // LANES
    count = rows // TILE
    per_chunk = count // 4
    half = rows // 8
    half_blocks = half // TILE
    group = heads * HEAD_DIM

    def body(
        low_ref, high_ref, place_ref, q_ref, k_ref, v_ref, ctx_ref, ql_ref, score, peak, total
    ):
        block = pl.program_id(0)
        own = place_ref[0]
        first = low_ref[block]
        last = high_ref[block]
        peak[...] = jnp.full_like(peak, -3e38)
        total[...] = jnp.zeros_like(total)
        q_heads = [q_ref[:, h * LANES : (h + 1) * LANES] for h in range(heads)]

        def where_is(j):
            spot = ((j // per_chunk) ^ own) * per_chunk + j % per_chunk
            return pl.multiple_of(spot * TILE, TILE)

        def score_step(j, carry):
            at = where_is(j)
            for h in range(heads):
                s = dot_nt(q_heads[h], k_ref[pl.ds(at, TILE), h * LANES : (h + 1) * LANES])
                score[h, j - first] = s
                top = s[:, 0:LANES]
                for c in range(1, TILE // LANES):
                    top = jnp.maximum(top, s[:, c * LANES : (c + 1) * LANES])
                peak[h] = jnp.maximum(peak[h], top)
            return carry

        lax.fori_loop(first, last, score_step, 0)
        tops = []
        for h in range(heads):
            top = jnp.max(peak[h], axis=1, keepdims=True)
            tops.append(top)
            peak[h] = jnp.broadcast_to(top, (TILE, LANES))

        def sum_step(j, carry):
            at = where_is(j)
            for h in range(heads):
                top = peak[h]
                parts = [
                    jnp.exp(score[h, j - first, :, c * LANES : (c + 1) * LANES] - top)
                    for c in range(TILE // LANES)
                ]
                p = jnp.concatenate(parts, axis=1).astype(bf16)
                total[h] += dot_nn(p, v_ref[pl.ds(at, TILE), h * LANES : (h + 1) * LANES])
            return carry

        lax.fori_loop(first, last, sum_step, 0)
        lane = lax.broadcasted_iota(jnp.int32, (TILE, LANES), 1)
        outs = []
        for h in range(heads):
            acc = total[h]
            norm = acc[:, HEAD_DIM : HEAD_DIM + 1]
            outs.append((acc[:, 0:HEAD_DIM] * (1.0 / norm)).astype(bf16))
            shift = -(tops[h] + jnp.log(norm))
            one = shift.astype(bf16).astype(f32)
            two = (shift - one).astype(bf16).astype(f32)
            three = shift - one - two
            q = q_heads[h].astype(f32)
            q = jnp.where(lane == HEAD_DIM + SEGMENTS, one, q)
            q = jnp.where(lane == HEAD_DIM + SEGMENTS + 1, two, q)
            q = jnp.where(lane == HEAD_DIM + SEGMENTS + 2, three, q)
            ql_ref[:, h * LANES : (h + 1) * LANES] = q.astype(bf16)
        ctx = jnp.concatenate(outs, axis=1)
        inside = block % per_chunk
        at = pl.multiple_of((inside % half_blocks) * TILE, TILE)

        @pl.when(inside < half_blocks)
        def _():
            ctx_ref[0, pl.ds(at, TILE), 0:group] = ctx

        @pl.when(inside >= half_blocks)
        def _():
            ctx_ref[0, pl.ds(at, TILE), group : 2 * group] = ctx

    row_spec = pl.BlockSpec((TILE, wide), lambda i, *_: (i, 0))
    return pl.pallas_call(
        body,
        grid_spec=pltpu.PrefetchScalarGridSpec(
            num_scalar_prefetch=3,
            grid=(count,),
            in_specs=[row_spec, WHOLE, WHOLE],
            out_specs=[
                pl.BlockSpec((1, half, 2 * group), lambda i, *_: (i // per_chunk, 0, 0)),
                row_spec,
            ],
            scratch_shapes=[
                pltpu.VMEM((heads, count, TILE, TILE), f32),
                pltpu.VMEM((heads, TILE, LANES), f32),
                pltpu.VMEM((heads, TILE, LANES), f32),
            ],
        ),
        out_shape=[
            jax.ShapeDtypeStruct((4, half, 2 * group), bf16),
            jax.ShapeDtypeStruct((rows, wide), bf16),
        ],
        compiler_params=kernel_params(),
        name="attention_forward",
    )(low, high, place, queries, keys, values)


def attention_backward(low, high, place, queries, keys, values, contexts, grads):
    rows, wide = queries.shape
    heads = wide // LANES
    count = rows // TILE
    per_chunk = count // 4
    half = rows // 8
    half_blocks = half // TILE
    group = heads * HEAD_DIM

    def body(low_ref, high_ref, place_ref, q_ref, k_ref, v_ref, c_ref, g0, g1, g2, g3, *rest):
        dq_ref, dk_ref, dv_ref, do_all, dq_all, acc_k, acc_v = rest
        block = pl.program_id(0)
        own = place_ref[0]
        first = low_ref[block]
        last = high_ref[block]

        @pl.when(block == 0)
        def _():
            dq_all[...] = jnp.zeros_like(dq_all)
            lane = lax.broadcasted_iota(jnp.int32, (TILE, HEAD_DIM), 1)
            for chunk, g_ref in enumerate((g0, g1, g2, g3)):

                def prepare(b, carry, chunk=chunk, g_ref=g_ref):
                    at = pl.multiple_of(b * TILE, TILE)
                    for side in range(2):
                        cols = slice(side * group, (side + 1) * group)
                        row = pl.multiple_of((2 * chunk + side) * half + at, TILE)
                        c = c_ref[chunk, pl.ds(at, TILE), cols].astype(f32)
                        g = g_ref[pl.ds(at, TILE), cols].astype(f32)
                        for h in range(heads):
                            lo = h * HEAD_DIM
                            gh = g[:, lo : lo + HEAD_DIM]
                            ch = c[:, lo : lo + HEAD_DIM]
                            delta = -jnp.sum(gh * ch, axis=1, keepdims=True)
                            one = delta.astype(bf16).astype(f32)
                            two = delta - one
                            tail = jnp.where(lane == 0, one, jnp.where(lane == 1, two, 0.0))
                            both = jnp.concatenate([gh, tail], axis=1).astype(bf16)
                            do_all[pl.ds(row, TILE), h * LANES : (h + 1) * LANES] = both
                    return carry

                lax.fori_loop(0, half_blocks, prepare, 0)

        acc_k[...] = jnp.zeros_like(acc_k)
        acc_v[...] = jnp.zeros_like(acc_v)

        def step(j, carry):
            spot = ((j // per_chunk) ^ own) * per_chunk + j % per_chunk
            at = pl.multiple_of(spot * TILE, TILE)
            for h in range(heads):
                to = slice(h * LANES, (h + 1) * LANES)
                q = q_ref[pl.ds(at, TILE), to]
                k = k_ref[:, to]
                do = do_all[pl.ds(at, TILE), to]
                p = jnp.exp(dot_nt(k, q))
                ds = (p * dot_nt(v_ref[:, to], do)).astype(bf16)
                acc_v[h] += dot_nn(p.astype(bf16), do)
                acc_k[h] += dot_nn(ds, q)
                dq_all[pl.ds(at, TILE), to] += dot_tn(ds, k)
            return carry

        lax.fori_loop(first, last, step, 0)
        dk = [acc_k[h, :, 0:HEAD_DIM] for h in range(heads)]
        dv = [acc_v[h, :, 0:HEAD_DIM] for h in range(heads)]
        dk_ref[...] = jnp.concatenate(dk, axis=1).astype(bf16)
        dv_ref[...] = jnp.concatenate(dv, axis=1).astype(bf16)

        @pl.when(block == count - 1)
        def _():
            def finish(b, carry):
                at = pl.multiple_of(b * TILE, TILE)
                dq = [
                    dq_all[pl.ds(at, TILE), h * LANES : h * LANES + HEAD_DIM] for h in range(heads)
                ]
                dq = jnp.concatenate(dq, axis=1) * HEAD_DIM ** (-0.5)
                dq_ref[pl.ds(at, TILE), :] = dq.astype(bf16)
                return carry

            lax.fori_loop(0, count, finish, 0)

    row_spec = pl.BlockSpec((TILE, wide), lambda i, *_: (i, 0))
    out_spec = pl.BlockSpec((TILE, group), lambda i, *_: (i, 0))
    out = jax.ShapeDtypeStruct((rows, group), bf16)
    return pl.pallas_call(
        body,
        grid_spec=pltpu.PrefetchScalarGridSpec(
            num_scalar_prefetch=3,
            grid=(count,),
            in_specs=[WHOLE, row_spec, row_spec] + [WHOLE] * 5,
            out_specs=[WHOLE, out_spec, out_spec],
            scratch_shapes=[
                pltpu.VMEM((rows, wide), bf16),
                pltpu.VMEM((rows, wide), f32),
                pltpu.VMEM((heads, TILE, LANES), f32),
                pltpu.VMEM((heads, TILE, LANES), f32),
            ],
        ),
        out_shape=[out] * 3,
        compiler_params=kernel_params(),
        name="attention_backward",
    )(low, high, place, queries, keys, values, contexts, *grads)


SQRT_HALF = 0.7071067811865476
PHI_SCALE = 0.3989422804014327


def norm_parts(values):
    centered = values - jnp.mean(values, axis=-1, keepdims=True)
    variance = jnp.mean(centered * centered, axis=-1, keepdims=True)
    scale = lax.rsqrt(variance + eps_norm)
    return centered * scale, scale


def tokens_forward(place, hidden, pieces, weights, up_bias, vectors):
    rows, width = hidden.shape
    half = rows // 2
    group = pieces[0].shape[1] // 2
    part = TILE
    steps = half // part
    size = 2 * part

    def body(place_ref, x_ref, c0, c1, c2, c3, w_ref, ub_ref, vec_ref, *outs):
        o_ref, ob_ref, nb_ref, act_ref, slope_ref, y1_ref, y2_ref, r1_ref, r2_ref = outs
        own = place_ref[0]
        first = x_ref[...].reshape(size, width).astype(f32) + vec_ref[0:1, :]
        for r, c_ref in enumerate((c0, c1, c2, c3)):
            ctx = jnp.concatenate([c_ref[:, 0:group], c_ref[:, group : 2 * group]], axis=0)
            first = first + dot_nt(ctx, w_ref[own ^ r, :, 2 * width : 2 * width + group])
        y1, r1 = norm_parts(first)
        y1_ref[...] = y1.reshape(2, part, width)
        r1_ref[...] = jnp.broadcast_to(r1, (size, LANES)).reshape(2, part, LANES)
        normed = y1 * vec_ref[1:2, :] + vec_ref[2:3, :]
        sent = normed.astype(bf16)
        nb_ref[...] = sent.reshape(2, part, width)
        second = normed + vec_ref[3:4, :]
        for t in range(4):
            cols = slice(t * width, (t + 1) * width)
            inner = dot_nn(sent, w_ref[t, :, 0:width]) + ub_ref[t : t + 1, :]
            cdf = 0.5 + 0.5 * lax.erf(inner * SQRT_HALF)
            act = (inner * cdf).astype(bf16)
            slope = cdf + inner * (PHI_SCALE * jnp.exp(-0.5 * inner * inner))
            act_ref[:, :, cols] = act.reshape(2, part, width)
            slope_ref[:, :, cols] = slope.astype(bf16).reshape(2, part, width)
            second = second + dot_nt(act, w_ref[t, :, width : 2 * width])
        y2, r2 = norm_parts(second)
        y2_ref[...] = y2.reshape(2, part, width)
        r2_ref[...] = jnp.broadcast_to(r2, (size, LANES)).reshape(2, part, LANES)
        result = y2 * vec_ref[4:5, :] + vec_ref[5:6, :]
        o_ref[...] = result.reshape(2, part, width)
        ob_ref[...] = result.astype(bf16).reshape(2, part, width)

    def spec(cols):
        return pl.BlockSpec((2, part, cols), lambda i, *_: (0, i, 0))

    def out(cols, kind):
        return jax.ShapeDtypeStruct((2, half, cols), kind)

    piece_spec = pl.BlockSpec((part, 2 * group), lambda i, *_: (i, 0))
    units = 4 * width
    results = pl.pallas_call(
        body,
        grid_spec=pltpu.PrefetchScalarGridSpec(
            num_scalar_prefetch=1,
            grid=(steps,),
            in_specs=[spec(width)] + [piece_spec] * 4 + [WHOLE] * 3,
            out_specs=[
                spec(width),
                spec(width),
                spec(width),
                spec(units),
                spec(units),
                spec(width),
                spec(width),
                spec(LANES),
                spec(LANES),
            ],
        ),
        out_shape=[
            out(width, f32),
            out(width, bf16),
            out(width, bf16),
            out(units, bf16),
            out(units, bf16),
            out(width, f32),
            out(width, f32),
            out(LANES, f32),
            out(LANES, f32),
        ],
        compiler_params=kernel_params(),
        name="tokens_forward",
    )(place, hidden.reshape(2, half, width), *pieces, weights, up_bias, vectors)
    return [item.reshape(rows, item.shape[2]) for item in results]


def tokens_backward(place, grad, saved, weights, vectors, group):
    slope, y1, y2, r1, r2 = saved
    rows, width = grad.shape
    half = rows // 2
    part = TILE
    steps = half // part
    size = 2 * part
    units = 4 * width

    def norm_back(g, y, r, gain):
        e = g * gain
        mean_e = jnp.mean(e, axis=-1, keepdims=True)
        mean_ey = jnp.mean(e * y, axis=-1, keepdims=True)
        return r * (e - mean_e - y * mean_ey)

    def body(place_ref, g_ref, sl_ref, y1_ref, y2_ref, r1_ref, r2_ref, w_ref, vec_ref, *outs):
        bg_ref, gi_ref, gf_ref, ag_ref, p0, p1, p2, p3, sum_ref = outs
        own = place_ref[0]

        @pl.when(pl.program_id(0) == 0)
        def _():
            sum_ref[...] = jnp.zeros_like(sum_ref)

        def total(values):
            return jnp.sum(values, axis=0, keepdims=True)

        g = g_ref[...].reshape(size, width)
        y2 = y2_ref[...].reshape(size, width)
        r2 = r2_ref[...].reshape(size, LANES)[:, 0:1]
        second = norm_back(g, y2, r2, vec_ref[4:5, :])
        sum_ref[0:1, :] += total(g * y2)
        sum_ref[1:2, :] += total(g)
        sum_ref[2:3, :] += total(second)
        branch = second.astype(bf16)
        bg_ref[...] = branch.reshape(2, part, width)
        normed = second
        for t in range(4):
            cols = slice(t * width, (t + 1) * width)
            slope_t = sl_ref[:, :, cols].reshape(size, width).astype(f32)
            inner = (dot_nn(branch, w_ref[t, :, width : 2 * width]) * slope_t).astype(bf16)
            gi_ref[:, :, cols] = inner.reshape(2, part, width)
            sum_ref[6 + t : 7 + t, :] += total(inner.astype(f32))
            normed = normed + dot_nt(inner, w_ref[t, :, 0:width])
        y1 = y1_ref[...].reshape(size, width)
        r1 = r1_ref[...].reshape(size, LANES)[:, 0:1]
        first = norm_back(normed, y1, r1, vec_ref[1:2, :])
        sum_ref[3:4, :] += total(normed * y1)
        sum_ref[4:5, :] += total(normed)
        sum_ref[5:6, :] += total(first)
        gf_ref[...] = first.reshape(2, part, width)
        sent = first.astype(bf16)
        ag_ref[...] = sent.reshape(2, part, width)
        for r, p_ref in enumerate((p0, p1, p2, p3)):
            ctx = dot_nn(sent, w_ref[own ^ r, :, 2 * width : 2 * width + group]).astype(bf16)
            p_ref[...] = jnp.concatenate([ctx[0:part], ctx[part:size]], axis=1)

    def spec(cols):
        return pl.BlockSpec((2, part, cols), lambda i, *_: (0, i, 0))

    def out(cols, kind):
        return jax.ShapeDtypeStruct((2, half, cols), kind)

    piece_spec = pl.BlockSpec((part, 2 * group), lambda i, *_: (i, 0))
    piece = jax.ShapeDtypeStruct((half, 2 * group), bf16)
    sums = jax.ShapeDtypeStruct((16, width), f32)

    def view(values):
        return values.reshape(2, half, values.shape[1])

    results = pl.pallas_call(
        body,
        grid_spec=pltpu.PrefetchScalarGridSpec(
            num_scalar_prefetch=1,
            grid=(steps,),
            in_specs=[
                spec(width),
                spec(units),
                spec(width),
                spec(width),
                spec(LANES),
                spec(LANES),
                WHOLE,
                WHOLE,
            ],
            out_specs=[spec(width), spec(units), spec(width), spec(width)]
            + [piece_spec] * 4
            + [pl.BlockSpec((16, width), lambda i, *_: (0, 0))],
        ),
        out_shape=[out(width, bf16), out(units, bf16), out(width, f32), out(width, bf16)]
        + [piece] * 4
        + [sums],
        compiler_params=kernel_params(),
        name="tokens_backward",
    )(place, view(grad), view(slope), view(y1), view(y2), view(r1), view(r2), weights, vectors)
    big = [item.reshape(rows, item.shape[2]) for item in results[:4]]
    return big, list(results[4:8]), results[8]


def weight_grads(place, sent, inner, branch, act, attn, pieces):
    rows, width = sent.shape
    half = rows // 2
    group = pieces[0].shape[1] // 2

    def body(place_ref, s_ref, i_ref, b_ref, a_ref, g_ref, c0, c1, c2, c3, o_ref):
        t = pl.program_id(0)
        own = place_ref[0]
        o_ref[0, :, 0:width] = dot_tn(s_ref[...], i_ref[...]).astype(bf16)
        o_ref[0, :, width : 2 * width] = dot_tn(b_ref[...], a_ref[...]).astype(bf16)
        for r, c_ref in enumerate((c0, c1, c2, c3)):

            @pl.when(t == own ^ r)
            def _(c_ref=c_ref):
                ctx = jnp.concatenate([c_ref[:, 0:group], c_ref[:, group : 2 * group]], axis=0)
                o_ref[0, :, 2 * width : 2 * width + group] = dot_tn(g_ref[...], ctx).astype(bf16)

    unit_spec = pl.BlockSpec((rows, width), lambda i, *_: (0, i))
    cols = 2 * width + group
    return pl.pallas_call(
        body,
        grid_spec=pltpu.PrefetchScalarGridSpec(
            num_scalar_prefetch=1,
            grid=(4,),
            in_specs=[WHOLE, unit_spec, WHOLE, unit_spec, WHOLE] + [WHOLE] * 4,
            out_specs=pl.BlockSpec((1, width, cols), lambda i, *_: (i, 0, 0)),
        ),
        out_shape=jax.ShapeDtypeStruct((4, width, cols), bf16),
        compiler_params=kernel_params(),
        name="weight_grads",
    )(place, sent, inner, branch, act, attn, *pieces)


def input_grads(grad_q, grad_k, grad_v, matrix):
    rows, group = grad_q.shape
    width = matrix.shape[0]
    chunk = rows // 4

    def body(q_ref, k_ref, v_ref, mat, o0, o1, o2, o3):
        full = dot_nt(q_ref[...], mat[:, 0:group])
        full = full + dot_nt(k_ref[...], mat[:, group : 2 * group])
        full = (full + dot_nt(v_ref[...], mat[:, 2 * group : 3 * group])).astype(bf16)
        for r, o_ref in enumerate((o0, o1, o2, o3)):

            @pl.when(pl.program_id(0) == r)
            def _(o_ref=o_ref):
                o_ref[...] = full

    spec = pl.BlockSpec((chunk, group), lambda i: (i, 0))
    out = jax.ShapeDtypeStruct((chunk, width), bf16)
    return pl.pallas_call(
        body,
        grid=(4,),
        in_specs=[spec] * 3 + [WHOLE],
        out_specs=[WHOLE] * 4,
        out_shape=[out] * 4,
        compiler_params=kernel_params(),
        name="input_grads",
    )(grad_q, grad_k, grad_v, matrix)


def projection_grads(pieces, grad_q, grad_k, grad_v):
    chunk, width = pieces[0].shape
    group = grad_q.shape[1]

    def body(p0, p1, p2, p3, q_ref, k_ref, v_ref, o_ref, b_ref):
        for n, g_ref in enumerate((q_ref, k_ref, v_ref)):
            cols = slice(n * group, (n + 1) * group)
            acc = jnp.zeros((width, group), f32)
            for r, p_ref in enumerate((p0, p1, p2, p3)):
                acc = acc + dot_tn(p_ref[...], g_ref[r * chunk : (r + 1) * chunk, :])
            o_ref[:, cols] = acc.astype(bf16)
            b_ref[n : n + 1, :] = jnp.sum(g_ref[...].astype(f32), axis=0, keepdims=True)

    return pl.pallas_call(
        body,
        in_specs=[WHOLE] * 7,
        out_specs=[WHOLE] * 2,
        out_shape=[
            jax.ShapeDtypeStruct((width, 3 * group), bf16),
            jax.ShapeDtypeStruct((8, group), f32),
        ],
        compiler_params=kernel_params(),
        name="projection_grads",
    )(*pieces, grad_q, grad_k, grad_v)


def pack_local(params):
    return jnp.concatenate([params[9], params[11].T, params[5].T], axis=1)


def gather_all(local):
    parts = lax.all_gather(local, ("tensor", "dp"), axis=0, tiled=False)
    return parts.reshape(4, -1, local.shape[1])


def layer_forward(hidden, sent, context, params, matrix, weights, up_bias):
    low, high, place, query_marks, key_marks = context
    vectors = jnp.stack([params[6], params[7], params[8], params[12], params[13], params[14]])
    vectors = jnp.concatenate([vectors, jnp.zeros_like(vectors[:2])], axis=0)
    chunks = gather_chunks(sent)
    queries, keys, values = project(
        chunks, matrix, params[3], params[4], query_marks, key_marks
    )
    contexts, queries = attention_forward(low, high, place, queries, keys, values)
    pieces = exchange_pieces([contexts[r] for r in range(4)])
    out, out_low, normed, act, slope, y1, y2, r1, r2 = tokens_forward(
        place, hidden, pieces, weights, up_bias, vectors
    )
    saved = (chunks, queries, keys, values, contexts, pieces, normed, act, slope, y1, y2, r1, r2)
    return out, out_low, saved + (vectors,)


def layer_backward(grad, context, params, matrix, weights, saved):
    low, high, place = context[:3]
    chunks, queries, keys, values, contexts, pieces, normed, act, slope = saved[:9]
    y1, y2, r1, r2, vectors = saved[9:]
    width = grad.shape[1]
    group = pieces[0].shape[1] // 2
    (branch, inner, first, attn), sends, sums = tokens_backward(
        place, grad, (slope, y1, y2, r1, r2), weights, vectors, group
    )
    grads = exchange_pieces(sends)
    packed = weight_grads(place, normed, inner, branch, act, attn, pieces)
    wide = lax.psum_scatter(
        packed.reshape(4 * width, -1), ("tensor", "dp"), scatter_dimension=0, tiled=True
    ).astype(f32)
    grad_q, grad_k, grad_v = attention_backward(
        low, high, place, queries, keys, values, contexts, grads
    )
    partial = input_grads(grad_q, grad_k, grad_v, matrix)
    grad_in = first + scatter_chunks(partial)
    proj, proj_bias = projection_grads(chunks, grad_q, grad_k, grad_v)
    narrow = lax.psum_scatter(proj, "dp", scatter_dimension=0, tiled=True).astype(f32)
    sums = butterfly(sums, ("tensor", "dp"))
    proj_bias = butterfly(proj_bias, ("dp",))
    up_rows = lax.dynamic_slice_in_dim(sums, 6 + place[0], 1, 0)[0]
    out = (
        narrow[:, 0:group],
        narrow[:, group : 2 * group],
        narrow[:, 2 * group : 3 * group],
        proj_bias[0],
        proj_bias[2],
        wide[:, 2 * width : 2 * width + group].T,
        sums[5],
        sums[3],
        sums[4],
        wide[:, 0:width],
        up_rows,
        wide[:, width : 2 * width].T,
        sums[2],
        sums[0],
        sums[1],
    )
    return grad_in, out


def block_bounds(segments, place):
    total = segments.shape[0]
    blocks = segments.reshape(-1, TILE)
    begin = jnp.sum((segments[None] < blocks[:, :1]).astype(jnp.int32), axis=1) // TILE
    end = jnp.sum((segments[None] <= blocks[:, -1:]).astype(jnp.int32), axis=1)
    end = (end + TILE - 1) // TILE
    both = jnp.stack([begin, end]).reshape(2, 4, -1)
    both = reorder(both, place, 1).reshape(2, total // TILE)
    return both[0], both[1]


def reorder(values, place, axis):
    parts = [lax.dynamic_slice_in_dim(values, place ^ r, 1, axis) for r in range(4)]
    return jnp.concatenate(parts, axis=axis)


def on_device(tokens, segment_ids, valid_mask, teacher, *params):
    ask_params, doc_params = params[:15], params[15:]
    rows, width = tokens.shape
    place = lax.axis_index("tensor")
    segments = segment_ids[0]
    low, high = block_bounds(segments, place)
    local = reorder(segments.reshape(4, rows), place, 0).reshape(-1)
    same = local[:, None] == jnp.arange(SEGMENTS, dtype=jnp.int32)[None]
    spare = HEAD_DIM - SEGMENTS
    query_marks = jnp.pad(jnp.where(same, 0.0, -BLOCKED).astype(bf16), ((0, 0), (0, spare)))
    key_marks = jnp.concatenate(
        [same.astype(bf16), jnp.ones((4 * rows, 3), bf16), jnp.zeros((4 * rows, spare - 3), bf16)],
        axis=1,
    )
    context = (low, high, place[None], query_marks, key_marks)

    ask_matrix = lax.all_gather(
        jnp.concatenate(ask_params[0:3], axis=1), "dp", axis=0, tiled=True
    )
    doc_local = jnp.concatenate(doc_params[0:3], axis=1)
    group3 = doc_local.shape[1]
    doc_local = jnp.pad(doc_local, ((0, 0), (0, LANES)))
    ask_weights = gather_all(pack_local(ask_params))
    doc_matrix = lax.all_gather(doc_local, "dp", axis=0, tiled=True)[:, :group3]
    doc_weights = gather_all(pack_local(doc_params))
    up_local = jnp.stack([ask_params[10], doc_params[10]])
    up_all = jnp.stack([up_local] + [flip(up_local, r) for r in range(1, 4)])
    up_all = reorder(up_all, place, 0)

    mask_rows = valid_mask.astype(f32)
    valid_total = butterfly(
        jnp.full((8, LANES), jnp.sum(mask_rows), f32), ("tensor", "dp")
    )[0, 0]
    all_rows = rows * lax.axis_size("dp") * lax.axis_size("tensor")

    middle, middle_low, ask_saved = layer_forward(
        tokens, tokens, context, ask_params, ask_matrix, ask_weights, up_all[:, 0]
    )
    final, final_low, doc_saved = layer_forward(
        middle, middle_low, context, doc_params, doc_matrix, doc_weights, up_all[:, 1]
    )
    grad_final = mask_rows[:, None] * (final - teacher.astype(f32)) * (all_rows / valid_total)
    grad_middle, doc_grads = layer_backward(
        grad_final, context, doc_params, doc_matrix, doc_weights, doc_saved
    )
    grad_input, ask_grads = layer_backward(
        grad_middle, context, ask_params, ask_matrix, ask_weights, ask_saved
    )
    return (final_low, grad_input) + ask_grads + doc_grads


def layer_specs():
    return (
        P("dp", "tensor"),
        P("dp", "tensor"),
        P("dp", "tensor"),
        P("tensor"),
        P("tensor"),
        P("tensor", "dp"),
        P(),
        P(),
        P(),
        P("dp", "tensor"),
        P("tensor"),
        P("tensor", "dp"),
        P(),
        P(),
        P(),
    )


def solution(mesh):
    rows = P(("dp", "tensor"), None)
    return jax.shard_map(
        on_device,
        mesh=mesh,
        in_specs=(rows, P("dp", None), P(("dp", "tensor")), rows) + layer_specs() * 2,
        out_specs=(rows, rows) + layer_specs() * 2,
        check_vma=False,
    )
```

```python
import jax
import jax.numpy as jnp
from jax import lax
from jax.experimental import pallas as pl
from jax.experimental.pallas import tpu as pltpu
from jax.sharding import PartitionSpec as P

HEAD_DIM = 64
LANES = 128
TILE = 256
BLOCKED = 1e9
SEGMENTS = 16
eps_norm = 1e-12

bf16 = jnp.bfloat16
f32 = jnp.float32
NT = (((1,), (1,)), ((), ()))
TN = (((0,), (0,)), ((), ()))
WHOLE = pl.BlockSpec(memory_space=pltpu.VMEM)


def dot_nn(first_mat, second_mat):
    return jnp.dot(first_mat, second_mat, preferred_element_type=f32)


def dot_nt(first_mat, second_mat):
    return lax.dot_general(first_mat, second_mat, NT, preferred_element_type=f32)


def dot_tn(first_mat, second_mat):
    return lax.dot_general(first_mat, second_mat, TN, preferred_element_type=f32)


def cost(flops):
    return pl.CostEstimate(flops=int(flops), bytes_accessed=0, transcendentals=0)


def kernel_params():
    return pltpu.CompilerParams(vmem_limit_bytes=60 * 1024 * 1024)


def flip(values, bit):
    size = lax.axis_size("tensor")
    return lax.ppermute(values, "tensor", [(i, i ^ bit) for i in range(size)])


def gather_chunks(own):
    half = own.shape[0] // 2
    near = flip(own, 1)
    far = [flip(own[:half], 2), flip(own[half:], 2)]
    last = [flip(part, 1) for part in far]
    return own, near, jnp.concatenate(far, axis=0), jnp.concatenate(last, axis=0)


def exchange_pieces(pieces):
    return [pieces[0]] + [flip(pieces[r], r) for r in range(1, 4)]


def scatter_chunks(chunks):
    crossing = chunks[2].astype(f32) + flip(chunks[3], 1).astype(f32)
    near = flip(chunks[1], 1).astype(f32)
    far = flip(crossing.astype(bf16), 2).astype(f32)
    return chunks[0].astype(f32) + near + far


def tie(*items):
    return lax.optimization_barrier(items)


def send_around(values, axis, step, count):
    size = lax.axis_size(axis)
    return [
        lax.ppermute(values, axis, [(i, i ^ (step * r)) for i in range(size)])
        for r in range(1, count)
    ]


def add_up(values, others):
    for other in others:
        values = values + other
    return values


def sum_over(values, axis):
    size = lax.axis_size(axis)
    step = 1
    while step < size:
        count = min(8, size // step)
        values = add_up(values, send_around(values, axis, step, count))
        step *= count
    return values


def project(pieces, matrix, query_bias, value_bias, query_marks, key_marks):
    rows, width = pieces[0].shape
    heads = matrix.shape[1] // 3 // HEAD_DIM
    group = heads * HEAD_DIM
    wide = heads * LANES
    sub = rows // 2

    def body(p0, p1, p2, p3, mat, bias_q, bias_v, mark_q, mark_k, out_q, out_k, out_v):
        chunk = pl.program_id(0)
        lane = lax.broadcasted_iota(jnp.int32, (sub, HEAD_DIM), 1)
        ones = jnp.where(lane < 2, 1.0, 0.0).astype(bf16)

        def run(piece):
            for part in range(2):
                at = slice(part * sub, (part + 1) * sub)
                full = dot_nn(piece[at, :], mat[...])
                for h in range(heads):
                    lo = h * HEAD_DIM
                    to = slice(h * LANES, (h + 1) * LANES)
                    q = full[:, lo : lo + HEAD_DIM] + bias_q[:, lo : lo + HEAD_DIM]
                    q = (q.astype(bf16).astype(f32) * HEAD_DIM ** (-0.5)).astype(bf16)
                    k = full[:, group + lo : group + lo + HEAD_DIM].astype(bf16)
                    v = full[:, 2 * group + lo : 2 * group + lo + HEAD_DIM]
                    v = (v + bias_v[:, lo : lo + HEAD_DIM]).astype(bf16)
                    out_q[at, to] = jnp.concatenate([q, mark_q[at, :]], axis=1)
                    out_k[at, to] = jnp.concatenate([k, mark_k[at, :]], axis=1)
                    out_v[at, to] = jnp.concatenate([v, ones], axis=1)

        for r, piece in enumerate((p0, p1, p2, p3)):

            @pl.when(chunk == r)
            def _(piece=piece):
                run(piece)

    out = jax.ShapeDtypeStruct((4 * rows, wide), bf16)
    spec = pl.BlockSpec((rows, wide), lambda i: (i, 0))
    mark_spec = pl.BlockSpec((rows, HEAD_DIM), lambda i: (i, 0))
    return pl.pallas_call(
        body,
        grid=(4,),
        in_specs=[WHOLE] * 7 + [mark_spec] * 2,
        out_specs=[spec] * 3,
        out_shape=[out] * 3,
        compiler_params=kernel_params(),
        cost_estimate=cost(6 * rows * 4 * pieces[0].shape[1] * matrix.shape[1]),
        name="project",
    )(*pieces, matrix, query_bias[None], value_bias[None], query_marks, key_marks)


def attention_forward(low, high, place, queries, keys, values):
    rows, wide = queries.shape
    heads = wide // LANES
    count = rows // TILE
    per_chunk = count // 4
    half = rows // 8
    half_blocks = half // TILE
    group = heads * HEAD_DIM

    def body(
        low_ref, high_ref, place_ref, q_ref, k_ref, v_ref, ctx_ref, ql_ref, score, peak, total
    ):
        block = pl.program_id(0)
        own = place_ref[0]
        first = low_ref[block]
        last = high_ref[block]
        peak[...] = jnp.full_like(peak, -3e38)
        total[...] = jnp.zeros_like(total)
        q_heads = [q_ref[:, h * LANES : (h + 1) * LANES] for h in range(heads)]

        def where_is(j):
            spot = ((j // per_chunk) ^ own) * per_chunk + j % per_chunk
            return pl.multiple_of(spot * TILE, TILE)

        def score_step(j, carry):
            at = where_is(j)
            for h in range(heads):
                s = dot_nt(q_heads[h], k_ref[pl.ds(at, TILE), h * LANES : (h + 1) * LANES])
                score[h, j - first] = s
                top = s[:, 0:LANES]
                for c in range(1, TILE // LANES):
                    top = jnp.maximum(top, s[:, c * LANES : (c + 1) * LANES])
                peak[h] = jnp.maximum(peak[h], top)
            return carry

        lax.fori_loop(first, last, score_step, 0)
        tops = []
        for h in range(heads):
            top = jnp.max(peak[h], axis=1, keepdims=True)
            tops.append(top)
            peak[h] = jnp.broadcast_to(top, (TILE, LANES))

        def sum_step(j, carry):
            at = where_is(j)
            for h in range(heads):
                top = peak[h]
                parts = [
                    jnp.exp(score[h, j - first, :, c * LANES : (c + 1) * LANES] - top)
                    for c in range(TILE // LANES)
                ]
                p = jnp.concatenate(parts, axis=1).astype(bf16)
                total[h] += dot_nn(p, v_ref[pl.ds(at, TILE), h * LANES : (h + 1) * LANES])
            return carry

        lax.fori_loop(first, last, sum_step, 0)
        lane = lax.broadcasted_iota(jnp.int32, (TILE, LANES), 1)
        outs = []
        for h in range(heads):
            acc = total[h]
            norm = acc[:, HEAD_DIM : HEAD_DIM + 1]
            outs.append((acc[:, 0:HEAD_DIM] * (1.0 / norm)).astype(bf16))
            shift = -(tops[h] + jnp.log(norm))
            one = shift.astype(bf16).astype(f32)
            two = (shift - one).astype(bf16).astype(f32)
            three = shift - one - two
            q = q_heads[h].astype(f32)
            q = jnp.where(lane == HEAD_DIM + SEGMENTS, one, q)
            q = jnp.where(lane == HEAD_DIM + SEGMENTS + 1, two, q)
            q = jnp.where(lane == HEAD_DIM + SEGMENTS + 2, three, q)
            ql_ref[:, h * LANES : (h + 1) * LANES] = q.astype(bf16)
        ctx = jnp.concatenate(outs, axis=1)
        inside = block % per_chunk
        at = pl.multiple_of((inside % half_blocks) * TILE, TILE)

        @pl.when(inside < half_blocks)
        def _():
            ctx_ref[0, pl.ds(at, TILE), 0:group] = ctx

        @pl.when(inside >= half_blocks)
        def _():
            ctx_ref[0, pl.ds(at, TILE), group : 2 * group] = ctx

    row_spec = pl.BlockSpec((TILE, wide), lambda i, *_: (i, 0))
    return pl.pallas_call(
        body,
        grid_spec=pltpu.PrefetchScalarGridSpec(
            num_scalar_prefetch=3,
            grid=(count,),
            in_specs=[row_spec, WHOLE, WHOLE],
            out_specs=[
                pl.BlockSpec((1, half, 2 * group), lambda i, *_: (i // per_chunk, 0, 0)),
                row_spec,
            ],
            scratch_shapes=[
                pltpu.VMEM((heads, count, TILE, TILE), f32),
                pltpu.VMEM((heads, TILE, LANES), f32),
                pltpu.VMEM((heads, TILE, LANES), f32),
            ],
        ),
        out_shape=[
            jax.ShapeDtypeStruct((4, half, 2 * group), bf16),
            jax.ShapeDtypeStruct((rows, wide), bf16),
        ],
        compiler_params=kernel_params(),
        cost_estimate=cost(12 * rows * rows * wide),
        name="attention_forward",
    )(low, high, place, queries, keys, values)


def attention_backward(low, high, place, queries, keys, values, contexts, grads):
    rows, wide = queries.shape
    heads = wide // LANES
    count = rows // TILE
    per_chunk = count // 4
    half = rows // 8
    half_blocks = half // TILE
    group = heads * HEAD_DIM

    def body(low_ref, high_ref, place_ref, q_ref, k_ref, v_ref, c_ref, g0, g1, g2, g3, *rest):
        dq_ref, dk_ref, dv_ref, do_all, dq_all, acc_k, acc_v = rest
        block = pl.program_id(0)
        own = place_ref[0]
        first = low_ref[block]
        last = high_ref[block]

        @pl.when(block == 0)
        def _():
            dq_all[...] = jnp.zeros_like(dq_all)
            lane = lax.broadcasted_iota(jnp.int32, (TILE, HEAD_DIM), 1)
            for chunk, g_ref in enumerate((g0, g1, g2, g3)):

                def prepare(b, carry, chunk=chunk, g_ref=g_ref):
                    at = pl.multiple_of(b * TILE, TILE)
                    for side in range(2):
                        cols = slice(side * group, (side + 1) * group)
                        row = pl.multiple_of((2 * chunk + side) * half + at, TILE)
                        c = c_ref[chunk, pl.ds(at, TILE), cols].astype(f32)
                        g = g_ref[pl.ds(at, TILE), cols].astype(f32)
                        for h in range(heads):
                            lo = h * HEAD_DIM
                            gh = g[:, lo : lo + HEAD_DIM]
                            ch = c[:, lo : lo + HEAD_DIM]
                            delta = -jnp.sum(gh * ch, axis=1, keepdims=True)
                            one = delta.astype(bf16).astype(f32)
                            two = delta - one
                            tail = jnp.where(lane == 0, one, jnp.where(lane == 1, two, 0.0))
                            both = jnp.concatenate([gh, tail], axis=1).astype(bf16)
                            do_all[pl.ds(row, TILE), h * LANES : (h + 1) * LANES] = both
                    return carry

                lax.fori_loop(0, half_blocks, prepare, 0)

        acc_k[...] = jnp.zeros_like(acc_k)
        acc_v[...] = jnp.zeros_like(acc_v)

        def step(j, carry):
            spot = ((j // per_chunk) ^ own) * per_chunk + j % per_chunk
            at = pl.multiple_of(spot * TILE, TILE)
            for h in range(heads):
                to = slice(h * LANES, (h + 1) * LANES)
                q = q_ref[pl.ds(at, TILE), to]
                k = k_ref[:, to]
                do = do_all[pl.ds(at, TILE), to]
                p = jnp.exp(dot_nt(k, q))
                ds = (p * dot_nt(v_ref[:, to], do)).astype(bf16)
                acc_v[h] += dot_nn(p.astype(bf16), do)
                acc_k[h] += dot_nn(ds, q)
                dq_all[pl.ds(at, TILE), to] += dot_tn(ds, k)
            return carry

        lax.fori_loop(first, last, step, 0)
        dk = [acc_k[h, :, 0:HEAD_DIM] for h in range(heads)]
        dv = [acc_v[h, :, 0:HEAD_DIM] for h in range(heads)]
        dk_ref[...] = jnp.concatenate(dk, axis=1).astype(bf16)
        dv_ref[...] = jnp.concatenate(dv, axis=1).astype(bf16)

        @pl.when(block == count - 1)
        def _():
            def finish(b, carry):
                at = pl.multiple_of(b * TILE, TILE)
                dq = [
                    dq_all[pl.ds(at, TILE), h * LANES : h * LANES + HEAD_DIM] for h in range(heads)
                ]
                dq = jnp.concatenate(dq, axis=1) * HEAD_DIM ** (-0.5)
                dq_ref[pl.ds(at, TILE), :] = dq.astype(bf16)
                return carry

            lax.fori_loop(0, count, finish, 0)

    row_spec = pl.BlockSpec((TILE, wide), lambda i, *_: (i, 0))
    out_spec = pl.BlockSpec((TILE, group), lambda i, *_: (i, 0))
    out = jax.ShapeDtypeStruct((rows, group), bf16)
    return pl.pallas_call(
        body,
        grid_spec=pltpu.PrefetchScalarGridSpec(
            num_scalar_prefetch=3,
            grid=(count,),
            in_specs=[WHOLE, row_spec, row_spec] + [WHOLE] * 5,
            out_specs=[WHOLE, out_spec, out_spec],
            scratch_shapes=[
                pltpu.VMEM((rows, wide), bf16),
                pltpu.VMEM((rows, wide), f32),
                pltpu.VMEM((heads, TILE, LANES), f32),
                pltpu.VMEM((heads, TILE, LANES), f32),
            ],
        ),
        out_shape=[out] * 3,
        compiler_params=kernel_params(),
        cost_estimate=cost(24 * rows * rows * wide),
        name="attention_backward",
    )(low, high, place, queries, keys, values, contexts, *grads)


SQRT_HALF = 0.7071067811865476
PHI_SCALE = 0.3989422804014327


def norm_parts(values):
    centered = values - jnp.mean(values, axis=-1, keepdims=True)
    variance = jnp.mean(centered * centered, axis=-1, keepdims=True)
    scale = lax.rsqrt(variance + eps_norm)
    return centered * scale, scale


def tokens_forward(place, hidden, pieces, weights, up_bias, vectors):
    rows, width = hidden.shape
    half = rows // 2
    group = pieces[0].shape[1] // 2
    part = TILE
    steps = half // part
    size = 2 * part

    def body(place_ref, x_ref, c0, c1, c2, c3, w_ref, ub_ref, vec_ref, *outs):
        o_ref, ob_ref, nb_ref, act_ref, slope_ref, y1_ref, y2_ref, r1_ref, r2_ref = outs
        own = place_ref[0]
        first = x_ref[...].reshape(size, width).astype(f32) + vec_ref[0:1, :]
        for r, c_ref in enumerate((c0, c1, c2, c3)):
            ctx = jnp.concatenate([c_ref[:, 0:group], c_ref[:, group : 2 * group]], axis=0)
            first = first + dot_nt(ctx, w_ref[own ^ r, :, 2 * width : 2 * width + group])
        y1, r1 = norm_parts(first)
        y1_ref[...] = y1.reshape(2, part, width)
        r1_ref[...] = jnp.broadcast_to(r1, (size, LANES)).reshape(2, part, LANES)
        normed = y1 * vec_ref[1:2, :] + vec_ref[2:3, :]
        sent = normed.astype(bf16)
        nb_ref[...] = sent.reshape(2, part, width)
        second = normed + vec_ref[3:4, :]
        for t in range(4):
            cols = slice(t * width, (t + 1) * width)
            inner = dot_nn(sent, w_ref[t, :, 0:width]) + ub_ref[t : t + 1, :]
            cdf = 0.5 + 0.5 * lax.erf(inner * SQRT_HALF)
            act = (inner * cdf).astype(bf16)
            slope = cdf + inner * (PHI_SCALE * jnp.exp(-0.5 * inner * inner))
            act_ref[:, :, cols] = act.reshape(2, part, width)
            slope_ref[:, :, cols] = slope.astype(bf16).reshape(2, part, width)
            second = second + dot_nt(act, w_ref[t, :, width : 2 * width])
        y2, r2 = norm_parts(second)
        y2_ref[...] = y2.reshape(2, part, width)
        r2_ref[...] = jnp.broadcast_to(r2, (size, LANES)).reshape(2, part, LANES)
        result = y2 * vec_ref[4:5, :] + vec_ref[5:6, :]
        o_ref[...] = result.reshape(2, part, width)
        ob_ref[...] = result.astype(bf16).reshape(2, part, width)

    def spec(cols):
        return pl.BlockSpec((2, part, cols), lambda i, *_: (0, i, 0))

    def out(cols, kind):
        return jax.ShapeDtypeStruct((2, half, cols), kind)

    piece_spec = pl.BlockSpec((part, 2 * group), lambda i, *_: (i, 0))
    units = 4 * width
    results = pl.pallas_call(
        body,
        grid_spec=pltpu.PrefetchScalarGridSpec(
            num_scalar_prefetch=1,
            grid=(steps,),
            in_specs=[spec(width)] + [piece_spec] * 4 + [WHOLE] * 3,
            out_specs=[
                spec(width),
                spec(width),
                spec(width),
                spec(units),
                spec(units),
                spec(width),
                spec(width),
                spec(LANES),
                spec(LANES),
            ],
        ),
        out_shape=[
            out(width, f32),
            out(width, bf16),
            out(width, bf16),
            out(units, bf16),
            out(units, bf16),
            out(width, f32),
            out(width, f32),
            out(LANES, f32),
            out(LANES, f32),
        ],
        compiler_params=kernel_params(),
        cost_estimate=cost(8 * rows * width * width * 3),
        name="tokens_forward",
    )(place, hidden.reshape(2, half, width), *pieces, weights, up_bias, vectors)
    return [item.reshape(rows, item.shape[2]) for item in results]


def tokens_backward(place, grad, saved, weights, vectors, group):
    slope, y1, y2, r1, r2 = saved
    rows, width = grad.shape
    half = rows // 2
    part = TILE
    steps = half // part
    size = 2 * part
    units = 4 * width

    def norm_back(g, y, r, gain):
        e = g * gain
        mean_e = jnp.mean(e, axis=-1, keepdims=True)
        mean_ey = jnp.mean(e * y, axis=-1, keepdims=True)
        return r * (e - mean_e - y * mean_ey)

    def body(place_ref, g_ref, sl_ref, y1_ref, y2_ref, r1_ref, r2_ref, w_ref, vec_ref, *outs):
        bg_ref, gi_ref, gf_ref, ag_ref, p0, p1, p2, p3, sum_ref = outs
        own = place_ref[0]

        @pl.when(pl.program_id(0) == 0)
        def _():
            sum_ref[...] = jnp.zeros_like(sum_ref)

        def total(values):
            return jnp.sum(values, axis=0, keepdims=True)

        g = g_ref[...].reshape(size, width)
        y2 = y2_ref[...].reshape(size, width)
        r2 = r2_ref[...].reshape(size, LANES)[:, 0:1]
        second = norm_back(g, y2, r2, vec_ref[4:5, :])
        sum_ref[0:1, :] += total(g * y2)
        sum_ref[1:2, :] += total(g)
        sum_ref[2:3, :] += total(second)
        branch = second.astype(bf16)
        bg_ref[...] = branch.reshape(2, part, width)
        normed = second
        for t in range(4):
            cols = slice(t * width, (t + 1) * width)
            slope_t = sl_ref[:, :, cols].reshape(size, width).astype(f32)
            inner = (dot_nn(branch, w_ref[t, :, width : 2 * width]) * slope_t).astype(bf16)
            gi_ref[:, :, cols] = inner.reshape(2, part, width)
            sum_ref[6 + t : 7 + t, :] += total(inner.astype(f32))
            normed = normed + dot_nt(inner, w_ref[t, :, 0:width])
        y1 = y1_ref[...].reshape(size, width)
        r1 = r1_ref[...].reshape(size, LANES)[:, 0:1]
        first = norm_back(normed, y1, r1, vec_ref[1:2, :])
        sum_ref[3:4, :] += total(normed * y1)
        sum_ref[4:5, :] += total(normed)
        sum_ref[5:6, :] += total(first)
        gf_ref[...] = first.reshape(2, part, width)
        sent = first.astype(bf16)
        ag_ref[...] = sent.reshape(2, part, width)
        for r, p_ref in enumerate((p0, p1, p2, p3)):
            ctx = dot_nn(sent, w_ref[own ^ r, :, 2 * width : 2 * width + group]).astype(bf16)
            p_ref[...] = jnp.concatenate([ctx[0:part], ctx[part:size]], axis=1)

    def spec(cols):
        return pl.BlockSpec((2, part, cols), lambda i, *_: (0, i, 0))

    def out(cols, kind):
        return jax.ShapeDtypeStruct((2, half, cols), kind)

    piece_spec = pl.BlockSpec((part, 2 * group), lambda i, *_: (i, 0))
    piece = jax.ShapeDtypeStruct((half, 2 * group), bf16)
    sums = jax.ShapeDtypeStruct((16, width), f32)

    def view(values):
        return values.reshape(2, half, values.shape[1])

    results = pl.pallas_call(
        body,
        grid_spec=pltpu.PrefetchScalarGridSpec(
            num_scalar_prefetch=1,
            grid=(steps,),
            in_specs=[
                spec(width),
                spec(units),
                spec(width),
                spec(width),
                spec(LANES),
                spec(LANES),
                WHOLE,
                WHOLE,
            ],
            out_specs=[spec(width), spec(units), spec(width), spec(width)]
            + [piece_spec] * 4
            + [pl.BlockSpec((16, width), lambda i, *_: (0, 0))],
        ),
        out_shape=[out(width, bf16), out(units, bf16), out(width, f32), out(width, bf16)]
        + [piece] * 4
        + [sums],
        compiler_params=kernel_params(),
        cost_estimate=cost(8 * rows * width * width * 3),
        name="tokens_backward",
    )(place, view(grad), view(slope), view(y1), view(y2), view(r1), view(r2), weights, vectors)
    big = [item.reshape(rows, item.shape[2]) for item in results[:4]]
    return big, list(results[4:8]), results[8]


def weight_grads(place, sent, inner, branch, act, attn, pieces):
    rows, width = sent.shape
    half = rows // 2
    group = pieces[0].shape[1] // 2

    def body(place_ref, s_ref, i_ref, b_ref, a_ref, g_ref, c0, c1, c2, c3, o_ref):
        t = pl.program_id(0)
        own = place_ref[0]
        o_ref[0, :, 0:width] = dot_tn(s_ref[...], i_ref[...]).astype(bf16)
        o_ref[0, :, width : 2 * width] = dot_tn(b_ref[...], a_ref[...]).astype(bf16)
        for r, c_ref in enumerate((c0, c1, c2, c3)):

            @pl.when(t == own ^ r)
            def _(c_ref=c_ref):
                ctx = jnp.concatenate([c_ref[:, 0:group], c_ref[:, group : 2 * group]], axis=0)
                o_ref[0, :, 2 * width : 2 * width + group] = dot_tn(g_ref[...], ctx).astype(bf16)

    unit_spec = pl.BlockSpec((rows, width), lambda i, *_: (0, i))
    cols = 2 * width + group
    return pl.pallas_call(
        body,
        grid_spec=pltpu.PrefetchScalarGridSpec(
            num_scalar_prefetch=1,
            grid=(4,),
            in_specs=[WHOLE, unit_spec, WHOLE, unit_spec, WHOLE] + [WHOLE] * 4,
            out_specs=pl.BlockSpec((1, width, cols), lambda i, *_: (i, 0, 0)),
        ),
        out_shape=jax.ShapeDtypeStruct((4, width, cols), bf16),
        compiler_params=kernel_params(),
        cost_estimate=cost(8 * rows * width * width * 3),
        name="weight_grads",
    )(place, sent, inner, branch, act, attn, *pieces)


def input_grads(grad_q, grad_k, grad_v, matrix):
    rows, group = grad_q.shape
    width = matrix.shape[0]
    chunk = rows // 4

    def body(q_ref, k_ref, v_ref, mat, o0, o1, o2, o3):
        full = dot_nt(q_ref[...], mat[:, 0:group])
        full = full + dot_nt(k_ref[...], mat[:, group : 2 * group])
        full = (full + dot_nt(v_ref[...], mat[:, 2 * group : 3 * group])).astype(bf16)
        for r, o_ref in enumerate((o0, o1, o2, o3)):

            @pl.when(pl.program_id(0) == r)
            def _(o_ref=o_ref):
                o_ref[...] = full

    spec = pl.BlockSpec((chunk, group), lambda i: (i, 0))
    out = jax.ShapeDtypeStruct((chunk, width), bf16)
    return pl.pallas_call(
        body,
        grid=(4,),
        in_specs=[spec] * 3 + [WHOLE],
        out_specs=[WHOLE] * 4,
        out_shape=[out] * 4,
        compiler_params=kernel_params(),
        cost_estimate=cost(6 * rows * width * 3 * group),
        name="input_grads",
    )(grad_q, grad_k, grad_v, matrix)


def projection_grads(pieces, grad_q, grad_k, grad_v):
    chunk, width = pieces[0].shape
    group = grad_q.shape[1]

    def body(p0, p1, p2, p3, q_ref, k_ref, v_ref, o_ref, b_ref):
        for n, g_ref in enumerate((q_ref, k_ref, v_ref)):
            cols = slice(n * group, (n + 1) * group)
            acc = jnp.zeros((width, group), f32)
            for r, p_ref in enumerate((p0, p1, p2, p3)):
                acc = acc + dot_tn(p_ref[...], g_ref[r * chunk : (r + 1) * chunk, :])
            o_ref[:, cols] = acc.astype(bf16)
            b_ref[n : n + 1, :] = jnp.sum(g_ref[...].astype(f32), axis=0, keepdims=True)

    return pl.pallas_call(
        body,
        in_specs=[WHOLE] * 7,
        out_specs=[WHOLE] * 2,
        out_shape=[
            jax.ShapeDtypeStruct((width, 3 * group), bf16),
            jax.ShapeDtypeStruct((8, group), f32),
        ],
        compiler_params=kernel_params(),
        cost_estimate=cost(24 * chunk * width * 3 * group),
        name="projection_grads",
    )(*pieces, grad_q, grad_k, grad_v)


def pack_local(params):
    return jnp.concatenate([params[9], params[11].T, params[5].T], axis=1)


def gather_all(local):
    parts = lax.all_gather(local, ("tensor", "dp"), axis=0, tiled=False)
    return parts.reshape(4, -1, local.shape[1])


def layer_forward(hidden, chunks, context, params, matrix, weights, up_bias, ahead=None):
    low, high, place, query_marks, key_marks = context
    vectors = jnp.stack([params[6], params[7], params[8], params[12], params[13], params[14]])
    vectors = jnp.concatenate([vectors, jnp.zeros_like(vectors[:2])], axis=0)
    queries, keys, values = project(
        chunks, matrix, params[3], params[4], query_marks, key_marks
    )
    contexts, queries = attention_forward(low, high, place, queries, keys, values)
    contexts, ahead = tie(contexts, ahead)
    pieces = exchange_pieces([contexts[r] for r in range(4)])
    out, out_low, normed, act, slope, y1, y2, r1, r2 = tokens_forward(
        place, hidden, pieces, weights, up_bias, vectors
    )
    saved = (chunks, queries, keys, values, contexts, pieces, normed, act, slope, y1, y2, r1, r2)
    return out, out_low, saved + (vectors,), ahead


def with_bias(proj, bias, parts):
    rows, cols = proj.shape
    high = bias.astype(bf16)
    low = (bias - high.astype(f32)).astype(bf16)
    tail = jnp.concatenate([high[None], low[None], jnp.zeros((14, cols), bf16)], axis=0)
    tail = jnp.broadcast_to(tail[None], (parts,) + tail.shape)
    return jnp.concatenate([proj.reshape(parts, rows // parts, cols), tail], axis=1)


def layer_backward(grad, context, matrix, weights, saved, earlier=None):
    low, high, place = context[:3]
    chunks, queries, keys, values, contexts, pieces, normed, act, slope = saved[:9]
    y1, y2, r1, r2, vectors = saved[9:]
    width = grad.shape[1]
    parts = lax.axis_size("dp")
    (branch, inner, first, attn), sends, sums = tokens_backward(
        place, grad, (slope, y1, y2, r1, r2), weights, vectors, pieces[0].shape[1] // 2
    )
    around = narrow = None
    if earlier is not None:
        sums = jnp.concatenate([earlier[0], sums], axis=0)
        around = send_around(sums, "tensor", 1, 4)
        narrow = lax.all_to_all(earlier[1], "dp", 0, 0, tiled=True)
    grads = exchange_pieces(sends)
    packed = weight_grads(place, normed, inner, branch, act, attn, pieces)
    grads, packed, around, narrow = tie(grads, packed, around, narrow)
    if earlier is not None:
        sums = sum_over(add_up(sums, around), "dp")
    wide = lax.psum_scatter(
        packed.reshape(4 * width, -1), ("tensor", "dp"), scatter_dimension=0, tiled=True
    ).astype(f32)
    grad_q, grad_k, grad_v = attention_backward(
        low, high, place, queries, keys, values, contexts, grads
    )
    if earlier is not None:
        grad_q, grad_k, grad_v, sums = tie(grad_q, grad_k, grad_v, sums)
    partial = input_grads(grad_q, grad_k, grad_v, matrix)
    grad_in = first + scatter_chunks(partial)
    proj, proj_bias = projection_grads(chunks, grad_q, grad_k, grad_v)
    both = with_bias(proj, proj_bias[0:3].reshape(-1), parts)
    if earlier is None:
        grad_in, wide, both = tie(grad_in, wide, both)
        return grad_in, wide, (sums, both)
    both, wide = tie(both, wide)
    both = lax.all_to_all(both, "dp", 0, 0, tiled=True)
    return grad_in, wide, (sums, both, narrow)


def layer_outputs(wide, narrow, sums, place):
    narrow = jnp.sum(narrow.astype(f32), axis=0)
    width = sums.shape[1]
    group = wide.shape[1] - 2 * width
    own = narrow.shape[0] - 16
    bias = narrow[own] + narrow[own + 1]
    up_row = lax.dynamic_slice_in_dim(sums, 6 + place[0], 1, 0)[0]
    return (
        narrow[:own, 0:group],
        narrow[:own, group : 2 * group],
        narrow[:own, 2 * group : 3 * group],
        bias[0:group],
        bias[2 * group : 3 * group],
        wide[:, 2 * width : 2 * width + group].T,
        sums[5],
        sums[3],
        sums[4],
        wide[:, 0:width],
        up_row,
        wide[:, width : 2 * width].T,
        sums[2],
        sums[0],
        sums[1],
    )


def block_bounds(segments, place):
    total = segments.shape[0]
    blocks = segments.reshape(-1, TILE)
    begin = jnp.sum((segments[None] < blocks[:, :1]).astype(jnp.int32), axis=1) // TILE
    end = jnp.sum((segments[None] <= blocks[:, -1:]).astype(jnp.int32), axis=1)
    end = (end + TILE - 1) // TILE
    both = jnp.stack([begin, end]).reshape(2, 4, -1)
    both = reorder(both, place, 1).reshape(2, total // TILE)
    return both[0], both[1]


def reorder(values, place, axis):
    parts = [lax.dynamic_slice_in_dim(values, place ^ r, 1, axis) for r in range(4)]
    return jnp.concatenate(parts, axis=axis)


def on_device(tokens, segment_ids, valid_mask, teacher, *params):
    ask_params, doc_params = params[:15], params[15:]
    rows, width = tokens.shape
    place = lax.axis_index("tensor")
    segments = segment_ids[0]
    low, high = block_bounds(segments, place)
    local = reorder(segments.reshape(4, rows), place, 0).reshape(-1)
    same = local[:, None] == jnp.arange(SEGMENTS, dtype=jnp.int32)[None]
    spare = HEAD_DIM - SEGMENTS
    query_marks = jnp.pad(jnp.where(same, 0.0, -BLOCKED).astype(bf16), ((0, 0), (0, spare)))
    key_marks = jnp.concatenate(
        [same.astype(bf16), jnp.ones((4 * rows, 3), bf16), jnp.zeros((4 * rows, spare - 3), bf16)],
        axis=1,
    )
    context = (low, high, place[None], query_marks, key_marks)

    ask_matrix = lax.all_gather(
        jnp.concatenate(ask_params[0:3], axis=1), "dp", axis=0, tiled=True
    )
    doc_local = jnp.concatenate(doc_params[0:3], axis=1)
    group3 = doc_local.shape[1]
    doc_local = jnp.pad(doc_local, ((0, 0), (0, LANES)))
    ask_weights = gather_all(pack_local(ask_params))
    doc_matrix = lax.all_gather(doc_local, "dp", axis=0, tiled=True)[:, :group3]
    up_local = jnp.stack([ask_params[10], doc_params[10]])
    up_all = jnp.stack([up_local] + [flip(up_local, r) for r in range(1, 4)])
    up_all = reorder(up_all, place, 0)

    mask_rows = valid_mask.astype(f32)
    valid_total = jnp.full((8, LANES), jnp.sum(mask_rows), f32)
    valid_total = sum_over(sum_over(valid_total, "tensor"), "dp")
    ask_matrix, up_all, valid_total = tie(ask_matrix, up_all, valid_total)
    valid_total = valid_total[0, 0]
    all_rows = rows * lax.axis_size("dp") * lax.axis_size("tensor")

    middle, middle_low, ask_saved, doc_matrix = layer_forward(
        tokens,
        gather_chunks(tokens),
        context,
        ask_params,
        ask_matrix,
        ask_weights,
        up_all[:, 0],
        doc_matrix,
    )
    doc_chunks, doc_pack = tie(gather_chunks(middle_low), pack_local(doc_params))
    doc_weights = gather_all(doc_pack)
    final, final_low, doc_saved, _ = layer_forward(
        middle, doc_chunks, context, doc_params, doc_matrix, doc_weights, up_all[:, 1]
    )
    grad_final = mask_rows[:, None] * (final - teacher.astype(f32)) * (all_rows / valid_total)
    grad_middle, doc_wide, pending = layer_backward(
        grad_final, context, doc_matrix, doc_weights, doc_saved
    )
    grad_input, ask_wide, (sums, ask_narrow, doc_narrow) = layer_backward(
        grad_middle, context, ask_matrix, ask_weights, ask_saved, pending
    )
    half = sums.shape[0] // 2
    doc_grads = layer_outputs(doc_wide, doc_narrow, sums[:half], context[2])
    ask_grads = layer_outputs(ask_wide, ask_narrow, sums[half:], context[2])
    return (final_low, grad_input) + ask_grads + doc_grads


def layer_specs():
    return (
        P("dp", "tensor"),
        P("dp", "tensor"),
        P("dp", "tensor"),
        P("tensor"),
        P("tensor"),
        P("tensor", "dp"),
        P(),
        P(),
        P(),
        P("dp", "tensor"),
        P("tensor"),
        P("tensor", "dp"),
        P(),
        P(),
        P(),
    )


def solution(mesh):
    rows = P(("dp", "tensor"), None)
    return jax.shard_map(
        on_device,
        mesh=mesh,
        in_specs=(rows, P("dp", None), P(("dp", "tensor")), rows) + layer_specs() * 2,
        out_specs=(rows, rows) + layer_specs() * 2,
        check_vma=False,
    )
```

```python
import jax
import jax.numpy as jnp
from jax import lax
from jax.experimental import pallas as pl
from jax.experimental.pallas import tpu as pltpu
from jax.sharding import PartitionSpec as P

HEAD_DIM = 64
LANES = 128
TILE = 256
BLOCKED = 1e9
SEGMENTS = 16
eps_norm = 1e-12

bf16 = jnp.bfloat16
f32 = jnp.float32
NT = (((1,), (1,)), ((), ()))
TN = (((0,), (0,)), ((), ()))
WHOLE = pl.BlockSpec(memory_space=pltpu.VMEM)


def dot_nn(first_mat, second_mat):
    return jnp.dot(first_mat, second_mat, preferred_element_type=f32)


def dot_nt(first_mat, second_mat):
    return lax.dot_general(first_mat, second_mat, NT, preferred_element_type=f32)


def dot_tn(first_mat, second_mat):
    return lax.dot_general(first_mat, second_mat, TN, preferred_element_type=f32)


def cost(flops):
    return pl.CostEstimate(flops=int(flops), bytes_accessed=0, transcendentals=0)


def kernel_params():
    return pltpu.CompilerParams(vmem_limit_bytes=60 * 1024 * 1024)


def flip(values, bit):
    size = lax.axis_size("tensor")
    return lax.ppermute(values, "tensor", [(i, i ^ bit) for i in range(size)])


def gather_chunks(own):
    half = own.shape[0] // 2
    near = flip(own, 1)
    far = [flip(own[:half], 2), flip(own[half:], 2)]
    last = [flip(part, 1) for part in far]
    return own, near, jnp.concatenate(far, axis=0), jnp.concatenate(last, axis=0)


def exchange_pieces(pieces):
    return [pieces[0]] + [flip(pieces[r], r) for r in range(1, 4)]


def scatter_chunks(chunks):
    crossing = chunks[2].astype(f32) + flip(chunks[3], 1).astype(f32)
    near = flip(chunks[1], 1).astype(f32)
    far = flip(crossing.astype(bf16), 2).astype(f32)
    return chunks[0].astype(f32) + near + far


def tie(*items):
    return lax.optimization_barrier(items)


def send_around(values, axis, step, count):
    size = lax.axis_size(axis)
    return [
        lax.ppermute(values, axis, [(i, i ^ (step * r)) for i in range(size)])
        for r in range(1, count)
    ]


def add_up(values, others):
    for other in others:
        values = values + other
    return values


def sum_over(values, axis):
    size = lax.axis_size(axis)
    step = 1
    while step < size:
        count = min(8, size // step)
        values = add_up(values, send_around(values, axis, step, count))
        step *= count
    return values


def project(pieces, matrix, query_bias, value_bias, query_marks, key_marks):
    rows, width = pieces[0].shape
    heads = matrix.shape[1] // 3 // HEAD_DIM
    group = heads * HEAD_DIM
    wide = heads * LANES
    sub = rows // 2

    def body(p0, p1, p2, p3, mat, bias_q, bias_v, mark_q, mark_k, out_q, out_k, out_v):
        chunk = pl.program_id(0)
        lane = lax.broadcasted_iota(jnp.int32, (sub, HEAD_DIM), 1)
        ones = jnp.where(lane < 2, 1.0, 0.0).astype(bf16)

        def run(piece):
            for part in range(2):
                at = slice(part * sub, (part + 1) * sub)
                full = dot_nn(piece[at, :], mat[...])
                for h in range(heads):
                    lo = h * HEAD_DIM
                    to = slice(h * LANES, (h + 1) * LANES)
                    q = full[:, lo : lo + HEAD_DIM] + bias_q[:, lo : lo + HEAD_DIM]
                    q = (q.astype(bf16).astype(f32) * HEAD_DIM ** (-0.5)).astype(bf16)
                    k = full[:, group + lo : group + lo + HEAD_DIM].astype(bf16)
                    v = full[:, 2 * group + lo : 2 * group + lo + HEAD_DIM]
                    v = (v + bias_v[:, lo : lo + HEAD_DIM]).astype(bf16)
                    out_q[at, to] = jnp.concatenate([q, mark_q[at, :]], axis=1)
                    out_k[at, to] = jnp.concatenate([k, mark_k[at, :]], axis=1)
                    out_v[at, to] = jnp.concatenate([v, ones], axis=1)

        for r, piece in enumerate((p0, p1, p2, p3)):

            @pl.when(chunk == r)
            def _(piece=piece):
                run(piece)

    out = jax.ShapeDtypeStruct((4 * rows, wide), bf16)
    spec = pl.BlockSpec((rows, wide), lambda i: (i, 0))
    mark_spec = pl.BlockSpec((rows, HEAD_DIM), lambda i: (i, 0))
    return pl.pallas_call(
        body,
        grid=(4,),
        in_specs=[WHOLE] * 7 + [mark_spec] * 2,
        out_specs=[spec] * 3,
        out_shape=[out] * 3,
        compiler_params=kernel_params(),
        cost_estimate=cost(6 * rows * 4 * pieces[0].shape[1] * matrix.shape[1]),
        name="project",
    )(*pieces, matrix, query_bias[None], value_bias[None], query_marks, key_marks)


def attention_forward(low, high, place, queries, keys, values):
    rows, wide = queries.shape
    heads = wide // LANES
    count = rows // TILE
    per_chunk = count // 4
    half = rows // 8
    half_blocks = half // TILE
    group = heads * HEAD_DIM

    def body(low_ref, high_ref, place_ref, q_ref, k_ref, v_ref, ctx_ref, ql_ref, *scratch):
        peak, fade, total, score = scratch
        block = pl.program_id(0)
        own = place_ref[0]
        first = low_ref[block]
        last = high_ref[block]
        peak[...] = jnp.full_like(peak, -3e38)
        total[...] = jnp.zeros_like(total)

        def where_is(j):
            spot = ((j // per_chunk) ^ own) * per_chunk + j % per_chunk
            return pl.multiple_of(spot * TILE, TILE)

        def rows_step(j):
            at = where_is(j)
            for h in range(heads):
                to = slice(h * LANES, (h + 1) * LANES)
                s = dot_nt(k_ref[pl.ds(at, TILE), to], q_ref[:, to])
                old = peak[h, 0:1, :]
                top = jnp.maximum(old, jnp.max(s, axis=0, keepdims=True))
                peak[h, 0:1, :] = top
                fade[h, 0:1, :] = jnp.exp(old - top)
                score[h] = s

        def sum_step(j):
            at = where_is(j)
            for h in range(heads):
                v = v_ref[pl.ds(at, TILE), h * LANES : (h + 1) * LANES]
                p = jnp.exp(score[h] - peak[h, 0:1, :]).astype(bf16)
                total[h] = total[h] * fade[h, 0:1, :] + dot_tn(v, p)

        def step(j, carry):
            sum_step(j - 1)
            rows_step(j)
            return carry

        rows_step(first)
        lax.fori_loop(first + 1, last, step, 0)
        sum_step(last - 1)
        feature = lax.broadcasted_iota(jnp.int32, (LANES, TILE), 0)
        lane = lax.broadcasted_iota(jnp.int32, (TILE, LANES), 1)
        mark = HEAD_DIM + SEGMENTS
        outs = []
        for h in range(heads):
            acc = total[h]
            norm = acc[HEAD_DIM : HEAD_DIM + 1, :]
            shift = -(peak[h, 0:1, :] + jnp.log(norm))
            one = shift.astype(bf16).astype(f32)
            two = (shift - one).astype(bf16).astype(f32)
            three = shift - one - two
            both = acc * (1.0 / norm)
            both = jnp.where(feature == mark, one, both)
            both = jnp.where(feature == mark + 1, two, both)
            both = jnp.where(feature == mark + 2, three, both)
            both = both.T.astype(bf16)
            outs.append(both[:, 0:HEAD_DIM])
            to = slice(h * LANES, (h + 1) * LANES)
            inside = (lane >= mark) & (lane < mark + 3)
            ql_ref[:, to] = jnp.where(inside, both, q_ref[:, to])
        ctx = jnp.concatenate(outs, axis=1)
        inside = block % per_chunk
        at = pl.multiple_of((inside % half_blocks) * TILE, TILE)

        @pl.when(inside < half_blocks)
        def _():
            ctx_ref[0, pl.ds(at, TILE), 0:group] = ctx

        @pl.when(inside >= half_blocks)
        def _():
            ctx_ref[0, pl.ds(at, TILE), group : 2 * group] = ctx

    row_spec = pl.BlockSpec((TILE, wide), lambda i, *_: (i, 0))
    return pl.pallas_call(
        body,
        grid_spec=pltpu.PrefetchScalarGridSpec(
            num_scalar_prefetch=3,
            grid=(count,),
            in_specs=[row_spec, WHOLE, WHOLE],
            out_specs=[
                pl.BlockSpec((1, half, 2 * group), lambda i, *_: (i // per_chunk, 0, 0)),
                row_spec,
            ],
            scratch_shapes=[
                pltpu.VMEM((heads, 8, TILE), f32),
                pltpu.VMEM((heads, 8, TILE), f32),
                pltpu.VMEM((heads, LANES, TILE), f32),
                pltpu.VMEM((heads, TILE, TILE), f32),
            ],
        ),
        out_shape=[
            jax.ShapeDtypeStruct((4, half, 2 * group), bf16),
            jax.ShapeDtypeStruct((rows, wide), bf16),
        ],
        compiler_params=kernel_params(),
        cost_estimate=cost(12 * rows * rows * wide),
        name="attention_forward",
    )(low, high, place, queries, keys, values)


def attention_backward(low, high, place, queries, keys, values, contexts, grads):
    rows, wide = queries.shape
    heads = wide // LANES
    count = rows // TILE
    per_chunk = count // 4
    half = rows // 8
    half_blocks = half // TILE
    group = heads * HEAD_DIM

    def body(low_ref, high_ref, place_ref, q_ref, k_ref, v_ref, c_ref, g0, g1, g2, g3, *rest):
        dq_ref, dk_ref, dv_ref, do_all, dq_all, acc_k, acc_v, prob, slope = rest
        block = pl.program_id(0)
        own = place_ref[0]
        first = low_ref[block]
        last = high_ref[block]

        @pl.when(block == 0)
        def _():
            dq_all[...] = jnp.zeros_like(dq_all)
            lane = lax.broadcasted_iota(jnp.int32, (TILE, HEAD_DIM), 1)
            for chunk, g_ref in enumerate((g0, g1, g2, g3)):

                def prepare(b, carry, chunk=chunk, g_ref=g_ref):
                    at = pl.multiple_of(b * TILE, TILE)
                    for side in range(2):
                        cols = slice(side * group, (side + 1) * group)
                        row = pl.multiple_of((2 * chunk + side) * half + at, TILE)
                        c = c_ref[chunk, pl.ds(at, TILE), cols].astype(f32)
                        g = g_ref[pl.ds(at, TILE), cols].astype(f32)
                        for h in range(heads):
                            lo = h * HEAD_DIM
                            gh = g[:, lo : lo + HEAD_DIM]
                            ch = c[:, lo : lo + HEAD_DIM]
                            delta = -jnp.sum(gh * ch, axis=1, keepdims=True)
                            one = delta.astype(bf16).astype(f32)
                            two = delta - one
                            tail = jnp.where(lane == 0, one, jnp.where(lane == 1, two, 0.0))
                            both = jnp.concatenate([gh, tail], axis=1).astype(bf16)
                            do_all[pl.ds(row, TILE), h * LANES : (h + 1) * LANES] = both
                    return carry

                lax.fori_loop(0, half_blocks, prepare, 0)

        acc_k[...] = jnp.zeros_like(acc_k)
        acc_v[...] = jnp.zeros_like(acc_v)

        def where_is(j):
            spot = ((j // per_chunk) ^ own) * per_chunk + j % per_chunk
            return pl.multiple_of(spot * TILE, TILE)

        def rows_step(j):
            at = where_is(j)
            for h in range(heads):
                to = slice(h * LANES, (h + 1) * LANES)
                p = jnp.exp(dot_nt(k_ref[:, to], q_ref[pl.ds(at, TILE), to]))
                dp = dot_nt(v_ref[:, to], do_all[pl.ds(at, TILE), to])
                prob[h] = p.astype(bf16)
                slope[h] = (p * dp).astype(bf16)

        def grad_step(j):
            at = where_is(j)
            for h in range(heads):
                to = slice(h * LANES, (h + 1) * LANES)
                ds = slope[h]
                acc_v[h] += dot_nn(prob[h], do_all[pl.ds(at, TILE), to])
                acc_k[h] += dot_nn(ds, q_ref[pl.ds(at, TILE), to])
                dq_all[at // TILE, h] += dot_tn(k_ref[:, to], ds)

        def step(j, carry):
            grad_step(j - 1)
            rows_step(j)
            return carry

        rows_step(first)
        lax.fori_loop(first + 1, last, step, 0)
        grad_step(last - 1)
        dk = [acc_k[h, :, 0:HEAD_DIM] for h in range(heads)]
        dv = [acc_v[h, :, 0:HEAD_DIM] for h in range(heads)]
        dk_ref[...] = jnp.concatenate(dk, axis=1).astype(bf16)
        dv_ref[...] = jnp.concatenate(dv, axis=1).astype(bf16)

        @pl.when(block == count - 1)
        def _():
            def finish(b, carry):
                at = pl.multiple_of(b * TILE, TILE)
                dq = [dq_all[b, h, 0:HEAD_DIM, :] for h in range(heads)]
                dq = jnp.concatenate(dq, axis=0).T * HEAD_DIM ** (-0.5)
                dq_ref[pl.ds(at, TILE), :] = dq.astype(bf16)
                return carry

            lax.fori_loop(0, count, finish, 0)

    row_spec = pl.BlockSpec((TILE, wide), lambda i, *_: (i, 0))
    out_spec = pl.BlockSpec((TILE, group), lambda i, *_: (i, 0))
    out = jax.ShapeDtypeStruct((rows, group), bf16)
    return pl.pallas_call(
        body,
        grid_spec=pltpu.PrefetchScalarGridSpec(
            num_scalar_prefetch=3,
            grid=(count,),
            in_specs=[WHOLE, row_spec, row_spec] + [WHOLE] * 5,
            out_specs=[WHOLE, out_spec, out_spec],
            scratch_shapes=[
                pltpu.VMEM((rows, wide), bf16),
                pltpu.VMEM((count, heads, LANES, TILE), f32),
                pltpu.VMEM((heads, TILE, LANES), f32),
                pltpu.VMEM((heads, TILE, LANES), f32),
                pltpu.VMEM((heads, TILE, TILE), bf16),
                pltpu.VMEM((heads, TILE, TILE), bf16),
            ],
        ),
        out_shape=[out] * 3,
        compiler_params=kernel_params(),
        cost_estimate=cost(24 * rows * rows * wide),
        name="attention_backward",
    )(low, high, place, queries, keys, values, contexts, *grads)


SQRT_HALF = 0.7071067811865476
PHI_SCALE = 0.3989422804014327


def norm_parts(values):
    centered = values - jnp.mean(values, axis=-1, keepdims=True)
    variance = jnp.mean(centered * centered, axis=-1, keepdims=True)
    scale = lax.rsqrt(variance + eps_norm)
    return centered * scale, scale


def tokens_forward(place, hidden, pieces, weights, up_bias, vectors):
    rows, width = hidden.shape
    half = rows // 2
    group = pieces[0].shape[1] // 2
    part = TILE
    steps = half // part
    size = 2 * part

    def body(place_ref, x_ref, c0, c1, c2, c3, w_ref, ub_ref, vec_ref, *outs):
        o_ref, ob_ref, nb_ref, act_ref, slope_ref, y1_ref, y2_ref, r1_ref, r2_ref = outs
        own = place_ref[0]
        first = x_ref[...].reshape(size, width).astype(f32) + vec_ref[0:1, :]
        for r, c_ref in enumerate((c0, c1, c2, c3)):
            ctx = jnp.concatenate([c_ref[:, 0:group], c_ref[:, group : 2 * group]], axis=0)
            first = first + dot_nt(ctx, w_ref[own ^ r, :, 2 * width : 2 * width + group])
        y1, r1 = norm_parts(first)
        y1_ref[...] = y1.reshape(2, part, width)
        r1_ref[...] = jnp.broadcast_to(r1, (size, LANES)).reshape(2, part, LANES)
        normed = y1 * vec_ref[1:2, :] + vec_ref[2:3, :]
        sent = normed.astype(bf16)
        nb_ref[...] = sent.reshape(2, part, width)
        second = normed + vec_ref[3:4, :]
        for t in range(4):
            cols = slice(t * width, (t + 1) * width)
            inner = dot_nn(sent, w_ref[t, :, 0:width]) + ub_ref[t : t + 1, :]
            cdf = 0.5 + 0.5 * lax.erf(inner * SQRT_HALF)
            act = (inner * cdf).astype(bf16)
            slope = cdf + inner * (PHI_SCALE * jnp.exp(-0.5 * inner * inner))
            act_ref[:, :, cols] = act.reshape(2, part, width)
            slope_ref[:, :, cols] = slope.astype(bf16).reshape(2, part, width)
            second = second + dot_nt(act, w_ref[t, :, width : 2 * width])
        y2, r2 = norm_parts(second)
        y2_ref[...] = y2.reshape(2, part, width)
        r2_ref[...] = jnp.broadcast_to(r2, (size, LANES)).reshape(2, part, LANES)
        result = y2 * vec_ref[4:5, :] + vec_ref[5:6, :]
        o_ref[...] = result.reshape(2, part, width)
        ob_ref[...] = result.astype(bf16).reshape(2, part, width)

    def spec(cols):
        return pl.BlockSpec((2, part, cols), lambda i, *_: (0, i, 0))

    def out(cols, kind):
        return jax.ShapeDtypeStruct((2, half, cols), kind)

    piece_spec = pl.BlockSpec((part, 2 * group), lambda i, *_: (i, 0))
    units = 4 * width
    results = pl.pallas_call(
        body,
        grid_spec=pltpu.PrefetchScalarGridSpec(
            num_scalar_prefetch=1,
            grid=(steps,),
            in_specs=[spec(width)] + [piece_spec] * 4 + [WHOLE] * 3,
            out_specs=[
                spec(width),
                spec(width),
                spec(width),
                spec(units),
                spec(units),
                spec(width),
                spec(width),
                spec(LANES),
                spec(LANES),
            ],
        ),
        out_shape=[
            out(width, f32),
            out(width, bf16),
            out(width, bf16),
            out(units, bf16),
            out(units, bf16),
            out(width, f32),
            out(width, f32),
            out(LANES, f32),
            out(LANES, f32),
        ],
        compiler_params=kernel_params(),
        cost_estimate=cost(8 * rows * width * width * 3),
        name="tokens_forward",
    )(place, hidden.reshape(2, half, width), *pieces, weights, up_bias, vectors)
    return [item.reshape(rows, item.shape[2]) for item in results]


def tokens_backward(place, grad, saved, weights, vectors, group):
    slope, y1, y2, r1, r2 = saved
    rows, width = grad.shape
    half = rows // 2
    part = TILE
    steps = half // part
    size = 2 * part
    units = 4 * width

    def norm_back(g, y, r, gain):
        e = g * gain
        mean_e = jnp.mean(e, axis=-1, keepdims=True)
        mean_ey = jnp.mean(e * y, axis=-1, keepdims=True)
        return r * (e - mean_e - y * mean_ey)

    def body(place_ref, g_ref, sl_ref, y1_ref, y2_ref, r1_ref, r2_ref, w_ref, vec_ref, *outs):
        bg_ref, gi_ref, gf_ref, ag_ref, p0, p1, p2, p3, sum_ref = outs
        own = place_ref[0]

        @pl.when(pl.program_id(0) == 0)
        def _():
            sum_ref[...] = jnp.zeros_like(sum_ref)

        def total(values):
            return jnp.sum(values, axis=0, keepdims=True)

        g = g_ref[...].reshape(size, width)
        y2 = y2_ref[...].reshape(size, width)
        r2 = r2_ref[...].reshape(size, LANES)[:, 0:1]
        second = norm_back(g, y2, r2, vec_ref[4:5, :])
        sum_ref[0:1, :] += total(g * y2)
        sum_ref[1:2, :] += total(g)
        sum_ref[2:3, :] += total(second)
        branch = second.astype(bf16)
        bg_ref[...] = branch.reshape(2, part, width)
        normed = second
        for t in range(4):
            cols = slice(t * width, (t + 1) * width)
            slope_t = sl_ref[:, :, cols].reshape(size, width).astype(f32)
            inner = (dot_nn(branch, w_ref[t, :, width : 2 * width]) * slope_t).astype(bf16)
            gi_ref[:, :, cols] = inner.reshape(2, part, width)
            sum_ref[6 + t : 7 + t, :] += total(inner.astype(f32))
            normed = normed + dot_nt(inner, w_ref[t, :, 0:width])
        y1 = y1_ref[...].reshape(size, width)
        r1 = r1_ref[...].reshape(size, LANES)[:, 0:1]
        first = norm_back(normed, y1, r1, vec_ref[1:2, :])
        sum_ref[3:4, :] += total(normed * y1)
        sum_ref[4:5, :] += total(normed)
        sum_ref[5:6, :] += total(first)
        gf_ref[...] = first.reshape(2, part, width)
        sent = first.astype(bf16)
        ag_ref[...] = sent.reshape(2, part, width)
        for r, p_ref in enumerate((p0, p1, p2, p3)):
            ctx = dot_nn(sent, w_ref[own ^ r, :, 2 * width : 2 * width + group]).astype(bf16)
            p_ref[...] = jnp.concatenate([ctx[0:part], ctx[part:size]], axis=1)

    def spec(cols):
        return pl.BlockSpec((2, part, cols), lambda i, *_: (0, i, 0))

    def out(cols, kind):
        return jax.ShapeDtypeStruct((2, half, cols), kind)

    piece_spec = pl.BlockSpec((part, 2 * group), lambda i, *_: (i, 0))
    piece = jax.ShapeDtypeStruct((half, 2 * group), bf16)
    sums = jax.ShapeDtypeStruct((16, width), f32)

    def view(values):
        return values.reshape(2, half, values.shape[1])

    results = pl.pallas_call(
        body,
        grid_spec=pltpu.PrefetchScalarGridSpec(
            num_scalar_prefetch=1,
            grid=(steps,),
            in_specs=[
                spec(width),
                spec(units),
                spec(width),
                spec(width),
                spec(LANES),
                spec(LANES),
                WHOLE,
                WHOLE,
            ],
            out_specs=[spec(width), spec(units), spec(width), spec(width)]
            + [piece_spec] * 4
            + [pl.BlockSpec((16, width), lambda i, *_: (0, 0))],
        ),
        out_shape=[out(width, bf16), out(units, bf16), out(width, f32), out(width, bf16)]
        + [piece] * 4
        + [sums],
        compiler_params=kernel_params(),
        cost_estimate=cost(8 * rows * width * width * 3),
        name="tokens_backward",
    )(place, view(grad), view(slope), view(y1), view(y2), view(r1), view(r2), weights, vectors)
    big = [item.reshape(rows, item.shape[2]) for item in results[:4]]
    return big, list(results[4:8]), results[8]


def weight_grads(place, sent, inner, branch, act, attn, pieces):
    rows, width = sent.shape
    half = rows // 2
    group = pieces[0].shape[1] // 2

    def body(place_ref, s_ref, i_ref, b_ref, a_ref, g_ref, c0, c1, c2, c3, o_ref):
        t = pl.program_id(0)
        own = place_ref[0]
        o_ref[0, :, 0:width] = dot_tn(s_ref[...], i_ref[...]).astype(bf16)
        o_ref[0, :, width : 2 * width] = dot_tn(b_ref[...], a_ref[...]).astype(bf16)
        for r, c_ref in enumerate((c0, c1, c2, c3)):

            @pl.when(t == own ^ r)
            def _(c_ref=c_ref):
                ctx = jnp.concatenate([c_ref[:, 0:group], c_ref[:, group : 2 * group]], axis=0)
                o_ref[0, :, 2 * width : 2 * width + group] = dot_tn(g_ref[...], ctx).astype(bf16)

    unit_spec = pl.BlockSpec((rows, width), lambda i, *_: (0, i))
    cols = 2 * width + group
    return pl.pallas_call(
        body,
        grid_spec=pltpu.PrefetchScalarGridSpec(
            num_scalar_prefetch=1,
            grid=(4,),
            in_specs=[WHOLE, unit_spec, WHOLE, unit_spec, WHOLE] + [WHOLE] * 4,
            out_specs=pl.BlockSpec((1, width, cols), lambda i, *_: (i, 0, 0)),
        ),
        out_shape=jax.ShapeDtypeStruct((4, width, cols), bf16),
        compiler_params=kernel_params(),
        cost_estimate=cost(8 * rows * width * width * 3),
        name="weight_grads",
    )(place, sent, inner, branch, act, attn, *pieces)


def input_grads(grad_q, grad_k, grad_v, matrix):
    rows, group = grad_q.shape
    width = matrix.shape[0]
    chunk = rows // 4

    def body(q_ref, k_ref, v_ref, mat, o0, o1, o2, o3):
        full = dot_nt(q_ref[...], mat[:, 0:group])
        full = full + dot_nt(k_ref[...], mat[:, group : 2 * group])
        full = (full + dot_nt(v_ref[...], mat[:, 2 * group : 3 * group])).astype(bf16)
        for r, o_ref in enumerate((o0, o1, o2, o3)):

            @pl.when(pl.program_id(0) == r)
            def _(o_ref=o_ref):
                o_ref[...] = full

    spec = pl.BlockSpec((chunk, group), lambda i: (i, 0))
    out = jax.ShapeDtypeStruct((chunk, width), bf16)
    return pl.pallas_call(
        body,
        grid=(4,),
        in_specs=[spec] * 3 + [WHOLE],
        out_specs=[WHOLE] * 4,
        out_shape=[out] * 4,
        compiler_params=kernel_params(),
        cost_estimate=cost(6 * rows * width * 3 * group),
        name="input_grads",
    )(grad_q, grad_k, grad_v, matrix)


def projection_grads(pieces, grad_q, grad_k, grad_v):
    chunk, width = pieces[0].shape
    group = grad_q.shape[1]

    def body(p0, p1, p2, p3, q_ref, k_ref, v_ref, o_ref, b_ref):
        for n, g_ref in enumerate((q_ref, k_ref, v_ref)):
            cols = slice(n * group, (n + 1) * group)
            acc = jnp.zeros((width, group), f32)
            for r, p_ref in enumerate((p0, p1, p2, p3)):
                acc = acc + dot_tn(p_ref[...], g_ref[r * chunk : (r + 1) * chunk, :])
            o_ref[:, cols] = acc.astype(bf16)
            b_ref[n : n + 1, :] = jnp.sum(g_ref[...].astype(f32), axis=0, keepdims=True)

    return pl.pallas_call(
        body,
        in_specs=[WHOLE] * 7,
        out_specs=[WHOLE] * 2,
        out_shape=[
            jax.ShapeDtypeStruct((width, 3 * group), bf16),
            jax.ShapeDtypeStruct((8, group), f32),
        ],
        compiler_params=kernel_params(),
        cost_estimate=cost(24 * chunk * width * 3 * group),
        name="projection_grads",
    )(*pieces, grad_q, grad_k, grad_v)


def pack_local(params):
    return jnp.concatenate([params[9], params[11].T, params[5].T], axis=1)


def gather_all(local):
    parts = lax.all_gather(local, ("tensor", "dp"), axis=0, tiled=False)
    return parts.reshape(4, -1, local.shape[1])


def layer_forward(hidden, chunks, context, params, matrix, weights, up_bias, ahead=None):
    low, high, place, query_marks, key_marks = context
    vectors = jnp.stack([params[6], params[7], params[8], params[12], params[13], params[14]])
    vectors = jnp.concatenate([vectors, jnp.zeros_like(vectors[:2])], axis=0)
    queries, keys, values = project(
        chunks, matrix, params[3], params[4], query_marks, key_marks
    )
    contexts, queries = attention_forward(low, high, place, queries, keys, values)
    contexts, ahead = tie(contexts, ahead)
    pieces = exchange_pieces([contexts[r] for r in range(4)])
    out, out_low, normed, act, slope, y1, y2, r1, r2 = tokens_forward(
        place, hidden, pieces, weights, up_bias, vectors
    )
    saved = (chunks, queries, keys, values, contexts, pieces, normed, act, slope, y1, y2, r1, r2)
    return out, out_low, saved + (vectors,), ahead


def with_bias(proj, bias, parts):
    rows, cols = proj.shape
    high = bias.astype(bf16)
    low = (bias - high.astype(f32)).astype(bf16)
    tail = jnp.concatenate([high[None], low[None], jnp.zeros((14, cols), bf16)], axis=0)
    tail = jnp.broadcast_to(tail[None], (parts,) + tail.shape)
    return jnp.concatenate([proj.reshape(parts, rows // parts, cols), tail], axis=1)


def layer_backward(grad, context, matrix, weights, saved, earlier=None):
    low, high, place = context[:3]
    chunks, queries, keys, values, contexts, pieces, normed, act, slope = saved[:9]
    y1, y2, r1, r2, vectors = saved[9:]
    width = grad.shape[1]
    parts = lax.axis_size("dp")
    (branch, inner, first, attn), sends, sums = tokens_backward(
        place, grad, (slope, y1, y2, r1, r2), weights, vectors, pieces[0].shape[1] // 2
    )
    around = narrow = None
    if earlier is not None:
        sums = jnp.concatenate([earlier[0], sums], axis=0)
        around = send_around(sums, "tensor", 1, 4)
        narrow = lax.all_to_all(earlier[1], "dp", 0, 0, tiled=True)
    grads = exchange_pieces(sends)
    packed = weight_grads(place, normed, inner, branch, act, attn, pieces)
    grads, packed, around, narrow = tie(grads, packed, around, narrow)
    if earlier is not None:
        sums = sum_over(add_up(sums, around), "dp")
    wide = lax.psum_scatter(
        packed.reshape(4 * width, -1), ("tensor", "dp"), scatter_dimension=0, tiled=True
    ).astype(f32)
    grad_q, grad_k, grad_v = attention_backward(
        low, high, place, queries, keys, values, contexts, grads
    )
    if earlier is not None:
        grad_q, grad_k, grad_v, sums = tie(grad_q, grad_k, grad_v, sums)
    partial = input_grads(grad_q, grad_k, grad_v, matrix)
    grad_in = first + scatter_chunks(partial)
    proj, proj_bias = projection_grads(chunks, grad_q, grad_k, grad_v)
    both = with_bias(proj, proj_bias[0:3].reshape(-1), parts)
    if earlier is None:
        grad_in, wide, both = tie(grad_in, wide, both)
        return grad_in, wide, (sums, both)
    both, wide = tie(both, wide)
    both = lax.all_to_all(both, "dp", 0, 0, tiled=True)
    return grad_in, wide, (sums, both, narrow)


def layer_outputs(wide, narrow, sums, place):
    narrow = jnp.sum(narrow.astype(f32), axis=0)
    width = sums.shape[1]
    group = wide.shape[1] - 2 * width
    own = narrow.shape[0] - 16
    bias = narrow[own] + narrow[own + 1]
    up_row = lax.dynamic_slice_in_dim(sums, 6 + place[0], 1, 0)[0]
    return (
        narrow[:own, 0:group],
        narrow[:own, group : 2 * group],
        narrow[:own, 2 * group : 3 * group],
        bias[0:group],
        bias[2 * group : 3 * group],
        wide[:, 2 * width : 2 * width + group].T,
        sums[5],
        sums[3],
        sums[4],
        wide[:, 0:width],
        up_row,
        wide[:, width : 2 * width].T,
        sums[2],
        sums[0],
        sums[1],
    )


def block_bounds(segments, place):
    total = segments.shape[0]
    blocks = segments.reshape(-1, TILE)
    begin = jnp.sum((segments[None] < blocks[:, :1]).astype(jnp.int32), axis=1) // TILE
    end = jnp.sum((segments[None] <= blocks[:, -1:]).astype(jnp.int32), axis=1)
    end = (end + TILE - 1) // TILE
    both = jnp.stack([begin, end]).reshape(2, 4, -1)
    both = reorder(both, place, 1).reshape(2, total // TILE)
    return both[0], both[1]


def reorder(values, place, axis):
    parts = [lax.dynamic_slice_in_dim(values, place ^ r, 1, axis) for r in range(4)]
    return jnp.concatenate(parts, axis=axis)


def on_device(tokens, segment_ids, valid_mask, teacher, *params):
    ask_params, doc_params = params[:15], params[15:]
    rows, width = tokens.shape
    place = lax.axis_index("tensor")
    segments = segment_ids[0]
    low, high = block_bounds(segments, place)
    local = reorder(segments.reshape(4, rows), place, 0).reshape(-1)
    same = local[:, None] == jnp.arange(SEGMENTS, dtype=jnp.int32)[None]
    spare = HEAD_DIM - SEGMENTS
    query_marks = jnp.pad(jnp.where(same, 0.0, -BLOCKED).astype(bf16), ((0, 0), (0, spare)))
    key_marks = jnp.concatenate(
        [same.astype(bf16), jnp.ones((4 * rows, 3), bf16), jnp.zeros((4 * rows, spare - 3), bf16)],
        axis=1,
    )
    context = (low, high, place[None], query_marks, key_marks)

    ask_matrix = lax.all_gather(
        jnp.concatenate(ask_params[0:3], axis=1), "dp", axis=0, tiled=True
    )
    doc_local = jnp.concatenate(doc_params[0:3], axis=1)
    group3 = doc_local.shape[1]
    doc_local = jnp.pad(doc_local, ((0, 0), (0, LANES)))
    ask_weights = gather_all(pack_local(ask_params))
    doc_matrix = lax.all_gather(doc_local, "dp", axis=0, tiled=True)[:, :group3]
    up_local = jnp.stack([ask_params[10], doc_params[10]])
    up_all = jnp.stack([up_local] + [flip(up_local, r) for r in range(1, 4)])
    up_all = reorder(up_all, place, 0)

    mask_rows = valid_mask.astype(f32)
    valid_total = jnp.full((8, LANES), jnp.sum(mask_rows), f32)
    valid_around = send_around(valid_total, "tensor", 1, 4)
    all_rows = rows * lax.axis_size("dp") * lax.axis_size("tensor")

    middle, middle_low, ask_saved, (doc_matrix, valid_around) = layer_forward(
        tokens,
        gather_chunks(tokens),
        context,
        ask_params,
        ask_matrix,
        ask_weights,
        up_all[:, 0],
        (doc_matrix, valid_around),
    )
    valid_total = sum_over(add_up(valid_total, valid_around), "dp")
    doc_chunks, doc_pack = tie(gather_chunks(middle_low), pack_local(doc_params))
    doc_weights = gather_all(doc_pack)
    final, final_low, doc_saved, valid_total = layer_forward(
        middle,
        doc_chunks,
        context,
        doc_params,
        doc_matrix,
        doc_weights,
        up_all[:, 1],
        valid_total,
    )
    valid_total = valid_total[0, 0]
    grad_final = mask_rows[:, None] * (final - teacher.astype(f32)) * (all_rows / valid_total)
    grad_middle, doc_wide, pending = layer_backward(
        grad_final, context, doc_matrix, doc_weights, doc_saved
    )
    grad_input, ask_wide, (sums, ask_narrow, doc_narrow) = layer_backward(
        grad_middle, context, ask_matrix, ask_weights, ask_saved, pending
    )
    half = sums.shape[0] // 2
    doc_grads = layer_outputs(doc_wide, doc_narrow, sums[:half], context[2])
    ask_grads = layer_outputs(ask_wide, ask_narrow, sums[half:], context[2])
    return (final_low, grad_input) + ask_grads + doc_grads


def layer_specs():
    return (
        P("dp", "tensor"),
        P("dp", "tensor"),
        P("dp", "tensor"),
        P("tensor"),
        P("tensor"),
        P("tensor", "dp"),
        P(),
        P(),
        P(),
        P("dp", "tensor"),
        P("tensor"),
        P("tensor", "dp"),
        P(),
        P(),
        P(),
    )


def solution(mesh):
    rows = P(("dp", "tensor"), None)
    return jax.shard_map(
        on_device,
        mesh=mesh,
        in_specs=(rows, P("dp", None), P(("dp", "tensor")), rows) + layer_specs() * 2,
        out_specs=(rows, rows) + layer_specs() * 2,
        check_vma=False,
    )
```

```python
import jax
import jax.numpy as jnp
from jax import lax
from jax.experimental import pallas as pl
from jax.experimental.pallas import tpu as pltpu
from jax.sharding import PartitionSpec as P

HEAD_DIM = 64
LANES = 128
TILE = 256
BLOCKED = 1e9
SEGMENTS = 16
eps_norm = 1e-12

bf16 = jnp.bfloat16
f32 = jnp.float32
NT = (((1,), (1,)), ((), ()))
TN = (((0,), (0,)), ((), ()))
WHOLE = pl.BlockSpec(memory_space=pltpu.VMEM)


def dot_nn(first_mat, second_mat):
    return jnp.dot(first_mat, second_mat, preferred_element_type=f32)


def dot_nt(first_mat, second_mat):
    return lax.dot_general(first_mat, second_mat, NT, preferred_element_type=f32)


def dot_tn(first_mat, second_mat):
    return lax.dot_general(first_mat, second_mat, TN, preferred_element_type=f32)


def cost(flops):
    return pl.CostEstimate(flops=int(flops), bytes_accessed=0, transcendentals=0)


def kernel_params():
    return pltpu.CompilerParams(vmem_limit_bytes=60 * 1024 * 1024)


def flip(values, bit):
    size = lax.axis_size("tensor")
    return lax.ppermute(values, "tensor", [(i, i ^ bit) for i in range(size)])


def gather_chunks(own):
    half = own.shape[0] // 2
    near = flip(own, 1)
    far = [flip(own[:half], 2), flip(own[half:], 2)]
    last = [flip(part, 1) for part in far]
    return own, near, jnp.concatenate(far, axis=0), jnp.concatenate(last, axis=0)


def exchange_pieces(pieces):
    return [pieces[0]] + [flip(pieces[r], r) for r in range(1, 4)]


def tie(*items):
    return lax.optimization_barrier(items)


def send_around(values, axis, step, count):
    size = lax.axis_size(axis)
    return [
        lax.ppermute(values, axis, [(i, i ^ (step * r)) for i in range(size)])
        for r in range(1, count)
    ]


def add_up(values, others):
    for other in others:
        values = values + other
    return values


def sum_over(values, axis):
    size = lax.axis_size(axis)
    step = 1
    while step < size:
        count = min(8, size // step)
        values = add_up(values, send_around(values, axis, step, count))
        step *= count
    return values


def project(pieces, matrix, query_bias, value_bias, query_marks, key_marks):
    rows, width = pieces[0].shape
    heads = matrix.shape[1] // 3 // HEAD_DIM
    group = heads * HEAD_DIM
    wide = heads * LANES
    sub = rows // 2

    def body(p0, p1, p2, p3, mat, bias_q, bias_v, mark_q, mark_k, out_q, out_k, out_v):
        chunk = pl.program_id(0)
        lane = lax.broadcasted_iota(jnp.int32, (sub, HEAD_DIM), 1)
        ones = jnp.where(lane < 2, 1.0, 0.0).astype(bf16)

        def run(piece):
            for part in range(2):
                at = slice(part * sub, (part + 1) * sub)
                full = dot_nn(piece[at, :], mat[...])
                for h in range(heads):
                    lo = h * HEAD_DIM
                    to = slice(h * LANES, (h + 1) * LANES)
                    q = full[:, lo : lo + HEAD_DIM] + bias_q[:, lo : lo + HEAD_DIM]
                    q = (q.astype(bf16).astype(f32) * HEAD_DIM ** (-0.5)).astype(bf16)
                    k = full[:, group + lo : group + lo + HEAD_DIM].astype(bf16)
                    v = full[:, 2 * group + lo : 2 * group + lo + HEAD_DIM]
                    v = (v + bias_v[:, lo : lo + HEAD_DIM]).astype(bf16)
                    out_q[at, to] = jnp.concatenate([q, mark_q[at, :]], axis=1)
                    out_k[at, to] = jnp.concatenate([k, mark_k[at, :]], axis=1)
                    out_v[at, to] = jnp.concatenate([v, ones], axis=1)

        for r, piece in enumerate((p0, p1, p2, p3)):

            @pl.when(chunk == r)
            def _(piece=piece):
                run(piece)

    out = jax.ShapeDtypeStruct((4 * rows, wide), bf16)
    spec = pl.BlockSpec((rows, wide), lambda i: (i, 0))
    mark_spec = pl.BlockSpec((rows, HEAD_DIM), lambda i: (i, 0))
    return pl.pallas_call(
        body,
        grid=(4,),
        in_specs=[WHOLE] * 7 + [mark_spec] * 2,
        out_specs=[spec] * 3,
        out_shape=[out] * 3,
        compiler_params=kernel_params(),
        cost_estimate=cost(6 * rows * 4 * pieces[0].shape[1] * matrix.shape[1]),
        name="project",
    )(*pieces, matrix, query_bias[None], value_bias[None], query_marks, key_marks)


def attention_forward(low, high, place, queries, keys, values, base):
    rows, wide = queries.shape
    heads = wide // LANES
    count = rows // TILE
    per_chunk = count // 4
    half = rows // 8
    half_blocks = half // TILE
    group = heads * HEAD_DIM
    skip = base * per_chunk

    def body(low_ref, high_ref, place_ref, q_ref, k_ref, v_ref, ctx_ref, ql_ref, *scratch):
        peak, fade, total, score = scratch
        block = pl.program_id(0) + skip
        own = place_ref[0]
        first = low_ref[block]
        last = high_ref[block]
        peak[...] = jnp.full_like(peak, -3e38)
        total[...] = jnp.zeros_like(total)

        def where_is(j):
            spot = ((j // per_chunk) ^ own) * per_chunk + j % per_chunk
            return pl.multiple_of(spot * TILE, TILE)

        def rows_step(j):
            at = where_is(j)
            for h in range(heads):
                to = slice(h * LANES, (h + 1) * LANES)
                s = dot_nt(k_ref[pl.ds(at, TILE), to], q_ref[:, to])
                old = peak[h, 0:1, :]
                top = jnp.maximum(old, jnp.max(s, axis=0, keepdims=True))
                peak[h, 0:1, :] = top
                fade[h, 0:1, :] = jnp.exp(old - top)
                score[h] = s

        def sum_step(j):
            at = where_is(j)
            for h in range(heads):
                v = v_ref[pl.ds(at, TILE), h * LANES : (h + 1) * LANES]
                p = jnp.exp(score[h] - peak[h, 0:1, :]).astype(bf16)
                total[h] = total[h] * fade[h, 0:1, :] + dot_tn(v, p)

        def step(j, carry):
            sum_step(j - 1)
            rows_step(j)
            return carry

        rows_step(first)
        lax.fori_loop(first + 1, last, step, 0)
        sum_step(last - 1)
        feature = lax.broadcasted_iota(jnp.int32, (LANES, TILE), 0)
        lane = lax.broadcasted_iota(jnp.int32, (TILE, LANES), 1)
        mark = HEAD_DIM + SEGMENTS
        outs = []
        for h in range(heads):
            acc = total[h]
            norm = acc[HEAD_DIM : HEAD_DIM + 1, :]
            shift = -(peak[h, 0:1, :] + jnp.log(norm))
            one = shift.astype(bf16).astype(f32)
            two = (shift - one).astype(bf16).astype(f32)
            three = shift - one - two
            both = acc * (1.0 / norm)
            both = jnp.where(feature == mark, one, both)
            both = jnp.where(feature == mark + 1, two, both)
            both = jnp.where(feature == mark + 2, three, both)
            both = both.T.astype(bf16)
            outs.append(both[:, 0:HEAD_DIM])
            to = slice(h * LANES, (h + 1) * LANES)
            inside = (lane >= mark) & (lane < mark + 3)
            ql_ref[:, to] = jnp.where(inside, both, q_ref[:, to])
        ctx = jnp.concatenate(outs, axis=1)
        inside = block % per_chunk
        at = pl.multiple_of((inside % half_blocks) * TILE, TILE)

        @pl.when(inside < half_blocks)
        def _():
            ctx_ref[0, pl.ds(at, TILE), 0:group] = ctx

        @pl.when(inside >= half_blocks)
        def _():
            ctx_ref[0, pl.ds(at, TILE), group : 2 * group] = ctx

    row_spec = pl.BlockSpec((TILE, wide), lambda i, *_: (i + skip, 0))
    return pl.pallas_call(
        body,
        grid_spec=pltpu.PrefetchScalarGridSpec(
            num_scalar_prefetch=3,
            grid=(count // 2,),
            in_specs=[row_spec, WHOLE, WHOLE],
            out_specs=[
                pl.BlockSpec((1, half, 2 * group), lambda i, *_: (i // per_chunk, 0, 0)),
                row_spec,
            ],
            scratch_shapes=[
                pltpu.VMEM((heads, 8, TILE), f32),
                pltpu.VMEM((heads, 8, TILE), f32),
                pltpu.VMEM((heads, LANES, TILE), f32),
                pltpu.VMEM((heads, TILE, TILE), f32),
            ],
        ),
        out_shape=[
            jax.ShapeDtypeStruct((2, half, 2 * group), bf16),
            jax.ShapeDtypeStruct((rows, wide), bf16),
        ],
        compiler_params=kernel_params(),
        input_output_aliases={3: 1},
        cost_estimate=cost(4 * rows * rows * wide),
        name="attention_forward",
    )(low, high, place, queries, keys, values)


def attention_backward(low, high, place, queries, keys, values, contexts, grads):
    rows, wide = queries.shape
    heads = wide // LANES
    count = rows // TILE
    per_chunk = count // 4
    half = rows // 8
    half_blocks = half // TILE
    group = heads * HEAD_DIM

    def body(low_ref, high_ref, place_ref, q_ref, k_ref, v_ref, near, far, g0, g1, g2, g3, *rest):
        dq_ref, dk_ref, dv_ref, do_all, dq_all, acc_k, acc_v, prob, slope = rest
        block = pl.program_id(0)
        own = place_ref[0]
        first = low_ref[block]
        last = high_ref[block]

        @pl.when(block == 0)
        def _():
            dq_all[...] = jnp.zeros_like(dq_all)
            lane = lax.broadcasted_iota(jnp.int32, (TILE, HEAD_DIM), 1)
            for chunk, g_ref in enumerate((g0, g1, g2, g3)):
                c_ref = (near, far)[chunk // 2]

                def prepare(b, carry, chunk=chunk, g_ref=g_ref, c_ref=c_ref):
                    at = pl.multiple_of(b * TILE, TILE)
                    for side in range(2):
                        cols = slice(side * group, (side + 1) * group)
                        row = pl.multiple_of((2 * chunk + side) * half + at, TILE)
                        c = c_ref[chunk % 2, pl.ds(at, TILE), cols].astype(f32)
                        g = g_ref[pl.ds(at, TILE), cols].astype(f32)
                        for h in range(heads):
                            lo = h * HEAD_DIM
                            gh = g[:, lo : lo + HEAD_DIM]
                            ch = c[:, lo : lo + HEAD_DIM]
                            delta = -jnp.sum(gh * ch, axis=1, keepdims=True)
                            one = delta.astype(bf16).astype(f32)
                            two = delta - one
                            tail = jnp.where(lane == 0, one, jnp.where(lane == 1, two, 0.0))
                            both = jnp.concatenate([gh, tail], axis=1).astype(bf16)
                            do_all[pl.ds(row, TILE), h * LANES : (h + 1) * LANES] = both
                    return carry

                lax.fori_loop(0, half_blocks, prepare, 0)

        acc_k[...] = jnp.zeros_like(acc_k)
        acc_v[...] = jnp.zeros_like(acc_v)

        def where_is(j):
            spot = ((j // per_chunk) ^ own) * per_chunk + j % per_chunk
            return pl.multiple_of(spot * TILE, TILE)

        def rows_step(j):
            at = where_is(j)
            for h in range(heads):
                to = slice(h * LANES, (h + 1) * LANES)
                p = jnp.exp(dot_nt(k_ref[:, to], q_ref[pl.ds(at, TILE), to]))
                dp = dot_nt(v_ref[:, to], do_all[pl.ds(at, TILE), to])
                prob[h] = p.astype(bf16)
                slope[h] = (p * dp).astype(bf16)

        def grad_step(j):
            at = where_is(j)
            for h in range(heads):
                to = slice(h * LANES, (h + 1) * LANES)
                ds = slope[h]
                acc_v[h] += dot_nn(prob[h], do_all[pl.ds(at, TILE), to])
                acc_k[h] += dot_nn(ds, q_ref[pl.ds(at, TILE), to])
                dq_all[at // TILE, h] += dot_tn(k_ref[:, to], ds)

        def step(j, carry):
            grad_step(j - 1)
            rows_step(j)
            return carry

        rows_step(first)
        lax.fori_loop(first + 1, last, step, 0)
        grad_step(last - 1)
        dk = [acc_k[h, :, 0:HEAD_DIM] for h in range(heads)]
        dv = [acc_v[h, :, 0:HEAD_DIM] for h in range(heads)]
        dk_ref[...] = jnp.concatenate(dk, axis=1).astype(bf16)
        dv_ref[...] = jnp.concatenate(dv, axis=1).astype(bf16)

        @pl.when(block == count - 1)
        def _():
            def finish(b, carry):
                at = pl.multiple_of(b * TILE, TILE)
                dq = [dq_all[b, h, 0:HEAD_DIM, :] for h in range(heads)]
                dq = jnp.concatenate(dq, axis=0).T * HEAD_DIM ** (-0.5)
                dq_ref[pl.ds(at, TILE), :] = dq.astype(bf16)
                return carry

            lax.fori_loop(0, count, finish, 0)

    row_spec = pl.BlockSpec((TILE, wide), lambda i, *_: (i, 0))
    out_spec = pl.BlockSpec((TILE, group), lambda i, *_: (i, 0))
    out = jax.ShapeDtypeStruct((rows, group), bf16)
    return pl.pallas_call(
        body,
        grid_spec=pltpu.PrefetchScalarGridSpec(
            num_scalar_prefetch=3,
            grid=(count,),
            in_specs=[WHOLE, row_spec, row_spec] + [WHOLE] * 6,
            out_specs=[WHOLE, out_spec, out_spec],
            scratch_shapes=[
                pltpu.VMEM((rows, wide), bf16),
                pltpu.VMEM((count, heads, LANES, TILE), f32),
                pltpu.VMEM((heads, TILE, LANES), f32),
                pltpu.VMEM((heads, TILE, LANES), f32),
                pltpu.VMEM((heads, TILE, TILE), bf16),
                pltpu.VMEM((heads, TILE, TILE), bf16),
            ],
        ),
        out_shape=[out] * 3,
        compiler_params=kernel_params(),
        cost_estimate=cost(24 * rows * rows * wide),
        name="attention_backward",
    )(low, high, place, queries, keys, values, *contexts, *grads)


SQRT_HALF = 0.7071067811865476
PHI_SCALE = 0.3989422804014327


def norm_parts(values):
    centered = values - jnp.mean(values, axis=-1, keepdims=True)
    variance = jnp.mean(centered * centered, axis=-1, keepdims=True)
    scale = lax.rsqrt(variance + eps_norm)
    return centered * scale, scale


def tokens_forward(place, hidden, pieces, weights, up_bias, vectors):
    rows, width = hidden.shape
    half = rows // 2
    group = pieces[0].shape[1] // 2
    part = TILE
    steps = half // part
    size = 2 * part

    def body(place_ref, x_ref, c0, c1, c2, c3, w_ref, ub_ref, vec_ref, *outs):
        o_ref, ob_ref, nb_ref, act_ref, slope_ref, y1_ref, y2_ref, r1_ref, r2_ref = outs
        own = place_ref[0]
        first = x_ref[...].reshape(size, width).astype(f32) + vec_ref[0:1, :]
        for r, c_ref in enumerate((c0, c1, c2, c3)):
            ctx = jnp.concatenate([c_ref[:, 0:group], c_ref[:, group : 2 * group]], axis=0)
            first = first + dot_nt(ctx, w_ref[own ^ r, :, 2 * width : 2 * width + group])
        y1, r1 = norm_parts(first)
        y1_ref[...] = y1.reshape(2, part, width)
        r1_ref[...] = jnp.broadcast_to(r1, (size, LANES)).reshape(2, part, LANES)
        normed = y1 * vec_ref[1:2, :] + vec_ref[2:3, :]
        sent = normed.astype(bf16)
        nb_ref[...] = sent.reshape(2, part, width)
        second = normed + vec_ref[3:4, :]
        for t in range(4):
            cols = slice(t * width, (t + 1) * width)
            inner = dot_nn(sent, w_ref[t, :, 0:width]) + ub_ref[t : t + 1, :]
            cdf = 0.5 + 0.5 * lax.erf(inner * SQRT_HALF)
            act = (inner * cdf).astype(bf16)
            slope = cdf + inner * (PHI_SCALE * jnp.exp(-0.5 * inner * inner))
            act_ref[:, :, cols] = act.reshape(2, part, width)
            slope_ref[:, :, cols] = slope.astype(bf16).reshape(2, part, width)
            second = second + dot_nt(act, w_ref[t, :, width : 2 * width])
        y2, r2 = norm_parts(second)
        y2_ref[...] = y2.reshape(2, part, width)
        r2_ref[...] = jnp.broadcast_to(r2, (size, LANES)).reshape(2, part, LANES)
        result = y2 * vec_ref[4:5, :] + vec_ref[5:6, :]
        o_ref[...] = result.reshape(2, part, width)
        ob_ref[...] = result.astype(bf16).reshape(2, part, width)

    def spec(cols):
        return pl.BlockSpec((2, part, cols), lambda i, *_: (0, i, 0))

    def out(cols, kind):
        return jax.ShapeDtypeStruct((2, half, cols), kind)

    piece_spec = pl.BlockSpec((part, 2 * group), lambda i, *_: (i, 0))
    units = 4 * width
    results = pl.pallas_call(
        body,
        grid_spec=pltpu.PrefetchScalarGridSpec(
            num_scalar_prefetch=1,
            grid=(steps,),
            in_specs=[spec(width)] + [piece_spec] * 4 + [WHOLE] * 3,
            out_specs=[
                spec(width),
                spec(width),
                spec(width),
                spec(units),
                spec(units),
                spec(width),
                spec(width),
                spec(LANES),
                spec(LANES),
            ],
        ),
        out_shape=[
            out(width, f32),
            out(width, bf16),
            out(width, bf16),
            out(units, bf16),
            out(units, bf16),
            out(width, f32),
            out(width, f32),
            out(LANES, f32),
            out(LANES, f32),
        ],
        compiler_params=kernel_params(),
        cost_estimate=cost(8 * rows * width * width * 3),
        name="tokens_forward",
    )(place, hidden.reshape(2, half, width), *pieces, weights, up_bias, vectors)
    return [item.reshape(rows, item.shape[2]) for item in results]


def tokens_backward(place, grad, saved, weights, vectors, group):
    slope, y1, y2, r1, r2 = saved
    rows, width = grad.shape
    half = rows // 2
    part = TILE
    steps = half // part
    size = 2 * part
    units = 4 * width

    def norm_back(g, y, r, gain):
        e = g * gain
        mean_e = jnp.mean(e, axis=-1, keepdims=True)
        mean_ey = jnp.mean(e * y, axis=-1, keepdims=True)
        return r * (e - mean_e - y * mean_ey)

    def body(place_ref, g_ref, sl_ref, y1_ref, y2_ref, r1_ref, r2_ref, w_ref, vec_ref, *outs):
        bg_ref, gi_ref, gf_ref, ag_ref, p0, p1, p2, p3, sum_ref = outs
        own = place_ref[0]

        @pl.when(pl.program_id(0) == 0)
        def _():
            sum_ref[...] = jnp.zeros_like(sum_ref)

        def total(values):
            return jnp.sum(values, axis=0, keepdims=True)

        g = g_ref[...].reshape(size, width)
        y2 = y2_ref[...].reshape(size, width)
        r2 = r2_ref[...].reshape(size, LANES)[:, 0:1]
        second = norm_back(g, y2, r2, vec_ref[4:5, :])
        sum_ref[0:1, :] += total(g * y2)
        sum_ref[1:2, :] += total(g)
        sum_ref[2:3, :] += total(second)
        branch = second.astype(bf16)
        bg_ref[...] = branch.reshape(2, part, width)
        normed = second
        for t in range(4):
            cols = slice(t * width, (t + 1) * width)
            slope_t = sl_ref[:, :, cols].reshape(size, width).astype(f32)
            inner = (dot_nn(branch, w_ref[t, :, width : 2 * width]) * slope_t).astype(bf16)
            gi_ref[:, :, cols] = inner.reshape(2, part, width)
            sum_ref[6 + t : 7 + t, :] += total(inner.astype(f32))
            normed = normed + dot_nt(inner, w_ref[t, :, 0:width])
        y1 = y1_ref[...].reshape(size, width)
        r1 = r1_ref[...].reshape(size, LANES)[:, 0:1]
        first = norm_back(normed, y1, r1, vec_ref[1:2, :])
        sum_ref[3:4, :] += total(normed * y1)
        sum_ref[4:5, :] += total(normed)
        sum_ref[5:6, :] += total(first)
        gf_ref[...] = first.reshape(2, part, width)
        sent = first.astype(bf16)
        ag_ref[...] = sent.reshape(2, part, width)
        for r, p_ref in enumerate((p0, p1, p2, p3)):
            ctx = dot_nn(sent, w_ref[own ^ r, :, 2 * width : 2 * width + group]).astype(bf16)
            p_ref[...] = jnp.concatenate([ctx[0:part], ctx[part:size]], axis=1)

    def spec(cols):
        return pl.BlockSpec((2, part, cols), lambda i, *_: (0, i, 0))

    def out(cols, kind):
        return jax.ShapeDtypeStruct((2, half, cols), kind)

    piece_spec = pl.BlockSpec((part, 2 * group), lambda i, *_: (i, 0))
    piece = jax.ShapeDtypeStruct((half, 2 * group), bf16)
    sums = jax.ShapeDtypeStruct((16, width), f32)

    def view(values):
        return values.reshape(2, half, values.shape[1])

    results = pl.pallas_call(
        body,
        grid_spec=pltpu.PrefetchScalarGridSpec(
            num_scalar_prefetch=1,
            grid=(steps,),
            in_specs=[
                spec(width),
                spec(units),
                spec(width),
                spec(width),
                spec(LANES),
                spec(LANES),
                WHOLE,
                WHOLE,
            ],
            out_specs=[spec(width), spec(units), spec(width), spec(width)]
            + [piece_spec] * 4
            + [pl.BlockSpec((16, width), lambda i, *_: (0, 0))],
        ),
        out_shape=[out(width, bf16), out(units, bf16), out(width, f32), out(width, bf16)]
        + [piece] * 4
        + [sums],
        compiler_params=kernel_params(),
        cost_estimate=cost(8 * rows * width * width * 3),
        name="tokens_backward",
    )(place, view(grad), view(slope), view(y1), view(y2), view(r1), view(r2), weights, vectors)
    big = [item.reshape(rows, item.shape[2]) for item in results[:4]]
    return big, list(results[4:8]), results[8]


def weight_grads(place, sent, inner, branch, act, attn, pieces):
    rows, width = sent.shape
    half = rows // 2
    group = pieces[0].shape[1] // 2

    def body(place_ref, s_ref, i_ref, b_ref, a_ref, g_ref, c0, c1, c2, c3, o_ref):
        t = pl.program_id(0)
        own = place_ref[0]
        o_ref[0, :, 0:width] = dot_tn(s_ref[...], i_ref[...]).astype(bf16)
        o_ref[0, :, width : 2 * width] = dot_tn(b_ref[...], a_ref[...]).astype(bf16)
        for r, c_ref in enumerate((c0, c1, c2, c3)):

            @pl.when(t == own ^ r)
            def _(c_ref=c_ref):
                ctx = jnp.concatenate([c_ref[:, 0:group], c_ref[:, group : 2 * group]], axis=0)
                o_ref[0, :, 2 * width : 2 * width + group] = dot_tn(g_ref[...], ctx).astype(bf16)

    unit_spec = pl.BlockSpec((rows, width), lambda i, *_: (0, i))
    cols = 2 * width + group
    return pl.pallas_call(
        body,
        grid_spec=pltpu.PrefetchScalarGridSpec(
            num_scalar_prefetch=1,
            grid=(4,),
            in_specs=[WHOLE, unit_spec, WHOLE, unit_spec, WHOLE] + [WHOLE] * 4,
            out_specs=pl.BlockSpec((1, width, cols), lambda i, *_: (i, 0, 0)),
        ),
        out_shape=jax.ShapeDtypeStruct((4, width, cols), bf16),
        compiler_params=kernel_params(),
        cost_estimate=cost(8 * rows * width * width * 3),
        name="weight_grads",
    )(place, sent, inner, branch, act, attn, *pieces)


def input_grads(grad_q, grad_k, grad_v, matrix, base, number):
    rows, group = grad_q.shape
    width = matrix.shape[0]
    chunk = rows // 4

    def body(q_ref, k_ref, v_ref, mat, *outs):
        full = dot_nt(q_ref[...], mat[:, 0:group])
        full = full + dot_nt(k_ref[...], mat[:, group : 2 * group])
        full = (full + dot_nt(v_ref[...], mat[:, 2 * group : 3 * group])).astype(bf16)
        for r, o_ref in enumerate(outs):

            @pl.when(pl.program_id(0) == number - 1 - r)
            def _(o_ref=o_ref):
                o_ref[...] = full

    spec = pl.BlockSpec((chunk, group), lambda i: (base + number - 1 - i, 0))
    out = jax.ShapeDtypeStruct((chunk, width), bf16)
    return pl.pallas_call(
        body,
        grid=(number,),
        in_specs=[spec] * 3 + [WHOLE],
        out_specs=[WHOLE] * number,
        out_shape=[out] * number,
        compiler_params=kernel_params(),
        cost_estimate=cost(6 * number * chunk * width * 3 * group),
        name="input_grads",
    )(grad_q, grad_k, grad_v, matrix)


def projection_grads(pieces, grad_q, grad_k, grad_v):
    chunk, width = pieces[0].shape
    group = grad_q.shape[1]

    def body(p0, p1, p2, p3, q_ref, k_ref, v_ref, o_ref, b_ref):
        for n, g_ref in enumerate((q_ref, k_ref, v_ref)):
            cols = slice(n * group, (n + 1) * group)
            acc = jnp.zeros((width, group), f32)
            for r, p_ref in enumerate((p0, p1, p2, p3)):
                acc = acc + dot_tn(p_ref[...], g_ref[r * chunk : (r + 1) * chunk, :])
            o_ref[:, cols] = acc.astype(bf16)
            b_ref[n : n + 1, :] = jnp.sum(g_ref[...].astype(f32), axis=0, keepdims=True)

    return pl.pallas_call(
        body,
        in_specs=[WHOLE] * 7,
        out_specs=[WHOLE] * 2,
        out_shape=[
            jax.ShapeDtypeStruct((width, 3 * group), bf16),
            jax.ShapeDtypeStruct((8, group), f32),
        ],
        compiler_params=kernel_params(),
        cost_estimate=cost(24 * chunk * width * 3 * group),
        name="projection_grads",
    )(*pieces, grad_q, grad_k, grad_v)


def pack_local(params):
    return jnp.concatenate([params[9], params[11].T, params[5].T], axis=1)


def gather_all(local):
    parts = lax.all_gather(local, ("tensor", "dp"), axis=0, tiled=False)
    return parts, parts.reshape(4, -1, local.shape[1])


def with_count(local, count):
    high = count // LANES
    digits = jnp.stack([high, count - high * LANES]).astype(bf16)
    digits = jnp.concatenate([digits, jnp.zeros((HEAD_DIM - 2,), bf16)])
    spare = jnp.broadcast_to(digits[None], (local.shape[0], HEAD_DIM))
    return jnp.concatenate([local, spare], axis=1)


def count_of(parts, column):
    digits = parts[:, 0, column : column + 2].astype(f32)
    return jnp.sum(digits[:, 0]) * LANES + jnp.sum(digits[:, 1])


def layer_forward(hidden, chunks, context, params, matrix, weights, up_bias, ahead=None):
    low, high, place, query_marks, key_marks = context
    vectors = jnp.stack([params[6], params[7], params[8], params[12], params[13], params[14]])
    vectors = jnp.concatenate([vectors, jnp.zeros_like(vectors[:2])], axis=0)
    queries, keys, values = project(
        chunks, matrix, params[3], params[4], query_marks, key_marks
    )
    far, queries = attention_forward(low, high, place, queries, keys, values, 2)
    sent = [flip(far[r], 2 + r) for r in range(2)]
    near, queries = attention_forward(low, high, place, queries, keys, values, 0)
    near, sent, ahead = tie(near, sent, ahead)
    pieces = [near[0], flip(near[1], 1)] + sent
    contexts = (near, far)
    out, out_low, normed, act, slope, y1, y2, r1, r2 = tokens_forward(
        place, hidden, pieces, weights, up_bias, vectors
    )
    saved = (chunks, queries, keys, values, contexts, pieces, normed, act, slope, y1, y2, r1, r2)
    return out, out_low, saved + (vectors,), ahead


def with_bias(proj, bias, parts):
    rows, cols = proj.shape
    high = bias.astype(bf16)
    low = (bias - high.astype(f32)).astype(bf16)
    tail = jnp.concatenate([high[None], low[None], jnp.zeros((14, cols), bf16)], axis=0)
    tail = jnp.broadcast_to(tail[None], (parts,) + tail.shape)
    return jnp.concatenate([proj.reshape(parts, rows // parts, cols), tail], axis=1)


def layer_backward(grad, context, matrix, weights, saved, earlier=None):
    low, high, place = context[:3]
    chunks, queries, keys, values, contexts, pieces, normed, act, slope = saved[:9]
    y1, y2, r1, r2, vectors = saved[9:]
    width = grad.shape[1]
    parts = lax.axis_size("dp")
    (branch, inner, first, attn), sends, sums = tokens_backward(
        place, grad, (slope, y1, y2, r1, r2), weights, vectors, pieces[0].shape[1] // 2
    )
    around = narrow = None
    if earlier is not None:
        sums = jnp.concatenate([earlier[0], sums], axis=0)
        around = send_around(sums, "tensor", 1, 4)
        narrow = lax.all_to_all(earlier[1], "dp", 0, 0, tiled=True)
    grads = exchange_pieces(sends)
    packed = weight_grads(place, normed, inner, branch, act, attn, pieces)
    grads, packed, around, narrow = tie(grads, packed, around, narrow)
    if earlier is not None:
        sums = add_up(sums, around)
    wide = lax.psum_scatter(
        packed.reshape(4 * width, -1), ("tensor", "dp"), scatter_dimension=0, tiled=True
    ).astype(f32)
    grad_q, grad_k, grad_v = attention_backward(
        low, high, place, queries, keys, values, contexts, grads
    )
    if earlier is not None:
        grad_q, grad_k, grad_v, sums = tie(grad_q, grad_k, grad_v, sums)
    (beyond,) = input_grads(grad_q, grad_k, grad_v, matrix, 3, 1)
    (across,) = input_grads(grad_q, grad_k, grad_v, matrix, 2, 1)
    crossing = (across.astype(f32) + flip(beyond, 1).astype(f32)).astype(bf16)
    crossing, grad_q, grad_k, grad_v = tie(crossing, grad_q, grad_k, grad_v)
    crossing = flip(crossing, 2)
    here, beside = input_grads(grad_q, grad_k, grad_v, matrix, 0, 2)
    grad_in = here.astype(f32) + flip(beside, 1).astype(f32) + crossing.astype(f32)
    grad_in = first + grad_in
    proj, proj_bias = projection_grads(chunks, grad_q, grad_k, grad_v)
    both = with_bias(proj, proj_bias[0:3].reshape(-1), parts)
    if earlier is None:
        grad_in, wide, both = tie(grad_in, wide, both)
        return grad_in, wide, (sums, both)
    both = lax.all_to_all(both, "dp", 0, 0, tiled=True)
    both, grad_in, wide, sums = tie(both, grad_in, wide, sum_over(sums, "dp"))
    return grad_in, wide, (sums, both, narrow)


def layer_outputs(wide, narrow, sums, place):
    narrow = jnp.sum(narrow.astype(f32), axis=0)
    width = sums.shape[1]
    group = wide.shape[1] - 2 * width
    own = narrow.shape[0] - 16
    bias = narrow[own] + narrow[own + 1]
    up_row = lax.dynamic_slice_in_dim(sums, 6 + place[0], 1, 0)[0]
    return (
        narrow[:own, 0:group],
        narrow[:own, group : 2 * group],
        narrow[:own, 2 * group : 3 * group],
        bias[0:group],
        bias[2 * group : 3 * group],
        wide[:, 2 * width : 2 * width + group].T,
        sums[5],
        sums[3],
        sums[4],
        wide[:, 0:width],
        up_row,
        wide[:, width : 2 * width].T,
        sums[2],
        sums[0],
        sums[1],
    )


def block_bounds(segments, place):
    total = segments.shape[0]
    blocks = segments.reshape(-1, TILE)
    begin = jnp.sum((segments[None] < blocks[:, :1]).astype(jnp.int32), axis=1) // TILE
    end = jnp.sum((segments[None] <= blocks[:, -1:]).astype(jnp.int32), axis=1)
    end = (end + TILE - 1) // TILE
    both = jnp.stack([begin, end]).reshape(2, 4, -1)
    both = reorder(both, place, 1).reshape(2, total // TILE)
    return both[0], both[1]


def reorder(values, place, axis):
    parts = [lax.dynamic_slice_in_dim(values, place ^ r, 1, axis) for r in range(4)]
    return jnp.concatenate(parts, axis=axis)


def on_device(tokens, segment_ids, valid_mask, teacher, *params):
    ask_params, doc_params = params[:15], params[15:]
    rows, width = tokens.shape
    place = lax.axis_index("tensor")
    segments = segment_ids[0]
    low, high = block_bounds(segments, place)
    local = reorder(segments.reshape(4, rows), place, 0).reshape(-1)
    same = local[:, None] == jnp.arange(SEGMENTS, dtype=jnp.int32)[None]
    spare = HEAD_DIM - SEGMENTS
    query_marks = jnp.pad(jnp.where(same, 0.0, -BLOCKED).astype(bf16), ((0, 0), (0, spare)))
    key_marks = jnp.concatenate(
        [same.astype(bf16), jnp.ones((4 * rows, 3), bf16), jnp.zeros((4 * rows, spare - 3), bf16)],
        axis=1,
    )
    context = (low, high, place[None], query_marks, key_marks)

    ask_matrix = lax.all_gather(
        jnp.concatenate(ask_params[0:3], axis=1), "dp", axis=0, tiled=True
    )
    doc_local = jnp.concatenate(doc_params[0:3], axis=1)
    group3 = doc_local.shape[1]
    doc_local = jnp.pad(doc_local, ((0, 0), (0, LANES)))
    _, ask_weights = gather_all(pack_local(ask_params))
    doc_matrix = lax.all_gather(doc_local, "dp", axis=0, tiled=True)[:, :group3]
    up_local = jnp.stack([ask_params[10], doc_params[10]])
    up_all = jnp.stack([up_local] + [flip(up_local, r) for r in range(1, 4)])
    up_all = reorder(up_all, place, 0)

    mask_rows = valid_mask.astype(f32)
    doc_pack = pack_local(doc_params)
    column = doc_pack.shape[1]
    doc_pack = with_count(doc_pack, jnp.sum(valid_mask))
    all_rows = rows * lax.axis_size("dp") * lax.axis_size("tensor")

    middle, middle_low, ask_saved, doc_matrix = layer_forward(
        tokens,
        gather_chunks(tokens),
        context,
        ask_params,
        ask_matrix,
        ask_weights,
        up_all[:, 0],
        doc_matrix,
    )
    doc_chunks, doc_pack = tie(gather_chunks(middle_low), doc_pack)
    doc_parts, doc_weights = gather_all(doc_pack)
    final, final_low, doc_saved, _ = layer_forward(
        middle,
        doc_chunks,
        context,
        doc_params,
        doc_matrix,
        doc_weights,
        up_all[:, 1],
    )
    valid_total = count_of(doc_parts, column)
    grad_final = mask_rows[:, None] * (final - teacher.astype(f32)) * (all_rows / valid_total)
    grad_middle, doc_wide, pending = layer_backward(
        grad_final, context, doc_matrix, doc_weights, doc_saved
    )
    grad_input, ask_wide, (sums, ask_narrow, doc_narrow) = layer_backward(
        grad_middle, context, ask_matrix, ask_weights, ask_saved, pending
    )
    half = sums.shape[0] // 2
    doc_grads = layer_outputs(doc_wide, doc_narrow, sums[:half], context[2])
    ask_grads = layer_outputs(ask_wide, ask_narrow, sums[half:], context[2])
    return (final_low, grad_input) + ask_grads + doc_grads


def layer_specs():
    return (
        P("dp", "tensor"),
        P("dp", "tensor"),
        P("dp", "tensor"),
        P("tensor"),
        P("tensor"),
        P("tensor", "dp"),
        P(),
        P(),
        P(),
        P("dp", "tensor"),
        P("tensor"),
        P("tensor", "dp"),
        P(),
        P(),
        P(),
    )


def solution(mesh):
    rows = P(("dp", "tensor"), None)
    return jax.shard_map(
        on_device,
        mesh=mesh,
        in_specs=(rows, P("dp", None), P(("dp", "tensor")), rows) + layer_specs() * 2,
        out_specs=(rows, rows) + layer_specs() * 2,
        check_vma=False,
    )
```

```python
import jax
import jax.numpy as jnp
from jax import lax
from jax.experimental import pallas as pl
from jax.experimental.pallas import tpu as pltpu
from jax.sharding import PartitionSpec as P

HEAD_DIM = 64
LANES = 128
TILE = 256
BLOCKED = 1e9
SEGMENTS = 16
eps_norm = 1e-12

bf16 = jnp.bfloat16
f32 = jnp.float32
NT = (((1,), (1,)), ((), ()))
TN = (((0,), (0,)), ((), ()))
WHOLE = pl.BlockSpec(memory_space=pltpu.VMEM)


def dot_nn(first_mat, second_mat):
    return jnp.dot(first_mat, second_mat, preferred_element_type=f32)


def dot_nt(first_mat, second_mat):
    return lax.dot_general(first_mat, second_mat, NT, preferred_element_type=f32)


def dot_tn(first_mat, second_mat):
    return lax.dot_general(first_mat, second_mat, TN, preferred_element_type=f32)


def cost(flops):
    return pl.CostEstimate(flops=int(flops), bytes_accessed=0, transcendentals=0)


def kernel_params():
    return pltpu.CompilerParams(vmem_limit_bytes=60 * 1024 * 1024)


def flip(values, bit):
    size = lax.axis_size("tensor")
    return lax.ppermute(values, "tensor", [(i, i ^ bit) for i in range(size)])


def gather_chunks(own, also=None):
    half = own.shape[0] // 2
    near = flip(own, 1)
    far = [flip(own[:half], 2), flip(own[half:], 2)]
    if also is not None:
        far, also = lax.optimization_barrier((far, also))
    last = [flip(part, 1) for part in far]
    return (own, near, jnp.concatenate(far, axis=0), jnp.concatenate(last, axis=0)), also


def exchange_pieces(pieces):
    return [pieces[0]] + [flip(pieces[r], r) for r in range(1, 4)]


def tie(*items):
    return lax.optimization_barrier(items)


def send_around(values, axis, step, count):
    size = lax.axis_size(axis)
    return [
        lax.ppermute(values, axis, [(i, i ^ (step * r)) for i in range(size)])
        for r in range(1, count)
    ]


def add_up(values, others):
    for other in others:
        values = values + other
    return values


def sum_over(values, axis):
    size = lax.axis_size(axis)
    step = 1
    while step < size:
        count = min(8, size // step)
        values = add_up(values, send_around(values, axis, step, count))
        step *= count
    return values


def project(pieces, matrix, query_bias, value_bias, query_marks, key_marks):
    rows, width = pieces[0].shape
    heads = matrix.shape[1] // 3 // HEAD_DIM
    group = heads * HEAD_DIM
    wide = heads * LANES
    sub = rows // 2

    def body(p0, p1, p2, p3, mat, bias_q, bias_v, mark_q, mark_k, out_q, out_k, out_v):
        chunk = pl.program_id(0)
        lane = lax.broadcasted_iota(jnp.int32, (sub, HEAD_DIM), 1)
        ones = jnp.where(lane < 2, 1.0, 0.0).astype(bf16)

        def run(piece):
            for part in range(2):
                at = slice(part * sub, (part + 1) * sub)
                full = dot_nn(piece[at, :], mat[...])
                for h in range(heads):
                    lo = h * HEAD_DIM
                    to = slice(h * LANES, (h + 1) * LANES)
                    q = full[:, lo : lo + HEAD_DIM] + bias_q[:, lo : lo + HEAD_DIM]
                    q = (q.astype(bf16).astype(f32) * HEAD_DIM ** (-0.5)).astype(bf16)
                    k = full[:, group + lo : group + lo + HEAD_DIM].astype(bf16)
                    v = full[:, 2 * group + lo : 2 * group + lo + HEAD_DIM]
                    v = (v + bias_v[:, lo : lo + HEAD_DIM]).astype(bf16)
                    out_q[at, to] = jnp.concatenate([q, mark_q[at, :]], axis=1)
                    out_k[at, to] = jnp.concatenate([k, mark_k[at, :]], axis=1)
                    out_v[at, to] = jnp.concatenate([v, ones], axis=1)

        for r, piece in enumerate((p0, p1, p2, p3)):

            @pl.when(chunk == r)
            def _(piece=piece):
                run(piece)

    out = jax.ShapeDtypeStruct((4 * rows, wide), bf16)
    spec = pl.BlockSpec((rows, wide), lambda i: (i, 0))
    mark_spec = pl.BlockSpec((rows, HEAD_DIM), lambda i: (i, 0))
    return pl.pallas_call(
        body,
        grid=(4,),
        in_specs=[WHOLE] * 7 + [mark_spec] * 2,
        out_specs=[spec] * 3,
        out_shape=[out] * 3,
        compiler_params=kernel_params(),
        cost_estimate=cost(6 * rows * 4 * pieces[0].shape[1] * matrix.shape[1]),
        name="project",
    )(*pieces, matrix, query_bias[None], value_bias[None], query_marks, key_marks)


def attention_forward(low, high, place, queries, keys, values, base):
    rows, wide = queries.shape
    heads = wide // LANES
    count = rows // TILE
    per_chunk = count // 4
    half = rows // 8
    half_blocks = half // TILE
    group = heads * HEAD_DIM
    skip = base * per_chunk

    def body(low_ref, high_ref, place_ref, q_ref, k_ref, v_ref, ctx_ref, ql_ref, *scratch):
        peak, fade, total, score = scratch
        block = pl.program_id(0) + skip
        own = place_ref[0]
        first = low_ref[block]
        last = high_ref[block]
        peak[...] = jnp.full_like(peak, -3e38)
        total[...] = jnp.zeros_like(total)

        def where_is(j):
            spot = ((j // per_chunk) ^ own) * per_chunk + j % per_chunk
            return pl.multiple_of(spot * TILE, TILE)

        def rows_step(j):
            at = where_is(j)
            for h in range(heads):
                to = slice(h * LANES, (h + 1) * LANES)
                s = dot_nt(k_ref[pl.ds(at, TILE), to], q_ref[:, to])
                old = peak[h, 0:1, :]
                top = jnp.maximum(old, jnp.max(s, axis=0, keepdims=True))
                peak[h, 0:1, :] = top
                fade[h, 0:1, :] = jnp.exp(old - top)
                score[h] = s

        def sum_step(j):
            at = where_is(j)
            for h in range(heads):
                v = v_ref[pl.ds(at, TILE), h * LANES : (h + 1) * LANES]
                p = jnp.exp(score[h] - peak[h, 0:1, :]).astype(bf16)
                total[h] = total[h] * fade[h, 0:1, :] + dot_tn(v, p)

        def step(j, carry):
            sum_step(j - 1)
            rows_step(j)
            return carry

        rows_step(first)
        lax.fori_loop(first + 1, last, step, 0)
        sum_step(last - 1)
        feature = lax.broadcasted_iota(jnp.int32, (LANES, TILE), 0)
        lane = lax.broadcasted_iota(jnp.int32, (TILE, LANES), 1)
        mark = HEAD_DIM + SEGMENTS
        outs = []
        for h in range(heads):
            acc = total[h]
            norm = acc[HEAD_DIM : HEAD_DIM + 1, :]
            shift = -(peak[h, 0:1, :] + jnp.log(norm))
            one = shift.astype(bf16).astype(f32)
            two = (shift - one).astype(bf16).astype(f32)
            three = shift - one - two
            both = acc * (1.0 / norm)
            both = jnp.where(feature == mark, one, both)
            both = jnp.where(feature == mark + 1, two, both)
            both = jnp.where(feature == mark + 2, three, both)
            both = both.T.astype(bf16)
            outs.append(both[:, 0:HEAD_DIM])
            to = slice(h * LANES, (h + 1) * LANES)
            inside = (lane >= mark) & (lane < mark + 3)
            ql_ref[:, to] = jnp.where(inside, both, q_ref[:, to])
        ctx = jnp.concatenate(outs, axis=1)
        inside = block % per_chunk
        at = pl.multiple_of((inside % half_blocks) * TILE, TILE)

        @pl.when(inside < half_blocks)
        def _():
            ctx_ref[0, pl.ds(at, TILE), 0:group] = ctx

        @pl.when(inside >= half_blocks)
        def _():
            ctx_ref[0, pl.ds(at, TILE), group : 2 * group] = ctx

    row_spec = pl.BlockSpec((TILE, wide), lambda i, *_: (i + skip, 0))
    return pl.pallas_call(
        body,
        grid_spec=pltpu.PrefetchScalarGridSpec(
            num_scalar_prefetch=3,
            grid=(count // 2,),
            in_specs=[row_spec, WHOLE, WHOLE],
            out_specs=[
                pl.BlockSpec((1, half, 2 * group), lambda i, *_: (i // per_chunk, 0, 0)),
                row_spec,
            ],
            scratch_shapes=[
                pltpu.VMEM((heads, 8, TILE), f32),
                pltpu.VMEM((heads, 8, TILE), f32),
                pltpu.VMEM((heads, LANES, TILE), f32),
                pltpu.VMEM((heads, TILE, TILE), f32),
            ],
        ),
        out_shape=[
            jax.ShapeDtypeStruct((2, half, 2 * group), bf16),
            jax.ShapeDtypeStruct((rows, wide), bf16),
        ],
        compiler_params=kernel_params(),
        input_output_aliases={3: 1},
        cost_estimate=cost(4 * rows * rows * wide),
        name="attention_forward",
    )(low, high, place, queries, keys, values)


def attention_backward(low, high, place, queries, keys, values, contexts, grads):
    rows, wide = queries.shape
    heads = wide // LANES
    count = rows // TILE
    per_chunk = count // 4
    half = rows // 8
    half_blocks = half // TILE
    group = heads * HEAD_DIM

    def body(low_ref, high_ref, place_ref, q_ref, k_ref, v_ref, near, far, g0, g1, g2, g3, *rest):
        dq_ref, dk_ref, dv_ref, do_all, dq_all, acc_k, acc_v, prob, slope = rest
        block = pl.program_id(0)
        own = place_ref[0]
        first = low_ref[block]
        last = high_ref[block]

        @pl.when(block == 0)
        def _():
            dq_all[...] = jnp.zeros_like(dq_all)
            lane = lax.broadcasted_iota(jnp.int32, (TILE, HEAD_DIM), 1)
            for chunk, g_ref in enumerate((g0, g1, g2, g3)):
                c_ref = (near, far)[chunk // 2]

                def prepare(b, carry, chunk=chunk, g_ref=g_ref, c_ref=c_ref):
                    at = pl.multiple_of(b * TILE, TILE)
                    for side in range(2):
                        cols = slice(side * group, (side + 1) * group)
                        row = pl.multiple_of((2 * chunk + side) * half + at, TILE)
                        c = c_ref[chunk % 2, pl.ds(at, TILE), cols].astype(f32)
                        g = g_ref[pl.ds(at, TILE), cols].astype(f32)
                        for h in range(heads):
                            lo = h * HEAD_DIM
                            gh = g[:, lo : lo + HEAD_DIM]
                            ch = c[:, lo : lo + HEAD_DIM]
                            delta = -jnp.sum(gh * ch, axis=1, keepdims=True)
                            one = delta.astype(bf16).astype(f32)
                            two = delta - one
                            tail = jnp.where(lane == 0, one, jnp.where(lane == 1, two, 0.0))
                            both = jnp.concatenate([gh, tail], axis=1).astype(bf16)
                            do_all[pl.ds(row, TILE), h * LANES : (h + 1) * LANES] = both
                    return carry

                lax.fori_loop(0, half_blocks, prepare, 0)

        acc_k[...] = jnp.zeros_like(acc_k)
        acc_v[...] = jnp.zeros_like(acc_v)

        def where_is(j):
            spot = ((j // per_chunk) ^ own) * per_chunk + j % per_chunk
            return pl.multiple_of(spot * TILE, TILE)

        def rows_step(j):
            at = where_is(j)
            for h in range(heads):
                to = slice(h * LANES, (h + 1) * LANES)
                p = jnp.exp(dot_nt(k_ref[:, to], q_ref[pl.ds(at, TILE), to]))
                dp = dot_nt(v_ref[:, to], do_all[pl.ds(at, TILE), to])
                prob[h] = p.astype(bf16)
                slope[h] = (p * dp).astype(bf16)

        def grad_step(j):
            at = where_is(j)
            for h in range(heads):
                to = slice(h * LANES, (h + 1) * LANES)
                ds = slope[h]
                acc_v[h] += dot_nn(prob[h], do_all[pl.ds(at, TILE), to])
                acc_k[h] += dot_nn(ds, q_ref[pl.ds(at, TILE), to])
                dq_all[at // TILE, h] += dot_tn(k_ref[:, to], ds)

        def step(j, carry):
            grad_step(j - 1)
            rows_step(j)
            return carry

        rows_step(first)
        lax.fori_loop(first + 1, last, step, 0)
        grad_step(last - 1)
        dk = [acc_k[h, :, 0:HEAD_DIM] for h in range(heads)]
        dv = [acc_v[h, :, 0:HEAD_DIM] for h in range(heads)]
        dk_ref[...] = jnp.concatenate(dk, axis=1).astype(bf16)
        dv_ref[...] = jnp.concatenate(dv, axis=1).astype(bf16)

        @pl.when(block == count - 1)
        def _():
            def finish(b, carry):
                at = pl.multiple_of(b * TILE, TILE)
                dq = [dq_all[b, h, 0:HEAD_DIM, :] for h in range(heads)]
                dq = jnp.concatenate(dq, axis=0).T * HEAD_DIM ** (-0.5)
                dq_ref[pl.ds(at, TILE), :] = dq.astype(bf16)
                return carry

            lax.fori_loop(0, count, finish, 0)

    row_spec = pl.BlockSpec((TILE, wide), lambda i, *_: (i, 0))
    out_spec = pl.BlockSpec((TILE, group), lambda i, *_: (i, 0))
    out = jax.ShapeDtypeStruct((rows, group), bf16)
    return pl.pallas_call(
        body,
        grid_spec=pltpu.PrefetchScalarGridSpec(
            num_scalar_prefetch=3,
            grid=(count,),
            in_specs=[WHOLE, row_spec, row_spec] + [WHOLE] * 6,
            out_specs=[WHOLE, out_spec, out_spec],
            scratch_shapes=[
                pltpu.VMEM((rows, wide), bf16),
                pltpu.VMEM((count, heads, LANES, TILE), f32),
                pltpu.VMEM((heads, TILE, LANES), f32),
                pltpu.VMEM((heads, TILE, LANES), f32),
                pltpu.VMEM((heads, TILE, TILE), bf16),
                pltpu.VMEM((heads, TILE, TILE), bf16),
            ],
        ),
        out_shape=[out] * 3,
        compiler_params=kernel_params(),
        cost_estimate=cost(24 * rows * rows * wide),
        name="attention_backward",
    )(low, high, place, queries, keys, values, *contexts, *grads)


SQRT_HALF = 0.7071067811865476
PHI_SCALE = 0.3989422804014327


def norm_parts(values):
    centered = values - jnp.mean(values, axis=-1, keepdims=True)
    variance = jnp.mean(centered * centered, axis=-1, keepdims=True)
    scale = lax.rsqrt(variance + eps_norm)
    return centered * scale, scale


def tokens_forward(place, hidden, pieces, weights, up_bias, vectors):
    rows, width = hidden.shape
    half = rows // 2
    group = pieces[0].shape[1] // 2
    part = TILE
    steps = half // part
    size = 2 * part

    def body(place_ref, x_ref, c0, c1, c2, c3, w_ref, ub_ref, vec_ref, *outs):
        o_ref, ob_ref, nb_ref, act_ref, slope_ref, y1_ref, y2_ref, r1_ref, r2_ref = outs
        own = place_ref[0]
        first = x_ref[...].reshape(size, width).astype(f32) + vec_ref[0:1, :]
        for r, c_ref in enumerate((c0, c1, c2, c3)):
            ctx = jnp.concatenate([c_ref[:, 0:group], c_ref[:, group : 2 * group]], axis=0)
            first = first + dot_nt(ctx, w_ref[own ^ r, :, 2 * width : 2 * width + group])
        y1, r1 = norm_parts(first)
        y1_ref[...] = y1.reshape(2, part, width)
        r1_ref[...] = jnp.broadcast_to(r1, (size, LANES)).reshape(2, part, LANES)
        normed = y1 * vec_ref[1:2, :] + vec_ref[2:3, :]
        sent = normed.astype(bf16)
        nb_ref[...] = sent.reshape(2, part, width)
        second = normed + vec_ref[3:4, :]
        for t in range(4):
            cols = slice(t * width, (t + 1) * width)
            inner = dot_nn(sent, w_ref[t, :, 0:width]) + ub_ref[t : t + 1, :]
            cdf = 0.5 + 0.5 * lax.erf(inner * SQRT_HALF)
            act = (inner * cdf).astype(bf16)
            slope = cdf + inner * (PHI_SCALE * jnp.exp(-0.5 * inner * inner))
            act_ref[:, :, cols] = act.reshape(2, part, width)
            slope_ref[:, :, cols] = slope.astype(bf16).reshape(2, part, width)
            second = second + dot_nt(act, w_ref[t, :, width : 2 * width])
        y2, r2 = norm_parts(second)
        y2_ref[...] = y2.reshape(2, part, width)
        r2_ref[...] = jnp.broadcast_to(r2, (size, LANES)).reshape(2, part, LANES)
        result = y2 * vec_ref[4:5, :] + vec_ref[5:6, :]
        o_ref[...] = result.reshape(2, part, width)
        ob_ref[...] = result.astype(bf16).reshape(2, part, width)

    def spec(cols):
        return pl.BlockSpec((2, part, cols), lambda i, *_: (0, i, 0))

    def out(cols, kind):
        return jax.ShapeDtypeStruct((2, half, cols), kind)

    piece_spec = pl.BlockSpec((part, 2 * group), lambda i, *_: (i, 0))
    units = 4 * width
    results = pl.pallas_call(
        body,
        grid_spec=pltpu.PrefetchScalarGridSpec(
            num_scalar_prefetch=1,
            grid=(steps,),
            in_specs=[spec(width)] + [piece_spec] * 4 + [WHOLE] * 3,
            out_specs=[
                spec(width),
                spec(width),
                spec(width),
                spec(units),
                spec(units),
                spec(width),
                spec(width),
                spec(LANES),
                spec(LANES),
            ],
        ),
        out_shape=[
            out(width, f32),
            out(width, bf16),
            out(width, bf16),
            out(units, bf16),
            out(units, bf16),
            out(width, f32),
            out(width, f32),
            out(LANES, f32),
            out(LANES, f32),
        ],
        compiler_params=kernel_params(),
        cost_estimate=cost(8 * rows * width * width * 3),
        name="tokens_forward",
    )(place, hidden.reshape(2, half, width), *pieces, weights, up_bias, vectors)
    return [item.reshape(rows, item.shape[2]) for item in results]


def tokens_backward(place, grad, saved, weights, vectors, group):
    slope, y1, y2, r1, r2 = saved
    rows, width = grad.shape
    half = rows // 2
    part = TILE
    steps = half // part
    size = 2 * part
    units = 4 * width

    def norm_back(g, y, r, gain):
        e = g * gain
        mean_e = jnp.mean(e, axis=-1, keepdims=True)
        mean_ey = jnp.mean(e * y, axis=-1, keepdims=True)
        return r * (e - mean_e - y * mean_ey)

    def body(place_ref, g_ref, sl_ref, y1_ref, y2_ref, r1_ref, r2_ref, w_ref, vec_ref, *outs):
        bg_ref, gi_ref, gf_ref, ag_ref, p0, p1, p2, p3, sum_ref = outs
        own = place_ref[0]

        @pl.when(pl.program_id(0) == 0)
        def _():
            sum_ref[...] = jnp.zeros_like(sum_ref)

        def total(values):
            return jnp.sum(values, axis=0, keepdims=True)

        g = g_ref[...].reshape(size, width)
        y2 = y2_ref[...].reshape(size, width)
        r2 = r2_ref[...].reshape(size, LANES)[:, 0:1]
        second = norm_back(g, y2, r2, vec_ref[4:5, :])
        sum_ref[0:1, :] += total(g * y2)
        sum_ref[1:2, :] += total(g)
        sum_ref[2:3, :] += total(second)
        branch = second.astype(bf16)
        bg_ref[...] = branch.reshape(2, part, width)
        normed = second
        for t in range(4):
            cols = slice(t * width, (t + 1) * width)
            slope_t = sl_ref[:, :, cols].reshape(size, width).astype(f32)
            inner = (dot_nn(branch, w_ref[t, :, width : 2 * width]) * slope_t).astype(bf16)
            gi_ref[:, :, cols] = inner.reshape(2, part, width)
            sum_ref[6 + t : 7 + t, :] += total(inner.astype(f32))
            normed = normed + dot_nt(inner, w_ref[t, :, 0:width])
        y1 = y1_ref[...].reshape(size, width)
        r1 = r1_ref[...].reshape(size, LANES)[:, 0:1]
        first = norm_back(normed, y1, r1, vec_ref[1:2, :])
        sum_ref[3:4, :] += total(normed * y1)
        sum_ref[4:5, :] += total(normed)
        sum_ref[5:6, :] += total(first)
        gf_ref[...] = first.reshape(2, part, width)
        sent = first.astype(bf16)
        ag_ref[...] = sent.reshape(2, part, width)
        for r, p_ref in enumerate((p0, p1, p2, p3)):
            ctx = dot_nn(sent, w_ref[own ^ r, :, 2 * width : 2 * width + group]).astype(bf16)
            p_ref[...] = jnp.concatenate([ctx[0:part], ctx[part:size]], axis=1)

    def spec(cols):
        return pl.BlockSpec((2, part, cols), lambda i, *_: (0, i, 0))

    def out(cols, kind):
        return jax.ShapeDtypeStruct((2, half, cols), kind)

    piece_spec = pl.BlockSpec((part, 2 * group), lambda i, *_: (i, 0))
    piece = jax.ShapeDtypeStruct((half, 2 * group), bf16)
    sums = jax.ShapeDtypeStruct((16, width), f32)

    def view(values):
        return values.reshape(2, half, values.shape[1])

    results = pl.pallas_call(
        body,
        grid_spec=pltpu.PrefetchScalarGridSpec(
            num_scalar_prefetch=1,
            grid=(steps,),
            in_specs=[
                spec(width),
                spec(units),
                spec(width),
                spec(width),
                spec(LANES),
                spec(LANES),
                WHOLE,
                WHOLE,
            ],
            out_specs=[spec(width), spec(units), spec(width), spec(width)]
            + [piece_spec] * 4
            + [pl.BlockSpec((16, width), lambda i, *_: (0, 0))],
        ),
        out_shape=[out(width, bf16), out(units, bf16), out(width, f32), out(width, bf16)]
        + [piece] * 4
        + [sums],
        compiler_params=kernel_params(),
        cost_estimate=cost(8 * rows * width * width * 3),
        name="tokens_backward",
    )(place, view(grad), view(slope), view(y1), view(y2), view(r1), view(r2), weights, vectors)
    big = [item.reshape(rows, item.shape[2]) for item in results[:4]]
    return big, list(results[4:8]), results[8]


def weight_grads(place, sent, inner, branch, act, attn, pieces):
    rows, width = sent.shape
    half = rows // 2
    group = pieces[0].shape[1] // 2

    def body(place_ref, s_ref, i_ref, b_ref, a_ref, g_ref, c0, c1, c2, c3, o_ref):
        t = pl.program_id(0)
        own = place_ref[0]
        o_ref[0, :, 0:width] = dot_tn(s_ref[...], i_ref[...]).astype(bf16)
        o_ref[0, :, width : 2 * width] = dot_tn(b_ref[...], a_ref[...]).astype(bf16)
        for r, c_ref in enumerate((c0, c1, c2, c3)):

            @pl.when(t == own ^ r)
            def _(c_ref=c_ref):
                ctx = jnp.concatenate([c_ref[:, 0:group], c_ref[:, group : 2 * group]], axis=0)
                o_ref[0, :, 2 * width : 2 * width + group] = dot_tn(g_ref[...], ctx).astype(bf16)

    unit_spec = pl.BlockSpec((rows, width), lambda i, *_: (0, i))
    cols = 2 * width + group
    return pl.pallas_call(
        body,
        grid_spec=pltpu.PrefetchScalarGridSpec(
            num_scalar_prefetch=1,
            grid=(4,),
            in_specs=[WHOLE, unit_spec, WHOLE, unit_spec, WHOLE] + [WHOLE] * 4,
            out_specs=pl.BlockSpec((1, width, cols), lambda i, *_: (i, 0, 0)),
        ),
        out_shape=jax.ShapeDtypeStruct((4, width, cols), bf16),
        compiler_params=kernel_params(),
        cost_estimate=cost(8 * rows * width * width * 3),
        name="weight_grads",
    )(place, sent, inner, branch, act, attn, *pieces)


def input_grads(grad_q, grad_k, grad_v, matrix, base, number):
    rows, group = grad_q.shape
    width = matrix.shape[0]
    chunk = rows // 4

    def body(q_ref, k_ref, v_ref, mat, *outs):
        full = dot_nt(q_ref[...], mat[:, 0:group])
        full = full + dot_nt(k_ref[...], mat[:, group : 2 * group])
        full = (full + dot_nt(v_ref[...], mat[:, 2 * group : 3 * group])).astype(bf16)
        for r, o_ref in enumerate(outs):

            @pl.when(pl.program_id(0) == number - 1 - r)
            def _(o_ref=o_ref):
                o_ref[...] = full

    spec = pl.BlockSpec((chunk, group), lambda i: (base + number - 1 - i, 0))
    out = jax.ShapeDtypeStruct((chunk, width), bf16)
    return pl.pallas_call(
        body,
        grid=(number,),
        in_specs=[spec] * 3 + [WHOLE],
        out_specs=[WHOLE] * number,
        out_shape=[out] * number,
        compiler_params=kernel_params(),
        cost_estimate=cost(6 * number * chunk * width * 3 * group),
        name="input_grads",
    )(grad_q, grad_k, grad_v, matrix)


def projection_grads(pieces, grad_q, grad_k, grad_v):
    chunk, width = pieces[0].shape
    group = grad_q.shape[1]

    def body(p0, p1, p2, p3, q_ref, k_ref, v_ref, o_ref, b_ref):
        for n, g_ref in enumerate((q_ref, k_ref, v_ref)):
            cols = slice(n * group, (n + 1) * group)
            acc = jnp.zeros((width, group), f32)
            for r, p_ref in enumerate((p0, p1, p2, p3)):
                acc = acc + dot_tn(p_ref[...], g_ref[r * chunk : (r + 1) * chunk, :])
            o_ref[:, cols] = acc.astype(bf16)
            b_ref[n : n + 1, :] = jnp.sum(g_ref[...].astype(f32), axis=0, keepdims=True)

    return pl.pallas_call(
        body,
        in_specs=[WHOLE] * 7,
        out_specs=[WHOLE] * 2,
        out_shape=[
            jax.ShapeDtypeStruct((width, 3 * group), bf16),
            jax.ShapeDtypeStruct((8, group), f32),
        ],
        compiler_params=kernel_params(),
        cost_estimate=cost(24 * chunk * width * 3 * group),
        name="projection_grads",
    )(*pieces, grad_q, grad_k, grad_v)


def pack_local(params):
    return jnp.concatenate([params[9], params[11].T, params[5].T], axis=1)


def gather_all(local):
    parts = lax.all_gather(local, ("tensor", "dp"), axis=0, tiled=False)
    return parts, parts.reshape(4, -1, local.shape[1])


def with_count(local, count):
    high = count // LANES
    digits = jnp.stack([high, count - high * LANES]).astype(bf16)
    digits = jnp.concatenate([digits, jnp.zeros((HEAD_DIM - 2,), bf16)])
    spare = jnp.broadcast_to(digits[None], (local.shape[0], HEAD_DIM))
    return jnp.concatenate([local, spare], axis=1)


def count_of(parts, column):
    digits = parts[:, 0, column : column + 2].astype(f32)
    return jnp.sum(digits[:, 0]) * LANES + jnp.sum(digits[:, 1])


def layer_forward(hidden, chunks, context, params, matrix, weights, up_bias, ahead=None):
    low, high, place, query_marks, key_marks = context
    vectors = jnp.stack([params[6], params[7], params[8], params[12], params[13], params[14]])
    vectors = jnp.concatenate([vectors, jnp.zeros_like(vectors[:2])], axis=0)
    queries, keys, values = project(
        chunks, matrix, params[3], params[4], query_marks, key_marks
    )
    far, queries = attention_forward(low, high, place, queries, keys, values, 2)
    sent = [flip(far[r], 2 + r) for r in range(2)]
    near, queries = attention_forward(low, high, place, queries, keys, values, 0)
    near, sent = tie(near, sent)
    pieces = [near[0], flip(near[1], 1)] + sent
    pieces, ahead = tie(pieces, ahead)
    contexts = (near, far)
    out, out_low, normed, act, slope, y1, y2, r1, r2 = tokens_forward(
        place, hidden, pieces, weights, up_bias, vectors
    )
    saved = (chunks, queries, keys, values, contexts, pieces, normed, act, slope, y1, y2, r1, r2)
    return out, out_low, saved + (vectors,), ahead


def with_bias(proj, bias, parts):
    rows, cols = proj.shape
    high = bias.astype(bf16)
    low = (bias - high.astype(f32)).astype(bf16)
    tail = jnp.concatenate([high[None], low[None], jnp.zeros((14, cols), bf16)], axis=0)
    tail = jnp.broadcast_to(tail[None], (parts,) + tail.shape)
    return jnp.concatenate([proj.reshape(parts, rows // parts, cols), tail], axis=1)


def layer_backward(grad, context, matrix, weights, saved, earlier=None):
    low, high, place = context[:3]
    chunks, queries, keys, values, contexts, pieces, normed, act, slope = saved[:9]
    y1, y2, r1, r2, vectors = saved[9:]
    width = grad.shape[1]
    parts = lax.axis_size("dp")
    (branch, inner, first, attn), sends, sums = tokens_backward(
        place, grad, (slope, y1, y2, r1, r2), weights, vectors, pieces[0].shape[1] // 2
    )
    around = narrow = None
    if earlier is not None:
        sums = jnp.concatenate([earlier[0], sums], axis=0)
        around = send_around(sums, "tensor", 1, 4)
        narrow = lax.all_to_all(earlier[1], "dp", 0, 0, tiled=True)
    grads = exchange_pieces(sends)
    packed = weight_grads(place, normed, inner, branch, act, attn, pieces)
    grads, packed, around, narrow = tie(grads, packed, around, narrow)
    if earlier is not None:
        sums = sum_over(add_up(sums, around), "dp")
    wide = lax.psum_scatter(
        packed.reshape(4 * width, -1), ("tensor", "dp"), scatter_dimension=0, tiled=True
    ).astype(f32)
    grad_q, grad_k, grad_v = attention_backward(
        low, high, place, queries, keys, values, contexts, grads
    )
    if earlier is not None:
        grad_q, grad_k, grad_v, sums = tie(grad_q, grad_k, grad_v, sums)
    (beyond,) = input_grads(grad_q, grad_k, grad_v, matrix, 3, 1)
    (across,) = input_grads(grad_q, grad_k, grad_v, matrix, 2, 1)
    crossing = (across.astype(f32) + flip(beyond, 1).astype(f32)).astype(bf16)
    crossing, grad_q, grad_k, grad_v = tie(crossing, grad_q, grad_k, grad_v)
    crossing = flip(crossing, 2)
    here, beside = input_grads(grad_q, grad_k, grad_v, matrix, 0, 2)
    grad_in = here.astype(f32) + flip(beside, 1).astype(f32) + crossing.astype(f32)
    grad_in = first + grad_in
    proj, proj_bias = projection_grads(chunks, grad_q, grad_k, grad_v)
    both = with_bias(proj, proj_bias[0:3].reshape(-1), parts)
    if earlier is None:
        grad_in, wide, both = tie(grad_in, wide, both)
        return grad_in, wide, (sums, both)
    both = lax.all_to_all(both, "dp", 0, 0, tiled=True)
    both, grad_in, wide = tie(both, grad_in, wide)
    return grad_in, wide, (sums, both, narrow)


def layer_outputs(wide, narrow, sums, place):
    narrow = jnp.sum(narrow.astype(f32), axis=0)
    width = sums.shape[1]
    group = wide.shape[1] - 2 * width
    own = narrow.shape[0] - 16
    bias = narrow[own] + narrow[own + 1]
    up_row = lax.dynamic_slice_in_dim(sums, 6 + place[0], 1, 0)[0]
    return (
        narrow[:own, 0:group],
        narrow[:own, group : 2 * group],
        narrow[:own, 2 * group : 3 * group],
        bias[0:group],
        bias[2 * group : 3 * group],
        wide[:, 2 * width : 2 * width + group].T,
        sums[5],
        sums[3],
        sums[4],
        wide[:, 0:width],
        up_row,
        wide[:, width : 2 * width].T,
        sums[2],
        sums[0],
        sums[1],
    )


def block_bounds(segments, place):
    total = segments.shape[0]
    blocks = segments.reshape(-1, TILE)
    begin = jnp.sum((segments[None] < blocks[:, :1]).astype(jnp.int32), axis=1) // TILE
    end = jnp.sum((segments[None] <= blocks[:, -1:]).astype(jnp.int32), axis=1)
    end = (end + TILE - 1) // TILE
    both = jnp.stack([begin, end]).reshape(2, 4, -1)
    both = reorder(both, place, 1).reshape(2, total // TILE)
    return both[0], both[1]


def reorder(values, place, axis):
    parts = [lax.dynamic_slice_in_dim(values, place ^ r, 1, axis) for r in range(4)]
    return jnp.concatenate(parts, axis=axis)


def on_device(tokens, segment_ids, valid_mask, teacher, *params):
    ask_params, doc_params = params[:15], params[15:]
    rows, width = tokens.shape
    place = lax.axis_index("tensor")
    segments = segment_ids[0]
    low, high = block_bounds(segments, place)
    local = reorder(segments.reshape(4, rows), place, 0).reshape(-1)
    same = local[:, None] == jnp.arange(SEGMENTS, dtype=jnp.int32)[None]
    spare = HEAD_DIM - SEGMENTS
    query_marks = jnp.pad(jnp.where(same, 0.0, -BLOCKED).astype(bf16), ((0, 0), (0, spare)))
    key_marks = jnp.concatenate(
        [same.astype(bf16), jnp.ones((4 * rows, 3), bf16), jnp.zeros((4 * rows, spare - 3), bf16)],
        axis=1,
    )
    context = (low, high, place[None], query_marks, key_marks)

    ask_matrix = lax.all_gather(
        jnp.concatenate(ask_params[0:3], axis=1), "dp", axis=0, tiled=True
    )
    doc_local = jnp.concatenate(doc_params[0:3], axis=1)
    group3 = doc_local.shape[1]
    doc_local = jnp.pad(doc_local, ((0, 0), (0, LANES)))
    _, ask_weights = gather_all(pack_local(ask_params))
    up_local = jnp.stack([ask_params[10], doc_params[10]])
    up_all = jnp.stack([up_local] + [flip(up_local, r) for r in range(1, 4)])
    up_all = reorder(up_all, place, 0)

    mask_rows = valid_mask.astype(f32)
    doc_pack = pack_local(doc_params)
    column = doc_pack.shape[1]
    doc_pack = with_count(doc_pack, jnp.sum(valid_mask))
    all_rows = rows * lax.axis_size("dp") * lax.axis_size("tensor")

    ask_chunks, ask_matrix = gather_chunks(tokens, ask_matrix)
    doc_matrix = lax.all_gather(doc_local, "dp", axis=0, tiled=True)[:, :group3]
    middle, middle_low, ask_saved, doc_pack = layer_forward(
        tokens,
        ask_chunks,
        context,
        ask_params,
        ask_matrix,
        ask_weights,
        up_all[:, 0],
        doc_pack,
    )
    middle_low, doc_matrix = tie(middle_low, doc_matrix)
    doc_chunks, _ = gather_chunks(middle_low)
    doc_parts, doc_weights = gather_all(doc_pack)
    final, final_low, doc_saved, _ = layer_forward(
        middle,
        doc_chunks,
        context,
        doc_params,
        doc_matrix,
        doc_weights,
        up_all[:, 1],
    )
    valid_total = count_of(doc_parts, column)
    grad_final = mask_rows[:, None] * (final - teacher.astype(f32)) * (all_rows / valid_total)
    grad_middle, doc_wide, pending = layer_backward(
        grad_final, context, doc_matrix, doc_weights, doc_saved
    )
    grad_input, ask_wide, (sums, ask_narrow, doc_narrow) = layer_backward(
        grad_middle, context, ask_matrix, ask_weights, ask_saved, pending
    )
    half = sums.shape[0] // 2
    doc_grads = layer_outputs(doc_wide, doc_narrow, sums[:half], context[2])
    ask_grads = layer_outputs(ask_wide, ask_narrow, sums[half:], context[2])
    return (final_low, grad_input) + ask_grads + doc_grads


def layer_specs():
    return (
        P("dp", "tensor"),
        P("dp", "tensor"),
        P("dp", "tensor"),
        P("tensor"),
        P("tensor"),
        P("tensor", "dp"),
        P(),
        P(),
        P(),
        P("dp", "tensor"),
        P("tensor"),
        P("tensor", "dp"),
        P(),
        P(),
        P(),
    )


def solution(mesh):
    rows = P(("dp", "tensor"), None)
    return jax.shard_map(
        on_device,
        mesh=mesh,
        in_specs=(rows, P("dp", None), P(("dp", "tensor")), rows) + layer_specs() * 2,
        out_specs=(rows, rows) + layer_specs() * 2,
        check_vma=False,
    )
```

```python
import jax
import jax.numpy as jnp
from jax import lax
from jax.experimental import pallas as pl
from jax.experimental.pallas import tpu as pltpu
from jax.sharding import PartitionSpec as P

HEAD_DIM = 64
LANES = 128
TILE = 256
BLOCKED = 1e9
SEGMENTS = 16
eps_norm = 1e-12

bf16 = jnp.bfloat16
f32 = jnp.float32
NT = (((1,), (1,)), ((), ()))
TN = (((0,), (0,)), ((), ()))
WHOLE = pl.BlockSpec(memory_space=pltpu.VMEM)


def dot_nn(first_mat, second_mat):
    return jnp.dot(first_mat, second_mat, preferred_element_type=f32)


def dot_nt(first_mat, second_mat):
    return lax.dot_general(first_mat, second_mat, NT, preferred_element_type=f32)


def dot_tn(first_mat, second_mat):
    return lax.dot_general(first_mat, second_mat, TN, preferred_element_type=f32)


def cost(flops):
    return pl.CostEstimate(flops=int(flops), bytes_accessed=0, transcendentals=0)


def kernel_params():
    return pltpu.CompilerParams(vmem_limit_bytes=60 * 1024 * 1024)


def flip(values, bit):
    size = lax.axis_size("tensor")
    return lax.ppermute(values, "tensor", [(i, i ^ bit) for i in range(size)])


def gather_chunks(own):
    half = own.shape[0] // 2
    near = flip(own, 1)
    far = [flip(own[:half], 2), flip(own[half:], 2)]
    last = [flip(part, 1) for part in far]
    return own, near, jnp.concatenate(far, axis=0), jnp.concatenate(last, axis=0)


def exchange_pieces(pieces):
    return [pieces[0]] + [flip(pieces[r], r) for r in range(1, 4)]


def tie(*items):
    return lax.optimization_barrier(items)


def send_around(values, axis, step, count):
    size = lax.axis_size(axis)
    return [
        lax.ppermute(values, axis, [(i, i ^ (step * r)) for i in range(size)])
        for r in range(1, count)
    ]


def add_up(values, others):
    for other in others:
        values = values + other
    return values


def sum_over(values, axis):
    size = lax.axis_size(axis)
    step = 1
    while step < size:
        count = min(8, size // step)
        values = add_up(values, send_around(values, axis, step, count))
        step *= count
    return values


def project(pieces, matrix, query_bias, value_bias, query_marks, key_marks):
    rows, width = pieces[0].shape
    heads = matrix.shape[1] // 3 // HEAD_DIM
    group = heads * HEAD_DIM
    wide = heads * LANES
    sub = rows // 2

    def body(p0, p1, p2, p3, mat, bias_q, bias_v, mark_q, mark_k, out_q, out_k, out_v):
        chunk = pl.program_id(0)
        lane = lax.broadcasted_iota(jnp.int32, (sub, HEAD_DIM), 1)
        ones = jnp.where(lane < 2, 1.0, 0.0).astype(bf16)

        def run(piece):
            for part in range(2):
                at = slice(part * sub, (part + 1) * sub)
                full = dot_nn(piece[at, :], mat[...])
                for h in range(heads):
                    lo = h * HEAD_DIM
                    to = slice(h * LANES, (h + 1) * LANES)
                    q = full[:, lo : lo + HEAD_DIM] + bias_q[:, lo : lo + HEAD_DIM]
                    q = (q.astype(bf16).astype(f32) * HEAD_DIM ** (-0.5)).astype(bf16)
                    k = full[:, group + lo : group + lo + HEAD_DIM].astype(bf16)
                    v = full[:, 2 * group + lo : 2 * group + lo + HEAD_DIM]
                    v = (v + bias_v[:, lo : lo + HEAD_DIM]).astype(bf16)
                    out_q[at, to] = jnp.concatenate([q, mark_q[at, :]], axis=1)
                    out_k[at, to] = jnp.concatenate([k, mark_k[at, :]], axis=1)
                    out_v[at, to] = jnp.concatenate([v, ones], axis=1)

        for r, piece in enumerate((p0, p1, p2, p3)):

            @pl.when(chunk == r)
            def _(piece=piece):
                run(piece)

    out = jax.ShapeDtypeStruct((4 * rows, wide), bf16)
    spec = pl.BlockSpec((rows, wide), lambda i: (i, 0))
    mark_spec = pl.BlockSpec((rows, HEAD_DIM), lambda i: (i, 0))
    return pl.pallas_call(
        body,
        grid=(4,),
        in_specs=[WHOLE] * 7 + [mark_spec] * 2,
        out_specs=[spec] * 3,
        out_shape=[out] * 3,
        compiler_params=kernel_params(),
        cost_estimate=cost(6 * rows * 4 * pieces[0].shape[1] * matrix.shape[1]),
        name="project",
    )(*pieces, matrix, query_bias[None], value_bias[None], query_marks, key_marks)


def attention_forward(low, high, place, queries, keys, values):
    rows, wide = queries.shape
    heads = wide // LANES
    count = rows // TILE
    per_chunk = count // 4
    half = rows // 8
    half_blocks = half // TILE
    group = heads * HEAD_DIM

    def body(low_ref, high_ref, place_ref, q_ref, k_ref, v_ref, ctx_ref, ql_ref, *scratch):
        peak, fade, total, score = scratch
        block = pl.program_id(0)
        own = place_ref[0]
        first = low_ref[block]
        last = high_ref[block]
        peak[...] = jnp.full_like(peak, -3e38)
        total[...] = jnp.zeros_like(total)

        def where_is(j):
            spot = ((j // per_chunk) ^ own) * per_chunk + j % per_chunk
            return pl.multiple_of(spot * TILE, TILE)

        def rows_step(j):
            at = where_is(j)
            for h in range(heads):
                to = slice(h * LANES, (h + 1) * LANES)
                s = dot_nt(k_ref[pl.ds(at, TILE), to], q_ref[:, to])
                old = peak[h, 0:1, :]
                top = jnp.maximum(old, jnp.max(s, axis=0, keepdims=True))
                peak[h, 0:1, :] = top
                fade[h, 0:1, :] = jnp.exp(old - top)
                score[h] = s

        def sum_step(j):
            at = where_is(j)
            for h in range(heads):
                v = v_ref[pl.ds(at, TILE), h * LANES : (h + 1) * LANES]
                p = jnp.exp(score[h] - peak[h, 0:1, :]).astype(bf16)
                total[h] = total[h] * fade[h, 0:1, :] + dot_tn(v, p)

        def step(j, carry):
            sum_step(j - 1)
            rows_step(j)
            return carry

        rows_step(first)
        lax.fori_loop(first + 1, last, step, 0)
        sum_step(last - 1)
        feature = lax.broadcasted_iota(jnp.int32, (LANES, TILE), 0)
        lane = lax.broadcasted_iota(jnp.int32, (TILE, LANES), 1)
        mark = HEAD_DIM + SEGMENTS
        outs = []
        for h in range(heads):
            acc = total[h]
            norm = acc[HEAD_DIM : HEAD_DIM + 1, :]
            shift = -(peak[h, 0:1, :] + jnp.log(norm))
            one = shift.astype(bf16).astype(f32)
            two = (shift - one).astype(bf16).astype(f32)
            three = shift - one - two
            both = acc * (1.0 / norm)
            both = jnp.where(feature == mark, one, both)
            both = jnp.where(feature == mark + 1, two, both)
            both = jnp.where(feature == mark + 2, three, both)
            both = both.T.astype(bf16)
            outs.append(both[:, 0:HEAD_DIM])
            to = slice(h * LANES, (h + 1) * LANES)
            inside = (lane >= mark) & (lane < mark + 3)
            ql_ref[:, to] = jnp.where(inside, both, q_ref[:, to])
        ctx = jnp.concatenate(outs, axis=1)
        inside = block % per_chunk
        at = pl.multiple_of((inside % half_blocks) * TILE, TILE)

        @pl.when(inside < half_blocks)
        def _():
            ctx_ref[0, pl.ds(at, TILE), 0:group] = ctx

        @pl.when(inside >= half_blocks)
        def _():
            ctx_ref[0, pl.ds(at, TILE), group : 2 * group] = ctx

    row_spec = pl.BlockSpec((TILE, wide), lambda i, *_: (i, 0))
    return pl.pallas_call(
        body,
        grid_spec=pltpu.PrefetchScalarGridSpec(
            num_scalar_prefetch=3,
            grid=(count,),
            in_specs=[row_spec, WHOLE, WHOLE],
            out_specs=[
                pl.BlockSpec((1, half, 2 * group), lambda i, *_: (i // per_chunk, 0, 0)),
                row_spec,
            ],
            scratch_shapes=[
                pltpu.VMEM((heads, 8, TILE), f32),
                pltpu.VMEM((heads, 8, TILE), f32),
                pltpu.VMEM((heads, LANES, TILE), f32),
                pltpu.VMEM((heads, TILE, TILE), f32),
            ],
        ),
        out_shape=[
            jax.ShapeDtypeStruct((4, half, 2 * group), bf16),
            jax.ShapeDtypeStruct((rows, wide), bf16),
        ],
        compiler_params=kernel_params(),
        cost_estimate=cost(12 * rows * rows * wide),
        name="attention_forward",
    )(low, high, place, queries, keys, values)


def attention_backward(low, high, place, queries, keys, values, contexts, grads):
    rows, wide = queries.shape
    heads = wide // LANES
    count = rows // TILE
    per_chunk = count // 4
    half = rows // 8
    half_blocks = half // TILE
    group = heads * HEAD_DIM

    def body(low_ref, high_ref, place_ref, q_ref, k_ref, v_ref, c_ref, g0, g1, g2, g3, *rest):
        dq_ref, dk_ref, dv_ref, do_all, dq_all, acc_k, acc_v, prob, slope = rest
        block = pl.program_id(0)
        own = place_ref[0]
        first = low_ref[block]
        last = high_ref[block]

        @pl.when(block == 0)
        def _():
            dq_all[...] = jnp.zeros_like(dq_all)
            lane = lax.broadcasted_iota(jnp.int32, (TILE, HEAD_DIM), 1)
            for chunk, g_ref in enumerate((g0, g1, g2, g3)):

                def prepare(b, carry, chunk=chunk, g_ref=g_ref):
                    at = pl.multiple_of(b * TILE, TILE)
                    for side in range(2):
                        cols = slice(side * group, (side + 1) * group)
                        row = pl.multiple_of((2 * chunk + side) * half + at, TILE)
                        c = c_ref[chunk, pl.ds(at, TILE), cols].astype(f32)
                        g = g_ref[pl.ds(at, TILE), cols].astype(f32)
                        for h in range(heads):
                            lo = h * HEAD_DIM
                            gh = g[:, lo : lo + HEAD_DIM]
                            ch = c[:, lo : lo + HEAD_DIM]
                            delta = -jnp.sum(gh * ch, axis=1, keepdims=True)
                            one = delta.astype(bf16).astype(f32)
                            two = delta - one
                            tail = jnp.where(lane == 0, one, jnp.where(lane == 1, two, 0.0))
                            both = jnp.concatenate([gh, tail], axis=1).astype(bf16)
                            do_all[pl.ds(row, TILE), h * LANES : (h + 1) * LANES] = both
                    return carry

                lax.fori_loop(0, half_blocks, prepare, 0)

        acc_k[...] = jnp.zeros_like(acc_k)
        acc_v[...] = jnp.zeros_like(acc_v)

        def where_is(j):
            spot = ((j // per_chunk) ^ own) * per_chunk + j % per_chunk
            return pl.multiple_of(spot * TILE, TILE)

        def rows_step(j):
            at = where_is(j)
            for h in range(heads):
                to = slice(h * LANES, (h + 1) * LANES)
                p = jnp.exp(dot_nt(k_ref[:, to], q_ref[pl.ds(at, TILE), to]))
                dp = dot_nt(v_ref[:, to], do_all[pl.ds(at, TILE), to])
                prob[h] = p.astype(bf16)
                slope[h] = (p * dp).astype(bf16)

        def grad_step(j):
            at = where_is(j)
            for h in range(heads):
                to = slice(h * LANES, (h + 1) * LANES)
                ds = slope[h]
                acc_v[h] += dot_nn(prob[h], do_all[pl.ds(at, TILE), to])
                acc_k[h] += dot_nn(ds, q_ref[pl.ds(at, TILE), to])
                dq_all[at // TILE, h] += dot_tn(k_ref[:, to], ds)

        def step(j, carry):
            grad_step(j - 1)
            rows_step(j)
            return carry

        rows_step(first)
        lax.fori_loop(first + 1, last, step, 0)
        grad_step(last - 1)
        dk = [acc_k[h, :, 0:HEAD_DIM] for h in range(heads)]
        dv = [acc_v[h, :, 0:HEAD_DIM] for h in range(heads)]
        dk_ref[...] = jnp.concatenate(dk, axis=1).astype(bf16)
        dv_ref[...] = jnp.concatenate(dv, axis=1).astype(bf16)

        @pl.when(block == count - 1)
        def _():
            def finish(b, carry):
                at = pl.multiple_of(b * TILE, TILE)
                dq = [dq_all[b, h, 0:HEAD_DIM, :] for h in range(heads)]
                dq = jnp.concatenate(dq, axis=0).T * HEAD_DIM ** (-0.5)
                dq_ref[pl.ds(at, TILE), :] = dq.astype(bf16)
                return carry

            lax.fori_loop(0, count, finish, 0)

    row_spec = pl.BlockSpec((TILE, wide), lambda i, *_: (i, 0))
    out_spec = pl.BlockSpec((TILE, group), lambda i, *_: (i, 0))
    out = jax.ShapeDtypeStruct((rows, group), bf16)
    return pl.pallas_call(
        body,
        grid_spec=pltpu.PrefetchScalarGridSpec(
            num_scalar_prefetch=3,
            grid=(count,),
            in_specs=[WHOLE, row_spec, row_spec] + [WHOLE] * 5,
            out_specs=[WHOLE, out_spec, out_spec],
            scratch_shapes=[
                pltpu.VMEM((rows, wide), bf16),
                pltpu.VMEM((count, heads, LANES, TILE), f32),
                pltpu.VMEM((heads, TILE, LANES), f32),
                pltpu.VMEM((heads, TILE, LANES), f32),
                pltpu.VMEM((heads, TILE, TILE), bf16),
                pltpu.VMEM((heads, TILE, TILE), bf16),
            ],
        ),
        out_shape=[out] * 3,
        compiler_params=kernel_params(),
        cost_estimate=cost(24 * rows * rows * wide),
        name="attention_backward",
    )(low, high, place, queries, keys, values, contexts, *grads)


SQRT_HALF = 0.7071067811865476
PHI_SCALE = 0.3989422804014327


def norm_parts(values):
    centered = values - jnp.mean(values, axis=-1, keepdims=True)
    variance = jnp.mean(centered * centered, axis=-1, keepdims=True)
    scale = lax.rsqrt(variance + eps_norm)
    return centered * scale, scale


def tokens_forward(place, hidden, pieces, weights, up_bias, vectors):
    rows, width = hidden.shape
    half = rows // 2
    group = pieces[0].shape[1] // 2
    part = TILE
    steps = half // part
    size = 2 * part

    def body(place_ref, x_ref, c0, c1, c2, c3, w_ref, ub_ref, vec_ref, *outs):
        o_ref, ob_ref, nb_ref, act_ref, slope_ref, y1_ref, y2_ref, r1_ref, r2_ref = outs
        own = place_ref[0]
        first = x_ref[...].reshape(size, width).astype(f32) + vec_ref[0:1, :]
        for r, c_ref in enumerate((c0, c1, c2, c3)):
            ctx = jnp.concatenate([c_ref[:, 0:group], c_ref[:, group : 2 * group]], axis=0)
            first = first + dot_nt(ctx, w_ref[own ^ r, :, 2 * width : 2 * width + group])
        y1, r1 = norm_parts(first)
        y1_ref[...] = y1.reshape(2, part, width)
        r1_ref[...] = jnp.broadcast_to(r1, (size, LANES)).reshape(2, part, LANES)
        normed = y1 * vec_ref[1:2, :] + vec_ref[2:3, :]
        sent = normed.astype(bf16)
        nb_ref[...] = sent.reshape(2, part, width)
        second = normed + vec_ref[3:4, :]
        for t in range(4):
            cols = slice(t * width, (t + 1) * width)
            inner = dot_nn(sent, w_ref[t, :, 0:width]) + ub_ref[t : t + 1, :]
            cdf = 0.5 + 0.5 * lax.erf(inner * SQRT_HALF)
            act = (inner * cdf).astype(bf16)
            slope = cdf + inner * (PHI_SCALE * jnp.exp(-0.5 * inner * inner))
            act_ref[:, :, cols] = act.reshape(2, part, width)
            slope_ref[:, :, cols] = slope.astype(bf16).reshape(2, part, width)
            second = second + dot_nt(act, w_ref[t, :, width : 2 * width])
        y2, r2 = norm_parts(second)
        y2_ref[...] = y2.reshape(2, part, width)
        r2_ref[...] = jnp.broadcast_to(r2, (size, LANES)).reshape(2, part, LANES)
        result = y2 * vec_ref[4:5, :] + vec_ref[5:6, :]
        o_ref[...] = result.reshape(2, part, width)
        ob_ref[...] = result.astype(bf16).reshape(2, part, width)

    def spec(cols):
        return pl.BlockSpec((2, part, cols), lambda i, *_: (0, i, 0))

    def out(cols, kind):
        return jax.ShapeDtypeStruct((2, half, cols), kind)

    piece_spec = pl.BlockSpec((part, 2 * group), lambda i, *_: (i, 0))
    units = 4 * width
    results = pl.pallas_call(
        body,
        grid_spec=pltpu.PrefetchScalarGridSpec(
            num_scalar_prefetch=1,
            grid=(steps,),
            in_specs=[spec(width)] + [piece_spec] * 4 + [WHOLE] * 3,
            out_specs=[
                spec(width),
                spec(width),
                spec(width),
                spec(units),
                spec(units),
                spec(width),
                spec(width),
                spec(LANES),
                spec(LANES),
            ],
        ),
        out_shape=[
            out(width, f32),
            out(width, bf16),
            out(width, bf16),
            out(units, bf16),
            out(units, bf16),
            out(width, f32),
            out(width, f32),
            out(LANES, f32),
            out(LANES, f32),
        ],
        compiler_params=kernel_params(),
        cost_estimate=cost(8 * rows * width * width * 3),
        name="tokens_forward",
    )(place, hidden.reshape(2, half, width), *pieces, weights, up_bias, vectors)
    return [item.reshape(rows, item.shape[2]) for item in results]


def tokens_backward(place, grad, saved, weights, vectors, group):
    slope, y1, y2, r1, r2 = saved
    rows, width = grad.shape
    half = rows // 2
    part = TILE
    steps = half // part
    size = 2 * part
    units = 4 * width

    def norm_back(g, y, r, gain):
        e = g * gain
        mean_e = jnp.mean(e, axis=-1, keepdims=True)
        mean_ey = jnp.mean(e * y, axis=-1, keepdims=True)
        return r * (e - mean_e - y * mean_ey)

    def body(place_ref, g_ref, sl_ref, y1_ref, y2_ref, r1_ref, r2_ref, w_ref, vec_ref, *outs):
        bg_ref, gi_ref, gf_ref, ag_ref, p0, p1, p2, p3, sum_ref = outs
        own = place_ref[0]

        @pl.when(pl.program_id(0) == 0)
        def _():
            sum_ref[...] = jnp.zeros_like(sum_ref)

        def total(values):
            return jnp.sum(values, axis=0, keepdims=True)

        g = g_ref[...].reshape(size, width)
        y2 = y2_ref[...].reshape(size, width)
        r2 = r2_ref[...].reshape(size, LANES)[:, 0:1]
        second = norm_back(g, y2, r2, vec_ref[4:5, :])
        sum_ref[0:1, :] += total(g * y2)
        sum_ref[1:2, :] += total(g)
        sum_ref[2:3, :] += total(second)
        branch = second.astype(bf16)
        bg_ref[...] = branch.reshape(2, part, width)
        normed = second
        for t in range(4):
            cols = slice(t * width, (t + 1) * width)
            slope_t = sl_ref[:, :, cols].reshape(size, width).astype(f32)
            inner = (dot_nn(branch, w_ref[t, :, width : 2 * width]) * slope_t).astype(bf16)
            gi_ref[:, :, cols] = inner.reshape(2, part, width)
            sum_ref[6 + t : 7 + t, :] += total(inner.astype(f32))
            normed = normed + dot_nt(inner, w_ref[t, :, 0:width])
        y1 = y1_ref[...].reshape(size, width)
        r1 = r1_ref[...].reshape(size, LANES)[:, 0:1]
        first = norm_back(normed, y1, r1, vec_ref[1:2, :])
        sum_ref[3:4, :] += total(normed * y1)
        sum_ref[4:5, :] += total(normed)
        sum_ref[5:6, :] += total(first)
        gf_ref[...] = first.reshape(2, part, width)
        sent = first.astype(bf16)
        ag_ref[...] = sent.reshape(2, part, width)
        for r, p_ref in enumerate((p0, p1, p2, p3)):
            ctx = dot_nn(sent, w_ref[own ^ r, :, 2 * width : 2 * width + group]).astype(bf16)
            p_ref[...] = jnp.concatenate([ctx[0:part], ctx[part:size]], axis=1)

    def spec(cols):
        return pl.BlockSpec((2, part, cols), lambda i, *_: (0, i, 0))

    def out(cols, kind):
        return jax.ShapeDtypeStruct((2, half, cols), kind)

    piece_spec = pl.BlockSpec((part, 2 * group), lambda i, *_: (i, 0))
    piece = jax.ShapeDtypeStruct((half, 2 * group), bf16)
    sums = jax.ShapeDtypeStruct((16, width), f32)

    def view(values):
        return values.reshape(2, half, values.shape[1])

    results = pl.pallas_call(
        body,
        grid_spec=pltpu.PrefetchScalarGridSpec(
            num_scalar_prefetch=1,
            grid=(steps,),
            in_specs=[
                spec(width),
                spec(units),
                spec(width),
                spec(width),
                spec(LANES),
                spec(LANES),
                WHOLE,
                WHOLE,
            ],
            out_specs=[spec(width), spec(units), spec(width), spec(width)]
            + [piece_spec] * 4
            + [pl.BlockSpec((16, width), lambda i, *_: (0, 0))],
        ),
        out_shape=[out(width, bf16), out(units, bf16), out(width, f32), out(width, bf16)]
        + [piece] * 4
        + [sums],
        compiler_params=kernel_params(),
        cost_estimate=cost(8 * rows * width * width * 3),
        name="tokens_backward",
    )(place, view(grad), view(slope), view(y1), view(y2), view(r1), view(r2), weights, vectors)
    big = [item.reshape(rows, item.shape[2]) for item in results[:4]]
    return big, list(results[4:8]), results[8]


def weight_grads(place, sent, inner, branch, act, attn, pieces):
    rows, width = sent.shape
    half = rows // 2
    group = pieces[0].shape[1] // 2

    def body(place_ref, s_ref, i_ref, b_ref, a_ref, g_ref, c0, c1, c2, c3, o_ref):
        t = pl.program_id(0)
        own = place_ref[0]
        o_ref[0, :, 0:width] = dot_tn(s_ref[...], i_ref[...]).astype(bf16)
        o_ref[0, :, width : 2 * width] = dot_tn(b_ref[...], a_ref[...]).astype(bf16)
        for r, c_ref in enumerate((c0, c1, c2, c3)):

            @pl.when(t == own ^ r)
            def _(c_ref=c_ref):
                ctx = jnp.concatenate([c_ref[:, 0:group], c_ref[:, group : 2 * group]], axis=0)
                o_ref[0, :, 2 * width : 2 * width + group] = dot_tn(g_ref[...], ctx).astype(bf16)

    unit_spec = pl.BlockSpec((rows, width), lambda i, *_: (0, i))
    cols = 2 * width + group
    return pl.pallas_call(
        body,
        grid_spec=pltpu.PrefetchScalarGridSpec(
            num_scalar_prefetch=1,
            grid=(4,),
            in_specs=[WHOLE, unit_spec, WHOLE, unit_spec, WHOLE] + [WHOLE] * 4,
            out_specs=pl.BlockSpec((1, width, cols), lambda i, *_: (i, 0, 0)),
        ),
        out_shape=jax.ShapeDtypeStruct((4, width, cols), bf16),
        compiler_params=kernel_params(),
        cost_estimate=cost(8 * rows * width * width * 3),
        name="weight_grads",
    )(place, sent, inner, branch, act, attn, *pieces)


def input_grads(grad_q, grad_k, grad_v, matrix, base, number):
    rows, group = grad_q.shape
    width = matrix.shape[0]
    chunk = rows // 4

    def body(q_ref, k_ref, v_ref, mat, *outs):
        full = dot_nt(q_ref[...], mat[:, 0:group])
        full = full + dot_nt(k_ref[...], mat[:, group : 2 * group])
        full = (full + dot_nt(v_ref[...], mat[:, 2 * group : 3 * group])).astype(bf16)
        for r, o_ref in enumerate(outs):

            @pl.when(pl.program_id(0) == number - 1 - r)
            def _(o_ref=o_ref):
                o_ref[...] = full

    spec = pl.BlockSpec((chunk, group), lambda i: (base + number - 1 - i, 0))
    out = jax.ShapeDtypeStruct((chunk, width), bf16)
    return pl.pallas_call(
        body,
        grid=(number,),
        in_specs=[spec] * 3 + [WHOLE],
        out_specs=[WHOLE] * number,
        out_shape=[out] * number,
        compiler_params=kernel_params(),
        cost_estimate=cost(6 * number * chunk * width * 3 * group),
        name="input_grads",
    )(grad_q, grad_k, grad_v, matrix)


def projection_grads(pieces, grad_q, grad_k, grad_v):
    chunk, width = pieces[0].shape
    group = grad_q.shape[1]

    def body(p0, p1, p2, p3, q_ref, k_ref, v_ref, o_ref, b_ref):
        for n, g_ref in enumerate((q_ref, k_ref, v_ref)):
            cols = slice(n * group, (n + 1) * group)
            acc = jnp.zeros((width, group), f32)
            for r, p_ref in enumerate((p0, p1, p2, p3)):
                acc = acc + dot_tn(p_ref[...], g_ref[r * chunk : (r + 1) * chunk, :])
            o_ref[:, cols] = acc.astype(bf16)
            b_ref[n : n + 1, :] = jnp.sum(g_ref[...].astype(f32), axis=0, keepdims=True)

    return pl.pallas_call(
        body,
        in_specs=[WHOLE] * 7,
        out_specs=[WHOLE] * 2,
        out_shape=[
            jax.ShapeDtypeStruct((width, 3 * group), bf16),
            jax.ShapeDtypeStruct((8, group), f32),
        ],
        compiler_params=kernel_params(),
        cost_estimate=cost(24 * chunk * width * 3 * group),
        name="projection_grads",
    )(*pieces, grad_q, grad_k, grad_v)


def pack_local(params):
    return jnp.concatenate([params[9], params[11].T, params[5].T], axis=1)


def gather_all(local):
    parts = lax.all_gather(local, ("tensor", "dp"), axis=0, tiled=False)
    return parts, parts.reshape(4, -1, local.shape[1])


def with_count(local, count):
    high = count // LANES
    digits = jnp.stack([high, count - high * LANES]).astype(bf16)
    digits = jnp.concatenate([digits, jnp.zeros((HEAD_DIM - 2,), bf16)])
    spare = jnp.broadcast_to(digits[None], (local.shape[0], HEAD_DIM))
    return jnp.concatenate([local, spare], axis=1)


def count_of(parts, column):
    digits = parts[:, 0, column : column + 2].astype(f32)
    return jnp.sum(digits[:, 0]) * LANES + jnp.sum(digits[:, 1])


def layer_forward(hidden, chunks, context, params, matrix, weights, up_bias, ahead=None):
    low, high, place, query_marks, key_marks = context
    vectors = jnp.stack([params[6], params[7], params[8], params[12], params[13], params[14]])
    vectors = jnp.concatenate([vectors, jnp.zeros_like(vectors[:2])], axis=0)
    queries, keys, values = project(
        chunks, matrix, params[3], params[4], query_marks, key_marks
    )
    contexts, queries = attention_forward(low, high, place, queries, keys, values)
    contexts, ahead = tie(contexts, ahead)
    pieces = exchange_pieces([contexts[r] for r in range(4)])
    out, out_low, normed, act, slope, y1, y2, r1, r2 = tokens_forward(
        place, hidden, pieces, weights, up_bias, vectors
    )
    saved = (chunks, queries, keys, values, contexts, pieces, normed, act, slope, y1, y2, r1, r2)
    return out, out_low, saved + (vectors,), ahead


def with_bias(proj, bias, parts):
    rows, cols = proj.shape
    high = bias.astype(bf16)
    low = (bias - high.astype(f32)).astype(bf16)
    tail = jnp.concatenate([high[None], low[None], jnp.zeros((14, cols), bf16)], axis=0)
    tail = jnp.broadcast_to(tail[None], (parts,) + tail.shape)
    return jnp.concatenate([proj.reshape(parts, rows // parts, cols), tail], axis=1)


def layer_backward(grad, context, matrix, weights, saved, earlier=None):
    low, high, place = context[:3]
    chunks, queries, keys, values, contexts, pieces, normed, act, slope = saved[:9]
    y1, y2, r1, r2, vectors = saved[9:]
    width = grad.shape[1]
    parts = lax.axis_size("dp")
    (branch, inner, first, attn), sends, sums = tokens_backward(
        place, grad, (slope, y1, y2, r1, r2), weights, vectors, pieces[0].shape[1] // 2
    )
    around = narrow = None
    if earlier is not None:
        sums = jnp.concatenate([earlier[0], sums], axis=0)
        around = send_around(sums, "tensor", 1, 4)
        narrow = lax.all_to_all(earlier[1], "dp", 0, 0, tiled=True)
    grads = exchange_pieces(sends)
    packed = weight_grads(place, normed, inner, branch, act, attn, pieces)
    grads, packed, around, narrow = tie(grads, packed, around, narrow)
    if earlier is not None:
        sums = sum_over(add_up(sums, around), "dp")
    wide = lax.psum_scatter(
        packed.reshape(4 * width, -1), ("tensor", "dp"), scatter_dimension=0, tiled=True
    ).astype(f32)
    grad_q, grad_k, grad_v = attention_backward(
        low, high, place, queries, keys, values, contexts, grads
    )
    if earlier is not None:
        grad_q, grad_k, grad_v, sums = tie(grad_q, grad_k, grad_v, sums)
    (beyond,) = input_grads(grad_q, grad_k, grad_v, matrix, 3, 1)
    (across,) = input_grads(grad_q, grad_k, grad_v, matrix, 2, 1)
    crossing = (across.astype(f32) + flip(beyond, 1).astype(f32)).astype(bf16)
    crossing, grad_q, grad_k, grad_v = tie(crossing, grad_q, grad_k, grad_v)
    crossing = flip(crossing, 2)
    here, beside = input_grads(grad_q, grad_k, grad_v, matrix, 0, 2)
    grad_in = here.astype(f32) + flip(beside, 1).astype(f32) + crossing.astype(f32)
    grad_in = first + grad_in
    proj, proj_bias = projection_grads(chunks, grad_q, grad_k, grad_v)
    both = with_bias(proj, proj_bias[0:3].reshape(-1), parts)
    if earlier is None:
        grad_in, wide, both = tie(grad_in, wide, both)
        return grad_in, wide, (sums, both)
    both = lax.all_to_all(both, "dp", 0, 0, tiled=True)
    both, grad_in, wide = tie(both, grad_in, wide)
    return grad_in, wide, (sums, both, narrow)


def layer_outputs(wide, narrow, sums, place):
    narrow = jnp.sum(narrow.astype(f32), axis=0)
    width = sums.shape[1]
    group = wide.shape[1] - 2 * width
    own = narrow.shape[0] - 16
    bias = narrow[own] + narrow[own + 1]
    up_row = lax.dynamic_slice_in_dim(sums, 6 + place[0], 1, 0)[0]
    return (
        narrow[:own, 0:group],
        narrow[:own, group : 2 * group],
        narrow[:own, 2 * group : 3 * group],
        bias[0:group],
        bias[2 * group : 3 * group],
        wide[:, 2 * width : 2 * width + group].T,
        sums[5],
        sums[3],
        sums[4],
        wide[:, 0:width],
        up_row,
        wide[:, width : 2 * width].T,
        sums[2],
        sums[0],
        sums[1],
    )


def block_bounds(segments, place):
    total = segments.shape[0]
    blocks = segments.reshape(-1, TILE)
    begin = jnp.sum((segments[None] < blocks[:, :1]).astype(jnp.int32), axis=1) // TILE
    end = jnp.sum((segments[None] <= blocks[:, -1:]).astype(jnp.int32), axis=1)
    end = (end + TILE - 1) // TILE
    both = jnp.stack([begin, end]).reshape(2, 4, -1)
    both = reorder(both, place, 1).reshape(2, total // TILE)
    return both[0], both[1]


def reorder(values, place, axis):
    parts = [lax.dynamic_slice_in_dim(values, place ^ r, 1, axis) for r in range(4)]
    return jnp.concatenate(parts, axis=axis)


def on_device(tokens, segment_ids, valid_mask, teacher, *params):
    ask_params, doc_params = params[:15], params[15:]
    rows, width = tokens.shape
    place = lax.axis_index("tensor")
    segments = segment_ids[0]
    low, high = block_bounds(segments, place)
    local = reorder(segments.reshape(4, rows), place, 0).reshape(-1)
    same = local[:, None] == jnp.arange(SEGMENTS, dtype=jnp.int32)[None]
    spare = HEAD_DIM - SEGMENTS
    query_marks = jnp.pad(jnp.where(same, 0.0, -BLOCKED).astype(bf16), ((0, 0), (0, spare)))
    key_marks = jnp.concatenate(
        [same.astype(bf16), jnp.ones((4 * rows, 3), bf16), jnp.zeros((4 * rows, spare - 3), bf16)],
        axis=1,
    )
    context = (low, high, place[None], query_marks, key_marks)

    ask_matrix = lax.all_gather(
        jnp.concatenate(ask_params[0:3], axis=1), "dp", axis=0, tiled=True
    )
    doc_local = jnp.concatenate(doc_params[0:3], axis=1)
    group3 = doc_local.shape[1]
    doc_local = jnp.pad(doc_local, ((0, 0), (0, LANES)))
    _, ask_weights = gather_all(pack_local(ask_params))
    doc_matrix = lax.all_gather(doc_local, "dp", axis=0, tiled=True)[:, :group3]
    up_local = jnp.stack([ask_params[10], doc_params[10]])
    up_all = jnp.stack([up_local] + [flip(up_local, r) for r in range(1, 4)])
    up_all = reorder(up_all, place, 0)

    mask_rows = valid_mask.astype(f32)
    doc_pack = pack_local(doc_params)
    column = doc_pack.shape[1]
    doc_pack = with_count(doc_pack, jnp.sum(valid_mask))
    all_rows = rows * lax.axis_size("dp") * lax.axis_size("tensor")

    middle, middle_low, ask_saved, doc_matrix = layer_forward(
        tokens,
        gather_chunks(tokens),
        context,
        ask_params,
        ask_matrix,
        ask_weights,
        up_all[:, 0],
        doc_matrix,
    )
    doc_chunks, doc_pack = tie(gather_chunks(middle_low), doc_pack)
    doc_parts, doc_weights = gather_all(doc_pack)
    final, final_low, doc_saved, _ = layer_forward(
        middle,
        doc_chunks,
        context,
        doc_params,
        doc_matrix,
        doc_weights,
        up_all[:, 1],
    )
    valid_total = count_of(doc_parts, column)
    grad_final = mask_rows[:, None] * (final - teacher.astype(f32)) * (all_rows / valid_total)
    grad_middle, doc_wide, pending = layer_backward(
        grad_final, context, doc_matrix, doc_weights, doc_saved
    )
    grad_input, ask_wide, (sums, ask_narrow, doc_narrow) = layer_backward(
        grad_middle, context, ask_matrix, ask_weights, ask_saved, pending
    )
    half = sums.shape[0] // 2
    doc_grads = layer_outputs(doc_wide, doc_narrow, sums[:half], context[2])
    ask_grads = layer_outputs(ask_wide, ask_narrow, sums[half:], context[2])
    return (final_low, grad_input) + ask_grads + doc_grads


def layer_specs():
    return (
        P("dp", "tensor"),
        P("dp", "tensor"),
        P("dp", "tensor"),
        P("tensor"),
        P("tensor"),
        P("tensor", "dp"),
        P(),
        P(),
        P(),
        P("dp", "tensor"),
        P("tensor"),
        P("tensor", "dp"),
        P(),
        P(),
        P(),
    )


def solution(mesh):
    rows = P(("dp", "tensor"), None)
    return jax.shard_map(
        on_device,
        mesh=mesh,
        in_specs=(rows, P("dp", None), P(("dp", "tensor")), rows) + layer_specs() * 2,
        out_specs=(rows, rows) + layer_specs() * 2,
        check_vma=False,
    )
```
